32 devices in a mesh: dp: 2 (over x), win: 4 (over y, core), tensor: 4 (over z).
Axes of the slice: x: 2, y: 2, z: 4, core: 2. Of those that a mesh axis runs over, the one named last changes fastest.
Arguments:
- tokens: bfloat16 [2, 12, 588, 768], P('dp', 'win', 'tensor'), may hold values from -6 to 6
- window_ids: int32 [2, 12, 3], P('dp', 'win'), may hold values from 0 to 25, as said below
- norm1_gain: bfloat16 [768], replicated, may hold values from 0.5 to 1.5
- norm1_bias: bfloat16 [768], replicated, may hold values from -1.75 to 1.75
- qkv_weight: bfloat16 [768, 3, 768], P(('dp', 'win'), None, 'tensor'), may hold values from -0.21875 to 0.21875
- qv_bias: bfloat16 [2, 768], P(None, 'tensor'), may hold values from -3 to 3
- rel_height: bfloat16 [27, 64], replicated, may hold values from -0.875 to 0.875
- rel_width: bfloat16 [27, 64], replicated, may hold values from -0.875 to 0.875
- proj_weight: bfloat16 [768, 768], P('tensor', ('dp', 'win')), may hold values from -0.875 to 0.875
- proj_bias: bfloat16 [768], replicated, may hold values from -1.75 to 1.75
- norm2_gain: bfloat16 [768], replicated, may hold values from 0.5 to 1.5
- norm2_bias: bfloat16 [768], replicated, may hold values from -1.75 to 1.75
- fc1_weight: bfloat16 [768, 3072], P(('dp', 'win'), 'tensor'), may hold values from -0.21875 to 0.21875
- fc1_bias: bfloat16 [3072], P('tensor'), may hold values from -3 to 3
- fc2_weight: bfloat16 [3072, 768], P('tensor', ('dp', 'win')), may hold values from -0.109375 to 0.109375
- fc2_bias: bfloat16 [768], replicated, may hold values from -1.75 to 1.75
- out_grad: bfloat16 [2, 12, 588, 768], P('dp', 'win', 'tensor'), may hold values from -6 to 6
Outputs:
- output: bfloat16 [2, 12, 588, 768], P('dp', 'win', 'tensor')
- grad_tokens: float32 [2, 12, 588, 768], P('dp', 'win', 'tensor')
- grad_norm1_gain: float32 [768], replicated
- grad_norm1_bias: float32 [768], replicated
- grad_qkv_weight: float32 [768, 3, 768], P(('dp', 'win'), None, 'tensor')
- grad_qv_bias: float32 [2, 768], replicated
- grad_rel_height: float32 [27, 64], replicated
- grad_rel_width: float32 [27, 64], replicated
- grad_proj_weight: float32 [768, 768], P('tensor', ('dp', 'win'))
- grad_proj_bias: float32 [768], replicated
- grad_norm2_gain: float32 [768], replicated
- grad_norm2_bias: float32 [768], replicated
- grad_fc1_weight: float32 [768, 3072], P(('dp', 'win'), 'tensor')
- grad_fc1_bias: float32 [3072], replicated
- grad_fc2_weight: float32 [3072, 768], P('tensor', ('dp', 'win'))
- grad_fc2_bias: float32 [768], replicated
The draws below stay inside these ranges and needn't reach their ends.
Inputs may be any that keep to these rules, and one draw needn't show every extreme that they name: `window_ids`: every window 0 to 24 of an image stands in exactly one slot of that image, the value 25 marks an empty slot, and in every image one index of win holds 9 windows.
All inputs are finite; a program needn't handle non-finite values.
Results may differ from the reference program's by a relative error of at most 0.015.
Values may be sent and summed in bfloat16 or wider, within the bound.
A program may use at most 128 MiB of HBM per device.

```python
import math
import jax
import jax.numpy as jnp
from jax import lax

D = 768
HEADS = 12
HD = 64
FF = 3072
WS = 14
GRID = 64
MB = 3
WMB = 3
WINDOWS = 25
WT = 196
RP = 27
ROWS = 588
GROUPS = 12
SLOTS = 36
IMAGES = 2


def draw_window_ids(key, part):
    per_device = MB * WMB

    def one_image(image_key):
        first_key, second_key, third_key = jax.random.split(image_key, 3)
        full_device = jax.random.randint(first_key, (), 0, SLOTS // per_device)
        order = jax.random.permutation(second_key, SLOTS)
        device_of = jnp.arange(SLOTS) // per_device
        score = jnp.where(device_of == full_device, 0, SLOTS) + order
        ranking = jnp.argsort(jnp.argsort(score, stable=True), stable=True)
        shuffled = jax.random.permutation(third_key, WINDOWS)
        picked = shuffled[jnp.minimum(ranking, WINDOWS - 1)]
        slot_ids = jnp.where(ranking < WINDOWS, picked, WINDOWS)
        return slot_ids.astype(jnp.int32).reshape(GROUPS, WMB)
    image_keys = jax.random.split(key, IMAGES)
    return jax.vmap(one_image)(image_keys)


def levels(stream_key, shape, cuts, smallest, largest):
    factor_of, own = 1.0, jax.random.fold_in(stream_key, 6)
    for dim, shards_of in cuts:
        draws = jnp.exp(jax.random.uniform(jax.random.fold_in(own, dim), (shards_of,), jnp.float32, smallest / len(cuts), largest / len(cuts)))
        factor_of = factor_of * jnp.repeat(draws, shape[dim] // shards_of).reshape([-1 if axis == dim else 1 for axis in range(len(shape))])
    return factor_of


def gaussian(own_key, extent, scale, reach, cuts=(), held_as=jnp.bfloat16):
    factor_of = levels(own_key, extent, cuts, -0.22, 0.18) if cuts else 1.0
    array = jax.random.normal(own_key, extent, jnp.float32) * scale * factor_of
    return jnp.minimum(jnp.maximum(array, -reach), reach).astype(held_as)


def setup_inputs(seed: int = 0) -> dict:
    seeds = jax.random.split(jax.random.key(seed), 18)
    tokens = gaussian(seeds[0], (IMAGES, GROUPS, ROWS, D), 1.0, 6.0, ((0, 2), (1, 4), (2, 4)))
    window_ids = draw_window_ids(jax.random.fold_in(seeds[17], 71), 0)
    norm1_gain = jnp.clip(1.0 + 0.1 * jax.random.normal(seeds[2], (D,), jnp.float32), 0.5, 1.5).astype(jnp.bfloat16)
    norm1_bias = gaussian(seeds[3], (D,), 0.3, 1.75)
    qkv_weight = gaussian(seeds[4], (D, 3, HEADS * HD), D ** -0.5, 0.21875, ((0, 8), (2, 4)))
    qv_bias = gaussian(seeds[5], (2, HEADS * HD), 0.5, 3.0, ((1, 4),))
    rel_height = gaussian(seeds[6], (RP, HD), 0.15, 0.875)
    rel_width = gaussian(seeds[7], (RP, HD), 0.15, 0.875)
    proj_weight = gaussian(seeds[8], (HEADS * HD, D), (D // 16) ** -0.5, 0.875, ((0, 4), (1, 8)))
    proj_bias = gaussian(seeds[9], (D,), 0.3, 1.75)
    norm2_gain = jnp.clip(1.0 + 0.1 * jax.random.normal(seeds[10], (D,), jnp.float32), 0.5, 1.5).astype(jnp.bfloat16)
    norm2_bias = gaussian(seeds[11], (D,), 0.3, 1.75)
    fc1_weight = gaussian(seeds[12], (D, FF), D ** -0.5, 0.21875, ((0, 8), (1, 4)))
    fc1_bias = gaussian(seeds[13], (FF,), 0.5, 3.0, ((0, 4),))
    fc2_weight = gaussian(seeds[14], (FF, D), FF ** -0.5, 0.109375, ((0, 4), (1, 8)))
    fc2_bias = gaussian(seeds[15], (D,), 0.3, 1.75)
    out_grad = gaussian(seeds[16], (IMAGES, GROUPS, ROWS, D), 1.0, 6.0, ((0, 2), (1, 4), (2, 4)))
    return {"tokens": tokens, "window_ids": window_ids, "norm1_gain": norm1_gain, "norm1_bias": norm1_bias, "qkv_weight": qkv_weight, "qv_bias": qv_bias, "rel_height": rel_height, "rel_width": rel_width, "proj_weight": proj_weight, "proj_bias": proj_bias, "norm2_gain": norm2_gain, "norm2_bias": norm2_bias, "fc1_weight": fc1_weight, "fc1_bias": fc1_bias, "fc2_weight": fc2_weight, "fc2_bias": fc2_bias, "out_grad": out_grad}


@jax.custom_vjp
def low(v):
    return lax.optimization_barrier(v.astype(jnp.bfloat16)).astype(jnp.float32)

@jax.custom_vjp
def low_back(v):
    return v

def low_keep(v):
    return (low(v), None)

def low_pass(kept, grad):
    return (grad,)

def back_keep(v):
    return (v, None)

def back_low(kept, grad):
    return (low(grad),)
low.defvjp(low_keep, low_pass)
low_back.defvjp(back_keep, back_low)

def matmul_high(left, right):
    return jnp.dot(left, right, precision=lax.Precision.HIGHEST)

def layer_norm(values, gain_vec, shift_vec):
    average = lax.optimization_barrier(jnp.mean(values, axis=-1, keepdims=True))
    centred = values - average
    spread = lax.optimization_barrier(jnp.mean(centred * centred, axis=-1, keepdims=True))
    return centred * lax.rsqrt(spread + 1e-06) * gain_vec + shift_vec

def window_mask(slot_ids):
    across = (GRID + WS - 1) // WS
    row_pos = lax.broadcasted_iota(jnp.int32, (WS, WS), 0)
    col_pos = lax.broadcasted_iota(jnp.int32, (WS, WS), 1)
    win_row = (slot_ids // across)[:, None, None]
    win_col = (slot_ids % across)[:, None, None]
    inside = (slot_ids < across * across)[:, None, None] & (win_row * WS + row_pos < GRID) & (win_col * WS + col_pos < GRID)
    return inside.astype(jnp.float32).reshape(-1)

def rel_table(table):
    offsets = lax.broadcasted_iota(jnp.int32, (WS, WS), 0) - lax.broadcasted_iota(jnp.int32, (WS, WS), 1) + (WS - 1)
    return table[offsets.astype(jnp.int32)]

def block_forward(param_set, rows_in, mask_rows):
    norm1_gain, norm1_bias, qkv_weight, qv_bias, rel_height, rel_width, proj_weight, proj_bias, norm2_gain, norm2_bias, fc1_weight, fc1_bias, fc2_weight, fc2_bias = param_set
    high = lax.Precision.HIGHEST
    head_scale = 1.0 / math.sqrt(HD)
    masked = mask_rows[:, None]
    normed = low(masked * layer_norm(rows_in, norm1_gain, norm1_bias))
    query = low_back(low(matmul_high(normed, qkv_weight[:, 0, :]) + qv_bias[0]))
    keys_all = low_back(low(matmul_high(normed, qkv_weight[:, 1, :])))
    values_all = low_back(low(matmul_high(normed, qkv_weight[:, 2, :]) + qv_bias[1]))
    shape_five = (WMB, WS, WS, HEADS, HD)
    query_win = query.reshape(shape_five)
    key_win = keys_all.reshape(shape_five)
    scores = jnp.einsum('wijhc,wklhc->whijkl', query_win, key_win, precision=high) * head_scale
    rel_rows = jnp.einsum('wijhc,ikc->whijk', query_win, rel_table(rel_height), precision=high)
    rel_cols = jnp.einsum('wijhc,jlc->whijl', query_win, rel_table(rel_width), precision=high)
    scores = scores + rel_rows[:, :, :, :, :, None] + rel_cols[:, :, :, :, None, :]
    scores = low_back(scores.reshape(WMB, HEADS, WT, WT))
    probs = low(jax.nn.softmax(scores, axis=-1))
    attended = jnp.einsum('whqk,wkhc->wqhc', probs, values_all.reshape(WMB, WT, HEADS, HD), precision=high)
    attended = low_back(low(attended.reshape(ROWS, HEADS * HD)))
    branch = low_back(matmul_high(attended, proj_weight))
    hidden = rows_in + masked * (branch + proj_bias)
    normed2 = low(layer_norm(hidden, norm2_gain, norm2_bias))
    upper = low_back(matmul_high(normed2, fc1_weight) + fc1_bias)
    activ = low(jax.nn.gelu(upper, approximate=False))
    mixed = low_back(matmul_high(activ, fc2_weight)) + fc2_bias
    return masked * (hidden + mixed)

def reference(tokens, window_ids, norm1_gain, norm1_bias, qkv_weight, qv_bias, rel_height, rel_width, proj_weight, proj_bias, norm2_gain, norm2_bias, fc1_weight, fc1_bias, fc2_weight, fc2_bias, out_grad):
    param_set = tuple((item.astype(jnp.float32) for item in (norm1_gain, norm1_bias, qkv_weight, qv_bias, rel_height, rel_width, proj_weight, proj_bias, norm2_gain, norm2_bias, fc1_weight, fc1_bias, fc2_weight, fc2_bias)))
    block_count = IMAGES * GROUPS
    rows_all = tokens.reshape(block_count, ROWS, D).astype(jnp.float32)
    ids_all = window_ids.reshape(block_count, WMB).astype(jnp.int32)
    cot_all = out_grad.reshape(block_count, ROWS, D).astype(jnp.float32)

    def step_block(totals, inputs):
        rows_in, ids_block, cot_rows = inputs
        mask_rows = window_mask(ids_block)
        result, pullback = jax.vjp(lambda params_in, rows_data: block_forward(params_in, rows_data, mask_rows), param_set, rows_in)
        grad_params, grad_rows = pullback(cot_rows)
        totals = jax.tree.map(lambda acc_val, new_val: acc_val + new_val, totals, grad_params)
        return (totals, (result.astype(jnp.bfloat16), grad_rows))
    zero_grads = jax.tree.map(jnp.zeros_like, param_set)
    totals, (outputs, grads_in) = lax.scan(step_block, zero_grads, (rows_all, ids_all, cot_all))
    out_shape = (IMAGES, GROUPS, ROWS, D)
    return (outputs.reshape(out_shape), grads_in.reshape(out_shape), totals[0], totals[1], totals[2], totals[3], totals[4], totals[5], totals[6], totals[7], totals[8], totals[9], totals[10], totals[11], totals[12], totals[13])
```

```python
import math
from functools import partial

import jax
import jax.numpy as jnp
import numpy as np
from jax import lax
from jax.experimental import pallas as pl
from jax.experimental.pallas import tpu as pltpu
from jax.sharding import PartitionSpec as P

HEADS = 12
HD = 64
WS = 14
GRID = 64
WT = 196
BT = 49
BP = 56
WR = 4 * BP
QR = 64
NR = 2 * WR + QR
NE = NR + WR
BF = jnp.bfloat16
F32 = jnp.float32

WINDOWS_OF = (((0, 0), (1, 0)), ((2, 0), (0, 1)), ((2, 2), (2, 1)), ((0, 2), (1, 2)))
SHARED = (1, 1)


def block_table():
    rows = []
    for dev in range(4):
        row = []
        for m, s in WINDOWS_OF[dev]:
            row += [m * 12 + 4 * s + j for j in range(4)]
        row.append(SHARED[0] * 12 + 4 * SHARED[1] + dev)
        row += [SHARED[0] * 12 + 4 * SHARED[1] + j for j in range(4)]
        rows.append(row)
    return np.array(rows, np.int32)


def home_table():
    table = block_table()
    place = {}
    for dev in range(4):
        for slot in range(9):
            place[int(table[dev, slot])] = dev * 9 + slot
    return np.array([[place[m * 12 + 3 * dev + b] for m in range(3) for b in range(3)] for dev in range(4)], np.int32)


def token_positions():
    row = np.arange(WR)
    off = row % BP
    token = (row // BP) * BT + np.minimum(off, BT - 1)
    return token // WS, token % WS, off < BT


def key_tail():
    i, j, valid = token_positions()
    tail = np.zeros((WR, 128), np.float32)
    for m in range(WS):
        tail[:, 64 + m] = i == m
        tail[:, 78 + m] = j == m
    tail[:, 92:120] = tail[:, 64:92]
    tail[:, :120] *= valid[:, None]
    tail[:, 120] = np.where(valid, 0.0, -1e30)
    return tail


def pick_lanes(i, j):
    lane = np.arange(128)[None, :]
    m = np.clip((lane - 64) % 28, 0, 27)
    is_w = m >= 14
    fwd = jnp.where(is_w, 32 + j[:, None] - (m - 14) + 13, i[:, None] - m + 13)
    fwd = jnp.where((lane >= 64) & (lane < 120), fwd, 0)
    d = lane % 32
    pos = jnp.where(lane >= 32, j[:, None], i[:, None]) + 13 - d
    ok = (pos >= 0) & (pos < WS) & (lane < 64) & (d < 27)
    back = jnp.where(ok, pos + jnp.where(lane >= 32, 78, 64), 127)
    return fwd.astype(jnp.int32), back.astype(jnp.int32)


def dotf(a, b, dims):
    return lax.dot_general(a, b, (dims, ((), ())), preferred_element_type=F32)


NN = ((1,), (0,))
NT = ((1,), (1,))
TN = ((0,), (0,))


def compute_kernel(
    x_ref, cot_ref, mask_ref, w_ref, vec_ref, qkvb_ref, fc1b_ref, ktail_ref, fwd_ref, back_ref, tab_ref, tabt_ref,
    out_ref, gn_ref, gh_ref, g_ref, vg_ref, tg_ref,
    nrm, proj, qaug, kaug, vals, probs, att, hid, nr2, mix, gn2, act, gup, gml, gbl, dqkv,
):
    g1, b1, pb, g2, b2, fb = (vec_ref[i : i + 1, :] for i in range(6))

    def stats(v):
        mu = jnp.mean(v, axis=-1, keepdims=True)
        c = v - mu
        var = jnp.mean(c * c, axis=-1, keepdims=True)
        return c, lax.rsqrt(var + 1e-6)

    vg_ref[...] = jnp.zeros_like(vg_ref)

    for r0 in range(0, NE, 32):
        rows = slice(r0, r0 + 32)
        c, rs = stats(x_ref[r0 // 8 : r0 // 8 + 4].astype(F32).reshape(32, 768))
        nrm[rows, :] = (mask_ref[rows, :] * (c * rs * g1 + b1)).astype(BF)

    def fwd_t(t, _):
        proj[...] = dotf(nrm[...], w_ref[0, t][:, :576], NN) + qkvb_ref[t]
        for h in range(3):
            hh = 3 * t + h
            qs = (proj[:NR, 64 * h : 64 * h + 64].astype(BF) * BF(0.125)).astype(BF)
            rel = dotf(qs, tabt_ref[...], NN)
            lane = lax.broadcasted_iota(jnp.int32, (NR, 128), 1)
            got = jnp.take_along_axis(rel, fwd_ref[...], axis=1, mode="promise_in_bounds")
            hi = got.astype(BF).astype(F32)
            tail = jnp.where(lane < 92, hi, got - hi)
            tail = jnp.where(lane == 120, 1.0, jnp.where(lane < 120, tail, 0.0)).astype(BF)
            qa = jnp.concatenate([qs, tail[:, 64:]], axis=1)
            qaug[hh] = qa
            for w in range(3):
                src = slice(w * WR, w * WR + WR) if w < 2 else slice(NR, NE)
                k = proj[src, 192 + 64 * h : 256 + 64 * h].astype(BF)
                kaug[hh, w] = jnp.concatenate([k, ktail_ref[:, 64:]], axis=1)
                vals[hh, w] = proj[src, 384 + 64 * h : 448 + 64 * h].astype(BF)
        return 0

    lax.fori_loop(0, 4, fwd_t, 0)
    mix[...] = jnp.zeros_like(mix)

    def att_t(t, _):
        for h in range(3):
            hh = 3 * t + h
            for w in range(3):
                rows = slice(w * WR, w * WR + WR) if w < 2 else slice(2 * WR, NR)
                s = dotf(qaug[hh, rows, :], kaug[hh, w], NT)
                e = jnp.exp(s - jnp.max(s, axis=-1, keepdims=True))
                p = (e * (1.0 / jnp.sum(e, axis=-1, keepdims=True))).astype(BF)
                probs[hh, rows, :] = p
                att[t, rows, 64 * h : 64 * h + 64] = dotf(p, vals[hh, w], NN).astype(BF)
        mix[...] += dotf(att[t], w_ref[0, t][:, 576:], NT)
        return 0

    lax.fori_loop(0, 4, att_t, 0)

    for r0 in range(0, NR, 32):
        rows = slice(r0, r0 + 32)
        x = x_ref[r0 // 8 : r0 // 8 + 4].astype(F32).reshape(32, 768)
        hv = x + mask_ref[rows, :] * (mix[rows, :] + pb)
        hid[rows, :] = hv
        c, rs = stats(hv)
        nr2[rows, :] = (c * rs * g2 + b2).astype(BF)
        gm = mask_ref[rows, :] * cot_ref[r0 // 8 : r0 // 8 + 4].astype(F32).reshape(32, 768)
        gml[rows, :] = gm.astype(BF)
    mix[...] = jnp.zeros_like(mix)
    gn2[...] = jnp.zeros_like(gn2)

    def mlp_t(t, _):
        for f in range(3):
            cols = slice(256 * f, 256 * f + 256)
            for r0 in range(0, NR, 128):
                rows = slice(r0, r0 + 128)
                up = dotf(nr2[rows, :], w_ref[1, t][:, cols], NN) + fc1b_ref[t][:, cols]
                ga = dotf(gml[rows, :], w_ref[2, t][:, cols], NN)
                cdf = 0.5 * (1.0 + lax.erf(up * (1.0 / math.sqrt(2.0))))
                pdf = jnp.exp(-0.5 * up * up) * (1.0 / math.sqrt(2.0 * math.pi))
                act[rows, cols] = (up * cdf).astype(BF)
                gup[rows, cols] = (ga * (cdf + up * pdf)).astype(BF)
        vg_ref[pl.ds(8 + t, 1), :] = jnp.sum(gup[...].astype(F32), axis=0, keepdims=True)
        mix[...] += dotf(act[...], w_ref[2, t], NT)
        gn2[...] += dotf(gup[...], w_ref[1, t], NT)
        g_ref[2, t] = dotf(gml[...], act[...], TN).astype(BF)
        g_ref[1, t] = dotf(nr2[...], gup[...], TN).astype(BF)
        return 0

    lax.fori_loop(0, 4, mlp_t, 0)

    sums = [jnp.zeros((8, 768), F32) for _ in range(4)]

    def fold(v):
        return jnp.sum(v.reshape(4, 8, 768), axis=0)

    for r0 in range(0, NR, 32):
        rows = slice(r0, r0 + 32)
        mk = mask_ref[rows, :]
        gm = mk * cot_ref[r0 // 8 : r0 // 8 + 4].astype(F32).reshape(32, 768)
        hv = hid[rows, :]
        out_ref[r0 // 8 : r0 // 8 + 4] = (mk * (hv + mix[rows, :] + fb)).reshape(4, 8, 768).astype(BF)
        c, rs = stats(hv)
        xh = c * rs
        gn = gn2[rows, :]
        e2 = gn * g2
        gh = gm + rs * (e2 - jnp.mean(e2, axis=-1, keepdims=True) - xh * jnp.mean(e2 * xh, axis=-1, keepdims=True))
        gb = mk * gh
        gh_ref[rows, :] = gh
        gbl[rows, :] = gb.astype(BF)
        for n, v in enumerate((gn * xh, gn, gb, gm)):
            sums[n] = sums[n] + fold(v)
    for n in range(4):
        vg_ref[n : n + 1, :] = jnp.sum(sums[n], axis=0, keepdims=True)
    tg_ref[...] = jnp.zeros_like(tg_ref)
    gn_ref[...] = jnp.zeros_like(gn_ref)

    def bwd_t(t, _):
        att_w = att[t]
        g_ref[0, t, :, 576:] = dotf(gbl[...], att_w, TN).astype(BF)
        proj[:NR, :192] = dotf(gbl[...], w_ref[0, t][:, 576:], NN)
        dqkv[...] = jnp.zeros_like(dqkv)
        for h in range(3):
            hh = 3 * t + h
            lo = 64 * h
            for w in range(3):
                rows = slice(w * WR, w * WR + WR) if w < 2 else slice(2 * WR, NR)
                dst = rows if w < 2 else slice(NR, NE)
                do = proj[rows, lo : lo + 64].astype(BF)
                p = probs[hh, rows, :]
                pf = p.astype(F32)
                dp = dotf(do, vals[hh, w], NT)
                delta = jnp.sum(pf * dp, axis=-1, keepdims=True)
                ds = (pf * (dp - delta)).astype(BF)
                dq = dotf(ds, kaug[hh, w], NN)
                qa = qaug[hh, rows, :]
                dqkv[dst, 192 + lo : 256 + lo] = dotf(ds, qa, TN)[:, :64].astype(BF)
                dqkv[dst, 384 + lo : 448 + lo] = dotf(p, do, TN).astype(BF)
                rel = jnp.take_along_axis(dq, back_ref[rows, :], axis=1, mode="promise_in_bounds").astype(BF)
                gq = dq[:, :64] * 0.125 + dotf(rel, tab_ref[...], NN)
                dqkv[rows, lo : lo + 64] = gq.astype(BF)
                tg_ref[...] += dotf(rel, qa, TN)[:64]
        vg_ref[pl.ds(12 + t, 1), 0:576] = jnp.sum(dqkv[...].astype(F32), axis=0, keepdims=True)
        g_ref[0, t, :, :576] = dotf(nrm[...], dqkv[...], TN).astype(BF)
        gn_ref[...] += dotf(dqkv[...], w_ref[0, t][:, :576], NT)
        return 0

    lax.fori_loop(0, 4, bwd_t, 0)


def compute(x, cot, mask, w, vec, qkvb, fc1b, ktail, fwd, back, tab, tabt):
    shp = jax.ShapeDtypeStruct
    vm = pl.BlockSpec(memory_space=pltpu.VMEM)
    return pl.pallas_call(
        compute_kernel,
        out_shape=(
            shp((NR // 8, 8, 768), BF), shp((NE, 768), F32), shp((NR, 768), F32), shp((3, 4, 768, 768), BF),
            shp((16, 768), F32), shp((64, 128), F32),
        ),
        in_specs=[vm] * 12,
        out_specs=(vm,) * 6,
        scratch_shapes=[
            pltpu.VMEM((NE, 768), BF), pltpu.VMEM((NE, 576), F32), pltpu.VMEM((HEADS, NR, 128), BF),
            pltpu.VMEM((HEADS, 3, WR, 128), BF), pltpu.VMEM((HEADS, 3, WR, 64), BF), pltpu.VMEM((HEADS, NR, WR), BF),
            pltpu.VMEM((4, NR, 192), BF), pltpu.VMEM((NR, 768), F32), pltpu.VMEM((NR, 768), BF),
            pltpu.VMEM((NR, 768), F32), pltpu.VMEM((NR, 768), F32), pltpu.VMEM((NR, 768), BF), pltpu.VMEM((NR, 768), BF),
            pltpu.VMEM((NR, 768), BF), pltpu.VMEM((NR, 768), BF), pltpu.VMEM((NE, 576), BF),
        ],
        compiler_params=pltpu.CompilerParams(vmem_limit_bytes=67043328),
    )(x, cot, mask, w, vec, qkvb, fc1b, ktail, fwd, back, tab, tabt)


MESH = pl.DeviceIdType.MESH


class Links:
    def __init__(self, send, recv):
        self.send, self.recv = send, recv
        self.x = lax.axis_index("dp")
        win = lax.axis_index("win")
        self.y, self.c = win // 2, win % 2
        self.z = lax.axis_index("tensor")
        self.xn = (1 - self.x, win, self.z)
        self.yn = (self.x, (1 - self.y) * 2 + self.c, self.z)
        self.sib = (self.x, self.y * 2 + 1 - self.c, self.z)
        self.win = win

    def zdev(self, z):
        return (self.x, self.win, z)

    def barrier(self):
        sem = pltpu.get_barrier_semaphore()
        others = [self.xn, self.yn, self.sib] + [self.zdev((self.z + d) % 4) for d in (1, 2, 3)]
        for dev in others:
            pl.semaphore_signal(sem, inc=1, device_id=dev, device_id_type=MESH)
        pl.semaphore_wait(sem, len(others))

    def copy(self, src, dst, n, dev):
        return pltpu.make_async_remote_copy(
            src_ref=src, dst_ref=dst, send_sem=self.send.at[n], recv_sem=self.recv.at[n], device_id=dev,
            device_id_type=MESH,
        )


AG_SEMS = 3 * 39


class Gather:
    def __init__(self, links, shard, w, local, base):
        self.l, self.shard, self.w, self.local, self.base = links, shard, w, local, base

    def sem(self, k, kind, i):
        start = {"z": 0, "x": 3, "y": 7, "hx": 11, "hy": 15, "so": 19, "sx": 23, "sy": 27, "sa": 31, "sb": 35}[kind]
        return self.base + k * 39 + start + i

    def rank(self, i):
        return (self.l.z + 4 - i) % 4

    def piece(self, k, i, px, py, c, half=None):
        ref = self.w.at[k, self.rank(i), px, py, c]
        return ref if half is None else ref.at[pl.ds(48 * half, 48)]

    def move(self, k, kind, i):
        l = self.l
        if kind == "z":
            src = self.shard.at[k]
            return l.copy(src, self.piece(k, 0, l.x, l.y, l.c), self.sem(k, kind, i - 1), l.zdev((l.z + i) % 4))
        px, py, half, dev = {
            "x": (l.x, l.y, None, l.xn), "y": (l.x, l.y, None, l.yn),
            "hx": (l.x, 1 - l.y, 1, l.xn), "hy": (1 - l.x, l.y, 0, l.yn),
            "so": (l.x, l.y, None, l.sib), "sx": (1 - l.x, l.y, None, l.sib), "sy": (l.x, 1 - l.y, None, l.sib),
            "sa": (1 - l.x, 1 - l.y, 0, l.sib), "sb": (1 - l.x, 1 - l.y, 1, l.sib),
        }[kind]
        dst = self.piece(k, i, px, py, l.c, half)
        own = kind in ("x", "y", "so") and i == 0
        return l.copy(self.shard.at[k] if own else dst, dst, self.sem(k, kind, i), dev)

    def start(self, k, kind, i):
        self.move(k, kind, i).start()

    def arrived(self, k, kind, i):
        self.move(k, kind, i).wait_recv()

    def own(self, k):
        l = self.l
        pltpu.make_async_copy(self.shard.at[k], self.piece(k, 0, l.x, l.y, l.c), self.local.at[k]).start()
        for i in (1, 3, 2):
            self.start(k, "z", i)
        for kind in ("x", "y", "so"):
            self.start(k, kind, 0)

    def along(self, k, i):
        self.arrived(k, "z", i)
        for kind in ("x", "y", "so"):
            self.start(k, kind, i)

    def across(self, k, i):
        self.arrived(k, "x", i)
        self.start(k, "hy", i)
        self.start(k, "sx", i)
        self.arrived(k, "y", i)
        self.start(k, "hx", i)
        self.start(k, "sy", i)

    def corner(self, k, i):
        self.arrived(k, "hy", i)
        self.start(k, "sa", i)
        self.arrived(k, "hx", i)
        self.start(k, "sb", i)

    def partner(self, k):
        l = self.l
        for i in range(4):
            for kind in ("so", "sx", "sy", "sa", "sb"):
                self.arrived(k, kind, i)
        pltpu.make_async_copy(self.shard.at[k], self.piece(k, 0, l.x, l.y, l.c), self.local.at[k]).wait()

    def drain(self):
        for k in range(3):
            for i in (1, 2, 3):
                self.move(k, "z", i).wait_send()
            for kind in ("x", "y", "hx", "hy", "so", "sx", "sy", "sa", "sb"):
                for i in range(4):
                    self.move(k, kind, i).wait_send()


RS_SEMS = 12 * 6


class Scatter:
    def __init__(self, links, g, r1, r2, r3, r4, base):
        self.l, self.g, self.r1, self.r2, self.r3, self.r4, self.base = links, g, r1, r2, r3, r4, base

    def moves(self, n, stage):
        l, s = self.l, self.base + 6 * n
        g = self.g(n)
        if stage == 1:
            return [l.copy(g.at[:, :, 1 - l.c], self.r1.at[n], s, l.sib)]
        if stage == 2:
            return [
                l.copy(g.at[:, 1 - l.y, l.c, 0:48], self.r2.at[n, 0], s + 1, l.yn),
                l.copy(g.at[1 - l.x, :, l.c, 48:96], self.r2.at[n, 1], s + 2, l.xn),
            ]
        return [
            l.copy(g.at[1 - l.x, l.y, l.c, 0:48], self.r3.at[n, 0], s + 3, l.xn),
            l.copy(g.at[l.x, 1 - l.y, l.c, 48:96], self.r3.at[n, 1], s + 4, l.yn),
        ]

    def start(self, n, stage):
        for m in self.moves(n, stage):
            m.start()

    def wait(self, n, stage):
        for m in self.moves(n, stage):
            m.wait_recv()

    def last(self, n, k, d):
        l, g = self.l, self.g(n)
        return l.copy(g.at[l.x, l.y, l.c], self.r4.at[k, d - 1], self.base + 6 * n + 5, l.zdev((l.z + d) % 4))

    def add1(self, n):
        l, g = self.l, self.g(n)
        for a in range(2):
            for b in range(2):
                ref = g.at[a, b, l.c]
                ref[...] = ref[...] + self.r1[n, a, b]

    def add2(self, n):
        l, g = self.l, self.g(n)
        for a in range(2):
            ref = g.at[a, l.y, l.c, 0:48]
            ref[...] = ref[...] + self.r2[n, 0, a]
            ref = g.at[l.x, a, l.c, 48:96]
            ref[...] = ref[...] + self.r2[n, 1, a]

    def add3(self, n):
        l, g = self.l, self.g(n)
        for h in range(2):
            ref = g.at[l.x, l.y, l.c, pl.ds(48 * h, 48)]
            ref[...] = ref[...] + self.r3[n, h]


class Rows:
    TABLE = block_table()

    def __init__(self, links, local):
        self.l, self.local = links, local

    @staticmethod
    def home(block):
        m, b = divmod(int(block), 12)
        return b // 3, m * 3 + b % 3

    @staticmethod
    def unit(slot):
        return 7 * slot if slot < 9 else NR // 8 + 7 * (slot - 9)

    def inward(self, held, rows, slots, base, do):
        l = self.l
        for me in range(4):

            @pl.when(l.z == me)
            def _():
                sent = 0
                for slot in range(slots):
                    for step in range(4):
                        dev = (me + step) % 4
                        owner, idx = self.home(self.TABLE[dev, slot])
                        if owner != me:
                            continue
                        dst = rows.at[pl.ds(self.unit(slot), 7)]
                        if dev == me:
                            if do != "drain":
                                c = pltpu.make_async_copy(held.at[idx], dst, self.local.at[base + slot])
                                c.start() if do == "start" else c.wait()
                            continue
                        sent += 1
                        if do == "wait":
                            continue
                        c = pltpu.make_async_remote_copy(
                            src_ref=held.at[idx], dst_ref=dst, send_sem=l.send.at[base + sent - 1],
                            recv_sem=l.recv.at[base + slot], device_id=l.zdev(dev), device_id_type=MESH,
                        )
                        c.start() if do == "start" else c.wait_send()
                    owner, idx = self.home(self.TABLE[me, slot])
                    if do == "wait" and owner != me:
                        pltpu.make_async_remote_copy(
                            src_ref=held.at[0], dst_ref=rows.at[pl.ds(self.unit(slot), 7)], send_sem=l.send.at[base],
                            recv_sem=l.recv.at[base + slot], device_id=l.zdev(owner), device_id_type=MESH,
                        ).wait_recv()

    def outward(self, rows, held, base, do):
        l = self.l
        for me in range(4):

            @pl.when(l.z == me)
            def _():
                for slot in range(9):
                    owner, idx = self.home(self.TABLE[me, slot])
                    src = rows.at[pl.ds(7 * slot, 7)]
                    if owner == me:
                        if do != "drain":
                            c = pltpu.make_async_copy(src, held.at[idx], self.local.at[base + slot])
                            c.start() if do == "start" else c.wait()
                    elif do != "wait":
                        c = pltpu.make_async_remote_copy(
                            src_ref=src, dst_ref=held.at[idx], send_sem=l.send.at[base + slot],
                            recv_sem=l.recv.at[base + idx], device_id=l.zdev(owner), device_id_type=MESH,
                        )
                        c.start() if do == "start" else c.wait_send()
                for dev in range(4):
                    for slot in range(9):
                        owner, idx = self.home(self.TABLE[dev, slot])
                        if do == "wait" and owner == me and dev != me:
                            pltpu.make_async_remote_copy(
                                src_ref=rows.at[pl.ds(0, 7)], dst_ref=held.at[idx], send_sem=l.send.at[base],
                                recv_sem=l.recv.at[base + idx], device_id=l.zdev(dev), device_id_type=MESH,
                            ).wait_recv()


XS, CS, GS = 0, 13, 13 + 9
AG0 = GS + 9


def gather_kernel(x_in, cot_in, shard, x, cot, w, send, recv, local):
    x[63] = jnp.zeros((8, 768), BF)
    cot[63] = jnp.zeros((8, 768), BF)
    links = Links(send, recv)
    links.barrier()
    rows = Rows(links, local)
    ag = Gather(links, shard, w, local.at[pl.ds(40, 3)], AG0)
    rows.inward(x_in, x, 13, XS, "start")
    ag.own(0)
    rows.inward(cot_in, cot, 9, CS, "start")
    order = [("along", 0), ("own", 1), ("across", 0), ("along", 1), ("own", 2), ("corner", 0), ("across", 1), ("along", 2),
             ("corner", 1), ("across", 2), ("corner", 2)]
    for kind, k in order:
        if kind == "own":
            ag.own(k)
        else:
            for i in (range(1, 4) if kind == "along" else range(4)):
                getattr(ag, kind)(k, i)
    for k in range(3):
        ag.partner(k)
    rows.inward(x_in, x, 13, XS, "wait")
    rows.inward(cot_in, cot, 9, CS, "wait")
    rows.inward(x_in, x, 13, XS, "drain")
    rows.inward(cot_in, cot, 9, CS, "drain")
    ag.drain()


def gather_call(xh, coth, shard):
    shp = jax.ShapeDtypeStruct
    vm = pl.BlockSpec(memory_space=pltpu.VMEM)
    n = AG0 + AG_SEMS
    return pl.pallas_call(
        gather_kernel,
        out_shape=(shp((NE // 8, 8, 768), BF), shp((NR // 8, 8, 768), BF), shp((3, 4, 2, 2, 2, 96, 768), BF)),
        in_specs=[vm] * 3,
        out_specs=(vm,) * 3,
        scratch_shapes=[pltpu.SemaphoreType.DMA((n,)), pltpu.SemaphoreType.DMA((n,)), pltpu.SemaphoreType.DMA((48,))],
        compiler_params=pltpu.CompilerParams(collective_id=0, has_side_effects=True, vmem_limit_bytes=67043328),
    )(xh, coth, shard)


RET0 = 0
DX0 = 9
SH0 = 18
VS0 = 21
RS0 = VS0 + 10


def scatter_kernel(g_in, x, mask_ref, gain_ref, gn_ref, gh_ref, vg_in, tg_in, out,
                   own, out_h, dx_h, vg_out, tg_out,
                   g, r1, r2, r3, r4, gs, gsr, dx, vg, tg, vr, tr, send, recv, local):
    links = Links(send, recv)
    for n in range(12):
        pltpu.make_async_copy(g_in.at[n // 4, (links.z + n % 4 + 1) % 4], g.at[n], local.at[20 + n]).start()
    links.barrier()
    rows = Rows(links, local)
    rs = Scatter(links, lambda n: g.at[n], r1, r2, r3, r4, RS0)
    rows.outward(out, out_h, RET0, "start")
    gs[...] = gn_ref[NR:].reshape(WR // 8, 8, 768).astype(BF)
    sh = [
        links.copy(gs.at[pl.ds(7 * ((links.z + d) % 4), 7)], gsr.at[d - 1], SH0 + d - 1, links.zdev((links.z + d) % 4))
        for d in (1, 2, 3)
    ]
    for c in sh:
        c.start()

    for n in range(12):
        pltpu.make_async_copy(g_in.at[n // 4, (links.z + n % 4 + 1) % 4], g.at[n], local.at[20 + n]).wait()
        rs.start(n, 1)
    for c in sh:
        c.wait_recv()
    first_norm_back(links, x, mask_ref, gain_ref, gn_ref, gh_ref, gs, gsr, dx, vg_in, vg.at[0])
    rows.outward(dx, dx_h, DX0, "start")
    tg[0] = tg_in[...]
    for n in range(12):
        rs.wait(n, 1)
        rs.add1(n)
        rs.start(n, 2)
    for n in range(12):
        rs.wait(n, 2)
        rs.add2(n)
        rs.start(n, 3)
    for n in range(12):
        rs.wait(n, 3)
        rs.add3(n)
        if n % 4 < 3:
            rs.last(n, n // 4, n % 4 + 1).start()
    small_sums(links, vg, tg, vr, tr)
    vg_out[...] = vg[5]
    tg_out[...] = tg[5]
    for k in range(3):
        for d in (1, 2, 3):
            rs.last(4 * k + d - 1, k, d).wait_recv()
        fin = g[4 * k + 3, links.x, links.y, links.c].astype(F32)
        for d in range(3):
            fin = fin + r4[k, d].astype(F32)
        own[k] = fin
    rows.outward(out, out_h, RET0, "wait")
    rows.outward(dx, dx_h, DX0, "wait")
    rows.outward(out, out_h, RET0, "drain")
    rows.outward(dx, dx_h, DX0, "drain")
    for c in sh:
        c.wait_send()
    for n in range(12):
        for stage in (1, 2, 3):
            for m in rs.moves(n, stage):
                m.wait_send()
        if n % 4 < 3:
            rs.last(n, n // 4, n % 4 + 1).wait_send()


def first_norm_back(links, x, mask_ref, gain_ref, gn_ref, gh_ref, gs, gsr, dx, vg_in, vg):
    own = gn_ref[pl.ds(pl.multiple_of(NR + 56 * links.z, 8), 56), :]
    for d in range(3):
        own = own + gsr[d].astype(F32).reshape(56, 768)
    quarter = gn_ref[2 * WR : 2 * WR + 56, :] + own
    g1 = gain_ref[0:1, :]
    s_gain = jnp.zeros((8, 768), F32)
    s_bias = jnp.zeros((8, 768), F32)
    for r0, n in [(r, 32) for r in range(0, 2 * WR, 32)] + [(2 * WR, 56)]:
        rows = slice(r0, r0 + n)
        v = x[r0 // 8 : (r0 + n) // 8].astype(F32).reshape(n, 768)
        c = v - jnp.mean(v, axis=-1, keepdims=True)
        rs = lax.rsqrt(jnp.mean(c * c, axis=-1, keepdims=True) + 1e-6)
        xh = c * rs
        gn = mask_ref[rows, :] * (gn_ref[rows, :] if n == 32 else quarter)
        e1 = gn * g1
        gx = gh_ref[rows, :] + rs * (
            e1 - jnp.mean(e1, axis=-1, keepdims=True) - xh * jnp.mean(e1 * xh, axis=-1, keepdims=True)
        )
        dx[r0 // 8 : (r0 + n) // 8] = gx.reshape(n // 8, 8, 768).astype(BF)
        s_gain = s_gain + jnp.sum((gn * xh).reshape(n // 8, 8, 768), axis=0)
        s_bias = s_bias + jnp.sum(gn.reshape(n // 8, 8, 768), axis=0)
    vg[...] = vg_in[...]
    vg[4:5, :] = jnp.sum(s_gain, axis=0, keepdims=True)
    vg[5:6, :] = jnp.sum(s_bias, axis=0, keepdims=True)


def small_sums(links, vg, tg, vr, tr):
    l = links
    partners = [l.sib, l.xn, l.yn, l.zdev((l.z // 2) * 2 + 1 - l.z % 2), l.zdev((l.z + 2) % 4)]
    copies = []
    for n, dev in enumerate(partners):
        pair = [l.copy(vg.at[n], vr.at[n], VS0 + 2 * n, dev), l.copy(tg.at[n], tr.at[n], VS0 + 2 * n + 1, dev)]
        for c in pair:
            c.start()
        for c in pair:
            c.wait_recv()
        vg[n + 1] = vg[n] + vr[n]
        tg[n + 1] = tg[n] + tr[n]
        copies += pair
    for c in copies:
        c.wait_send()


def scatter_call(grads, x, mask, vec, gn, gh, vg, tg, out):
    shp = jax.ShapeDtypeStruct
    vm = pl.BlockSpec(memory_space=pltpu.VMEM)
    n = RS0 + RS_SEMS
    return pl.pallas_call(
        scatter_kernel,
        out_shape=(
            shp((3, 96, 768), F32), shp((9, 7, 8, 768), BF), shp((9, 7, 8, 768), BF), shp((16, 768), F32), shp((64, 128), F32),
        ),
        in_specs=[pl.BlockSpec(memory_space=pl.ANY)] + [vm] * 8,
        out_specs=(vm,) * 5,
        scratch_shapes=[
            pltpu.VMEM((12, 2, 2, 2, 96, 768), BF), pltpu.VMEM((12, 2, 2, 96, 768), BF), pltpu.VMEM((12, 2, 2, 48, 768), BF),
            pltpu.VMEM((12, 2, 48, 768), BF), pltpu.VMEM((3, 3, 96, 768), BF), pltpu.VMEM((WR // 8, 8, 768), BF),
            pltpu.VMEM((3, 7, 8, 768), BF), pltpu.VMEM((NR // 8, 8, 768), BF), pltpu.VMEM((6, 16, 768), F32),
            pltpu.VMEM((6, 64, 128), F32), pltpu.VMEM((5, 16, 768), F32), pltpu.VMEM((5, 64, 128), F32),
            pltpu.SemaphoreType.DMA((n,)), pltpu.SemaphoreType.DMA((n,)), pltpu.SemaphoreType.DMA((32,)),
        ],
        compiler_params=pltpu.CompilerParams(collective_id=1, has_side_effects=True, vmem_limit_bytes=67043328),
    )(grads, x, mask, vec, gn, gh, vg, tg, out)


def plain_gather(xh, coth, shard):
    mine = lax.dynamic_index_in_dim(jnp.asarray(block_table()), lax.axis_index("tensor"), 0, keepdims=False)

    def spread(held, count):
        blocks = lax.all_gather(held.reshape(3, 3, 7, 8, 768), "tensor", axis=1).reshape(36, 7, 8, 768)
        got = jnp.take(blocks, mine[:count], axis=0).reshape(-1, 8, 768)
        return jnp.concatenate([got[:63], jnp.zeros((1, 8, 768), BF), got[63:]], axis=0)

    whole = lax.all_gather(lax.all_gather(shard, ("dp", "win"), axis=1, tiled=True), "tensor", axis=1)
    return spread(xh, 13), spread(coth, 9), whole


def plain_scatter(grads, x, mask, vec, gn, gh, vg, tg, out):
    shared = lax.psum_scatter(gn[NR:], "tensor", scatter_dimension=0, tiled=True)
    gn = mask * (gn[:NR] + jnp.pad(shared, ((2 * WR, QR - BP), (0, 0))))
    xf = x[: NR // 8].reshape(NR, 768).astype(F32)
    cen = xf - jnp.mean(xf, axis=-1, keepdims=True)
    rs = lax.rsqrt(jnp.mean(cen * cen, axis=-1, keepdims=True) + 1e-6)
    xh = cen * rs
    e1 = gn * vec[0]
    gx = gh + rs * (e1 - jnp.mean(e1, axis=-1, keepdims=True) - xh * jnp.mean(e1 * xh, axis=-1, keepdims=True))
    vg = vg.at[4].set(jnp.sum(gn * xh, axis=0)).at[5].set(jnp.sum(gn, axis=0))
    back_to = lax.dynamic_index_in_dim(jnp.asarray(home_table()), lax.axis_index("tensor"), 0, keepdims=False)

    def bring(rows):
        blocks = lax.all_gather(rows[:63].reshape(9, 7, 8, 768), "tensor", axis=0, tiled=True)
        return jnp.take(blocks, back_to, axis=0)

    own = lax.psum_scatter(grads.reshape(3, 4, 768, 768), "tensor", scatter_dimension=1, tiled=False)
    own = lax.psum_scatter(own, ("dp", "win"), scatter_dimension=1, tiled=True).astype(F32)
    vg, tg = lax.psum((vg, tg), ("dp", "win", "tensor"))
    return own, bring(out), bring(gx.astype(BF).reshape(NR // 8, 8, 768)), vg, tg


def per_device(
    links, tokens, window_ids, norm1_gain, norm1_bias, qkv_weight, qv_bias, rel_height, rel_width, proj_weight, proj_bias,
    norm2_gain, norm2_bias, fc1_weight, fc1_bias, fc2_weight, fc2_bias, out_grad,
):
    rank = lax.axis_index("tensor")

    def home_blocks(rows):
        return jnp.pad(rows.reshape(9, BT, 768), ((0, 0), (0, BP - BT), (0, 0))).reshape(9, 7, 8, 768)

    shard = jnp.stack(
        [
            jnp.concatenate([qkv_weight.reshape(-1, 576), proj_weight.T], axis=1),
            fc1_weight,
            fc2_weight.T,
        ]
    )
    x, cot, whole = (gather_call if links else plain_gather)(home_blocks(tokens), home_blocks(out_grad), shard)
    whole = whole.reshape(3, 4, 768, 768)

    wi, wj, wv = token_positions()
    wi, wj, wv = jnp.asarray(wi, jnp.int32), jnp.asarray(wj, jnp.int32), jnp.asarray(wv)
    qi = jnp.pad(lax.dynamic_slice_in_dim(wi, rank * BP, BP), (0, QR - BP))
    qj = jnp.pad(lax.dynamic_slice_in_dim(wj, rank * BP, BP), (0, QR - BP))
    qv = jnp.pad(lax.dynamic_slice_in_dim(wv, rank * BP, BP), (0, QR - BP))
    ids = window_ids.reshape(9)
    slots = jnp.asarray([[m * 3 + s for m, s in WINDOWS_OF[dev]] + [4, 4] for dev in range(4)], jnp.int32)
    wid = jnp.take(ids, lax.dynamic_index_in_dim(slots, rank, 0, keepdims=False), axis=0)

    across = (GRID + WS - 1) // WS

    def valid(w, i, j, ok):
        return ok & (w < across * across) & ((w // across) * WS + i < GRID) & ((w % across) * WS + j < GRID)

    mask = jnp.concatenate(
        [valid(wid[0], wi, wj, wv), valid(wid[1], wi, wj, wv), valid(wid[2], qi, qj, qv), valid(wid[3], wi, wj, wv)]
    ).astype(F32)[:, None]
    ii = jnp.concatenate([wi, wi, qi])
    jj = jnp.concatenate([wj, wj, qj])
    fwd, back = pick_lanes(ii, jj)

    small = jnp.concatenate(
        [fc1_bias[None], jnp.pad(qv_bias.reshape(1, 384), ((0, 0), (0, 384))), jnp.zeros((14, 768), BF)], axis=0
    )
    small = lax.all_gather(small, "tensor", axis=0).astype(F32)
    fc1b = small[:, 0:1, :]
    qkvb = jnp.concatenate([small[:, 1:2, :192], jnp.zeros((4, 1, 192), F32), small[:, 1:2, 192:384]], axis=2)
    vec = jnp.stack(
        [norm1_gain, norm1_bias, proj_bias, norm2_gain, norm2_bias, fc2_bias, fc2_bias, fc2_bias]
    ).astype(F32)
    tab = jnp.zeros((128, 64), BF).at[0:27].set(rel_height).at[32:59].set(rel_width)
    tabt = (tab * BF(8)).T
    ktail = jnp.asarray(key_tail(), BF)

    out, gn, gh, grads, vg, tg = compute(x, cot, mask, whole, vec, qkvb, fc1b, ktail, fwd, back, tab, tabt)
    own, out, dx, vg, tg = (scatter_call if links else plain_scatter)(
        grads.reshape(3, 4, 2, 2, 2, 96, 768), x, mask[:NR], vec, gn, gh, vg, tg, out
    )

    def tokens_of(blocks):
        return blocks.reshape(9, BP, 768)[:, :BT].reshape(tokens.shape)

    output = tokens_of(out)
    grad_tokens = tokens_of(dx).astype(F32)
    g_qkv = own[0, :, :576].reshape(qkv_weight.shape)
    g_proj = own[0, :, 576:].T
    g_fc1 = own[1]
    g_fc2 = own[2].T
    g_qv = jnp.stack([vg[12:16, :192].reshape(-1), vg[12:16, 384:576].reshape(-1)])
    return (
        output, grad_tokens, vg[4], vg[5], g_qkv, g_qv, tg[0:27, :64] * 8.0, tg[32:59, :64] * 8.0, g_proj,
        vg[2], vg[0], vg[1], g_fc1, vg[8:12].reshape(-1), g_fc2, vg[3],
    )


def solution(mesh):
    in_specs = (
        P("dp", "win", "tensor", None), P("dp", "win", None), P(), P(), P(("dp", "win"), None, "tensor"),
        P(None, "tensor"), P(), P(), P("tensor", ("dp", "win")), P(), P(), P(), P(("dp", "win"), "tensor"), P("tensor"),
        P("tensor", ("dp", "win")), P(), P("dp", "win", "tensor", None),
    )
    out_specs = (
        P("dp", "win", "tensor", None), P("dp", "win", "tensor", None), P(), P(), P(("dp", "win"), None, "tensor"), P(),
        P(), P(), P("tensor", ("dp", "win")), P(), P(), P(), P(("dp", "win"), "tensor"), P(),
        P("tensor", ("dp", "win")), P(),
    )
    links = dict(mesh.shape) == {"dp": 2, "win": 4, "tensor": 4}
    return jax.shard_map(partial(per_device, links), mesh=mesh, in_specs=in_specs, out_specs=out_specs, check_vma=False)
```

```python
import math
from functools import partial

import jax
import jax.numpy as jnp
import numpy as np
from jax import lax
from jax.experimental import pallas as pl
from jax.experimental.pallas import tpu as pltpu
from jax.sharding import PartitionSpec as P

HEADS = 12
HD = 64
WS = 14
GRID = 64
WT = 196
BT = 49
BP = 56
WR = 4 * BP
QR = 64
NR = 2 * WR + QR
NE = NR + WR
BF = jnp.bfloat16
F32 = jnp.float32

WINDOWS_OF = (((0, 0), (1, 0)), ((2, 0), (0, 1)), ((2, 2), (2, 1)), ((0, 2), (1, 2)))
SHARED = (1, 1)


def block_table():
    rows = []
    for dev in range(4):
        row = []
        for m, s in WINDOWS_OF[dev]:
            row += [m * 12 + 4 * s + j for j in range(4)]
        row.append(SHARED[0] * 12 + 4 * SHARED[1] + dev)
        row += [SHARED[0] * 12 + 4 * SHARED[1] + j for j in range(4)]
        rows.append(row)
    return np.array(rows, np.int32)


def home_table():
    table = block_table()
    place = {}
    for dev in range(4):
        for slot in range(9):
            place[int(table[dev, slot])] = dev * 9 + slot
    return np.array([[place[m * 12 + 3 * dev + b] for m in range(3) for b in range(3)] for dev in range(4)], np.int32)


def token_positions():
    row = np.arange(WR)
    off = row % BP
    token = (row // BP) * BT + np.minimum(off, BT - 1)
    return token // WS, token % WS, off < BT


def key_tail():
    i, j, valid = token_positions()
    tail = np.zeros((WR, 128), np.float32)
    for m in range(WS):
        tail[:, 64 + m] = i == m
        tail[:, 78 + m] = j == m
    tail[:, 92:120] = tail[:, 64:92]
    tail[:, :120] *= valid[:, None]
    tail[:, 120] = np.where(valid, 0.0, -1e30)
    return tail


def pick_lanes(i, j):
    lane = np.arange(128)[None, :]
    m = np.clip((lane - 64) % 28, 0, 27)
    is_w = m >= 14
    fwd = jnp.where(is_w, 32 + j[:, None] - (m - 14) + 13, i[:, None] - m + 13)
    fwd = jnp.where((lane >= 64) & (lane < 120), fwd, 0)
    d = lane % 32
    pos = jnp.where(lane >= 32, j[:, None], i[:, None]) + 13 - d
    ok = (pos >= 0) & (pos < WS) & (lane < 64) & (d < 27)
    back = jnp.where(ok, pos + jnp.where(lane >= 32, 78, 64), 127)
    return fwd.astype(jnp.int32), back.astype(jnp.int32)


def dotf(a, b, dims):
    return lax.dot_general(a, b, (dims, ((), ())), preferred_element_type=F32)


NN = ((1,), (0,))
NT = ((1,), (1,))
TN = ((0,), (0,))


def compute_kernel(
    x_ref, cot_ref, mask_ref, w_ref, vec_ref, qkvb_ref, fc1b_ref, ktail_ref, fwd_ref, back_ref, tab_ref, tabt_ref,
    out_ref, gn_ref, gh_ref, g_ref, vg_ref, tg_ref,
    nrm, proj, qaug, kaug, vals, probs, att, hid, nr2, mix, gn2, act, gup, gml, gbl, dqkv,
):
    g1, b1, pb, g2, b2, fb = (vec_ref[i : i + 1, :] for i in range(6))

    def stats(v):
        mu = jnp.mean(v, axis=-1, keepdims=True)
        c = v - mu
        var = jnp.mean(c * c, axis=-1, keepdims=True)
        return c, lax.rsqrt(var + 1e-6)

    vg_ref[...] = jnp.zeros_like(vg_ref)

    for r0 in range(0, NE, 32):
        rows = slice(r0, r0 + 32)
        c, rs = stats(x_ref[r0 // 8 : r0 // 8 + 4].astype(F32).reshape(32, 768))
        nrm[rows, :] = (mask_ref[rows, :] * (c * rs * g1 + b1)).astype(BF)

    def fwd_t(t, _):
        proj[...] = dotf(nrm[...], w_ref[0, t][:, :576], NN) + qkvb_ref[t]
        for h in range(3):
            hh = 3 * t + h
            qs = (proj[:NR, 64 * h : 64 * h + 64].astype(BF) * BF(0.125)).astype(BF)
            rel = dotf(qs, tabt_ref[...], NN)
            lane = lax.broadcasted_iota(jnp.int32, (NR, 128), 1)
            got = jnp.take_along_axis(rel, fwd_ref[...], axis=1, mode="promise_in_bounds")
            hi = got.astype(BF).astype(F32)
            tail = jnp.where(lane < 92, hi, got - hi)
            tail = jnp.where(lane == 120, 1.0, jnp.where(lane < 120, tail, 0.0)).astype(BF)
            qa = jnp.concatenate([qs, tail[:, 64:]], axis=1)
            qaug[hh] = qa
            for w in range(3):
                src = slice(w * WR, w * WR + WR) if w < 2 else slice(NR, NE)
                k = proj[src, 192 + 64 * h : 256 + 64 * h].astype(BF)
                kaug[hh, w] = jnp.concatenate([k, ktail_ref[:, 64:]], axis=1)
                vals[hh, w] = proj[src, 384 + 64 * h : 448 + 64 * h].astype(BF)
        return 0

    lax.fori_loop(0, 4, fwd_t, 0)
    mix[...] = jnp.zeros_like(mix)

    def att_t(t, _):
        for h in range(3):
            hh = 3 * t + h
            for w in range(3):
                rows = slice(w * WR, w * WR + WR) if w < 2 else slice(2 * WR, NR)
                s = dotf(qaug[hh, rows, :], kaug[hh, w], NT)
                e = jnp.exp(s - jnp.max(s, axis=-1, keepdims=True))
                p = (e * (1.0 / jnp.sum(e, axis=-1, keepdims=True))).astype(BF)
                probs[hh, rows, :] = p
                att[t, rows, 64 * h : 64 * h + 64] = dotf(p, vals[hh, w], NN).astype(BF)
        mix[...] += dotf(att[t], w_ref[0, t][:, 576:], NT)
        return 0

    lax.fori_loop(0, 4, att_t, 0)

    for r0 in range(0, NR, 32):
        rows = slice(r0, r0 + 32)
        x = x_ref[r0 // 8 : r0 // 8 + 4].astype(F32).reshape(32, 768)
        hv = x + mask_ref[rows, :] * (mix[rows, :] + pb)
        hid[rows, :] = hv
        c, rs = stats(hv)
        nr2[rows, :] = (c * rs * g2 + b2).astype(BF)
        gm = mask_ref[rows, :] * cot_ref[r0 // 8 : r0 // 8 + 4].astype(F32).reshape(32, 768)
        gml[rows, :] = gm.astype(BF)
    mix[...] = jnp.zeros_like(mix)
    gn2[...] = jnp.zeros_like(gn2)

    def mlp_t(t, _):
        for f in range(3):
            cols = slice(256 * f, 256 * f + 256)
            for r0 in range(0, NR, 128):
                rows = slice(r0, r0 + 128)
                up = dotf(nr2[rows, :], w_ref[1, t][:, cols], NN) + fc1b_ref[t][:, cols]
                ga = dotf(gml[rows, :], w_ref[2, t][:, cols], NN)
                cdf = 0.5 * (1.0 + lax.erf(up * (1.0 / math.sqrt(2.0))))
                pdf = jnp.exp(-0.5 * up * up) * (1.0 / math.sqrt(2.0 * math.pi))
                act[rows, cols] = (up * cdf).astype(BF)
                gup[rows, cols] = (ga * (cdf + up * pdf)).astype(BF)
        vg_ref[pl.ds(8 + t, 1), :] = jnp.sum(gup[...].astype(F32), axis=0, keepdims=True)
        mix[...] += dotf(act[...], w_ref[2, t], NT)
        gn2[...] += dotf(gup[...], w_ref[1, t], NT)
        g_ref[2, t] = dotf(gml[...], act[...], TN).astype(BF)
        g_ref[1, t] = dotf(nr2[...], gup[...], TN).astype(BF)
        return 0

    lax.fori_loop(0, 4, mlp_t, 0)

    sums = [jnp.zeros((8, 768), F32) for _ in range(4)]

    def fold(v):
        return jnp.sum(v.reshape(4, 8, 768), axis=0)

    for r0 in range(0, NR, 32):
        rows = slice(r0, r0 + 32)
        mk = mask_ref[rows, :]
        gm = mk * cot_ref[r0 // 8 : r0 // 8 + 4].astype(F32).reshape(32, 768)
        hv = hid[rows, :]
        out_ref[r0 // 8 : r0 // 8 + 4] = (mk * (hv + mix[rows, :] + fb)).reshape(4, 8, 768).astype(BF)
        c, rs = stats(hv)
        xh = c * rs
        gn = gn2[rows, :]
        e2 = gn * g2
        gh = gm + rs * (e2 - jnp.mean(e2, axis=-1, keepdims=True) - xh * jnp.mean(e2 * xh, axis=-1, keepdims=True))
        gb = mk * gh
        gh_ref[rows, :] = gh
        gbl[rows, :] = gb.astype(BF)
        for n, v in enumerate((gn * xh, gn, gb, gm)):
            sums[n] = sums[n] + fold(v)
    for n in range(4):
        vg_ref[n : n + 1, :] = jnp.sum(sums[n], axis=0, keepdims=True)
    tg_ref[...] = jnp.zeros_like(tg_ref)
    gn_ref[...] = jnp.zeros_like(gn_ref)

    def bwd_t(t, _):
        att_w = att[t]
        g_ref[0, t, :, 576:] = dotf(gbl[...], att_w, TN).astype(BF)
        proj[:NR, :192] = dotf(gbl[...], w_ref[0, t][:, 576:], NN)
        dqkv[...] = jnp.zeros_like(dqkv)
        for h in range(3):
            hh = 3 * t + h
            lo = 64 * h
            for w in range(3):
                rows = slice(w * WR, w * WR + WR) if w < 2 else slice(2 * WR, NR)
                dst = rows if w < 2 else slice(NR, NE)
                do = proj[rows, lo : lo + 64].astype(BF)
                p = probs[hh, rows, :]
                pf = p.astype(F32)
                dp = dotf(do, vals[hh, w], NT)
                delta = jnp.sum(pf * dp, axis=-1, keepdims=True)
                ds = (pf * (dp - delta)).astype(BF)
                dq = dotf(ds, kaug[hh, w], NN)
                qa = qaug[hh, rows, :]
                dqkv[dst, 192 + lo : 256 + lo] = dotf(ds, qa, TN)[:, :64].astype(BF)
                dqkv[dst, 384 + lo : 448 + lo] = dotf(p, do, TN).astype(BF)
                rel = jnp.take_along_axis(dq, back_ref[rows, :], axis=1, mode="promise_in_bounds").astype(BF)
                gq = dq[:, :64] * 0.125 + dotf(rel, tab_ref[...], NN)
                dqkv[rows, lo : lo + 64] = gq.astype(BF)
                tg_ref[...] += dotf(rel, qa, TN)[:64]
        vg_ref[pl.ds(12 + t, 1), 0:576] = jnp.sum(dqkv[...].astype(F32), axis=0, keepdims=True)
        g_ref[0, t, :, :576] = dotf(nrm[...], dqkv[...], TN).astype(BF)
        gn_ref[...] += dotf(dqkv[...], w_ref[0, t][:, :576], NT)
        return 0

    lax.fori_loop(0, 4, bwd_t, 0)


def compute(x, cot, mask, w, vec, qkvb, fc1b, ktail, fwd, back, tab, tabt):
    shp = jax.ShapeDtypeStruct
    vm = pl.BlockSpec(memory_space=pltpu.VMEM)
    return pl.pallas_call(
        compute_kernel,
        out_shape=(
            shp((NR // 8, 8, 768), BF), shp((NE, 768), F32), shp((NR, 768), F32), shp((3, 4, 768, 768), BF),
            shp((16, 768), F32), shp((64, 128), F32),
        ),
        in_specs=[vm] * 12,
        out_specs=(vm,) * 6,
        scratch_shapes=[
            pltpu.VMEM((NE, 768), BF), pltpu.VMEM((NE, 576), F32), pltpu.VMEM((HEADS, NR, 128), BF),
            pltpu.VMEM((HEADS, 3, WR, 128), BF), pltpu.VMEM((HEADS, 3, WR, 64), BF), pltpu.VMEM((HEADS, NR, WR), BF),
            pltpu.VMEM((4, NR, 192), BF), pltpu.VMEM((NR, 768), F32), pltpu.VMEM((NR, 768), BF),
            pltpu.VMEM((NR, 768), F32), pltpu.VMEM((NR, 768), F32), pltpu.VMEM((NR, 768), BF), pltpu.VMEM((NR, 768), BF),
            pltpu.VMEM((NR, 768), BF), pltpu.VMEM((NR, 768), BF), pltpu.VMEM((NE, 576), BF),
        ],
        compiler_params=pltpu.CompilerParams(vmem_limit_bytes=67043328),
    )(x, cot, mask, w, vec, qkvb, fc1b, ktail, fwd, back, tab, tabt)


MESH = pl.DeviceIdType.MESH


class Links:
    def __init__(self, send, recv):
        self.send, self.recv = send, recv
        self.x = lax.axis_index("dp")
        win = lax.axis_index("win")
        self.y, self.c = win // 2, win % 2
        self.z = lax.axis_index("tensor")
        self.xn = (1 - self.x, win, self.z)
        self.yn = (self.x, (1 - self.y) * 2 + self.c, self.z)
        self.sib = (self.x, self.y * 2 + 1 - self.c, self.z)
        self.win = win

    def zdev(self, z):
        return (self.x, self.win, z)

    def barrier(self):
        sem = pltpu.get_barrier_semaphore()
        others = [self.xn, self.yn, self.sib] + [self.zdev((self.z + d) % 4) for d in (1, 2, 3)]
        for dev in others:
            pl.semaphore_signal(sem, inc=1, device_id=dev, device_id_type=MESH)
        pl.semaphore_wait(sem, len(others))

    def copy(self, src, dst, n, dev):
        return pltpu.make_async_remote_copy(
            src_ref=src, dst_ref=dst, send_sem=self.send.at[n], recv_sem=self.recv.at[n], device_id=dev,
            device_id_type=MESH,
        )


AG_SEMS = 3 * 39


class Gather:
    def __init__(self, links, shard, w, local, base):
        self.l, self.shard, self.w, self.local, self.base = links, shard, w, local, base

    def sem(self, k, kind, i):
        start = {"z": 0, "x": 3, "y": 7, "hx": 11, "hy": 15, "so": 19, "sx": 23, "sy": 27, "sa": 31, "sb": 35}[kind]
        return self.base + k * 39 + start + i

    def rank(self, i):
        return (self.l.z + 4 - i) % 4

    def piece(self, k, i, px, py, c, half=None):
        ref = self.w.at[k, self.rank(i), px, py, c]
        return ref if half is None else ref.at[pl.ds(48 * half, 48)]

    def move(self, k, kind, i):
        l = self.l
        if kind == "z":
            src = self.shard.at[k]
            return l.copy(src, self.piece(k, 0, l.x, l.y, l.c), self.sem(k, kind, i - 1), l.zdev((l.z + i) % 4))
        px, py, half, dev = {
            "x": (l.x, l.y, None, l.xn), "y": (l.x, l.y, None, l.yn),
            "hx": (l.x, 1 - l.y, 1, l.xn), "hy": (1 - l.x, l.y, 0, l.yn),
            "so": (l.x, l.y, None, l.sib), "sx": (1 - l.x, l.y, None, l.sib), "sy": (l.x, 1 - l.y, None, l.sib),
            "sa": (1 - l.x, 1 - l.y, 0, l.sib), "sb": (1 - l.x, 1 - l.y, 1, l.sib),
        }[kind]
        dst = self.piece(k, i, px, py, l.c, half)
        own = kind in ("x", "y", "so") and i == 0
        return l.copy(self.shard.at[k] if own else dst, dst, self.sem(k, kind, i), dev)

    def start(self, k, kind, i):
        self.move(k, kind, i).start()

    def arrived(self, k, kind, i):
        self.move(k, kind, i).wait_recv()

    def keep(self, k):
        l = self.l
        return pltpu.make_async_copy(self.shard.at[k], self.piece(k, 0, l.x, l.y, l.c), self.local.at[k])

    def own_z(self, k):
        for i in (1, 3, 2):
            self.start(k, "z", i)

    def along(self, k, i):
        if i:
            self.arrived(k, "z", i)
        else:
            self.keep(k).start()
        for kind in ("x", "y", "so"):
            self.start(k, kind, i)

    def across(self, k, i):
        self.arrived(k, "x", i)
        self.start(k, "hy", i)
        self.start(k, "sx", i)
        self.arrived(k, "y", i)
        self.start(k, "hx", i)
        self.start(k, "sy", i)

    def corner(self, k, i):
        self.arrived(k, "hy", i)
        self.start(k, "sa", i)
        self.arrived(k, "hx", i)
        self.start(k, "sb", i)

    def partner(self, k, i):
        for kind in ("so", "sx", "sy", "sa", "sb"):
            self.arrived(k, kind, i)
        if not i:
            self.keep(k).wait()

    def drain(self, k, i):
        for kind in ("x", "y", "hx", "hy", "so", "sx", "sy", "sa", "sb"):
            self.move(k, kind, i).wait_send()


RS_SEMS = 12 * 6


class Scatter:
    def __init__(self, links, w, r1, r2, r3, r4, base):
        self.l, self.w, self.r1, self.r2, self.r3, self.r4, self.base = links, w, r1, r2, r3, r4, base

    def g(self, k, i):
        return self.w.at[k, (self.l.z + 4 - i) % 4]

    def moves(self, k, i, stage):
        l, n = self.l, 4 * k + i
        s = self.base + 6 * n
        g = self.g(k, i)
        if stage == 1:
            return [l.copy(g.at[:, :, 1 - l.c], self.r1.at[n], s, l.sib)]
        if stage == 2:
            return [
                l.copy(g.at[:, 1 - l.y, l.c, 0:48], self.r2.at[n, 0], s + 1, l.yn),
                l.copy(g.at[1 - l.x, :, l.c, 48:96], self.r2.at[n, 1], s + 2, l.xn),
            ]
        if stage == 3:
            return [
                l.copy(g.at[1 - l.x, l.y, l.c, 0:48], self.r3.at[n, 0], s + 3, l.xn),
                l.copy(g.at[l.x, 1 - l.y, l.c, 48:96], self.r3.at[n, 1], s + 4, l.yn),
            ]
        return [l.copy(g.at[l.x, l.y, l.c], self.r4.at[k, i - 1], s + 5, l.zdev((l.z + 4 - i) % 4))] if i else []

    def start(self, k, i, stage):
        for m in self.moves(k, i, stage):
            m.start()

    def wait(self, k, i, stage):
        for m in self.moves(k, i, stage):
            m.wait_recv()

    def step(self, k, i, stage):
        l, g, n = self.l, self.g(k, i), 4 * k + i
        self.wait(k, i, stage - 1)
        if stage == 2:
            for a in range(2):
                for b in range(2):
                    ref = g.at[a, b, l.c]
                    ref[...] = ref[...] + self.r1[n, a, b]
        elif stage == 3:
            for a in range(2):
                ref = g.at[a, l.y, l.c, 0:48]
                ref[...] = ref[...] + self.r2[n, 0, a]
                ref = g.at[l.x, a, l.c, 48:96]
                ref[...] = ref[...] + self.r2[n, 1, a]
        else:
            for h in range(2):
                ref = g.at[l.x, l.y, l.c, pl.ds(48 * h, 48)]
                ref[...] = ref[...] + self.r3[n, h]
        self.start(k, i, stage)

    def total(self, k):
        l = self.l
        fin = self.g(k, 0)[l.x, l.y, l.c].astype(F32)
        for i in (1, 2, 3):
            self.wait(k, i, 4)
            fin = fin + self.r4[k, i - 1].astype(F32)
        return fin

    def drain(self):
        for k in range(3):
            for i in range(4):
                for stage in (1, 2, 3, 4):
                    for m in self.moves(k, i, stage):
                        m.wait_send()


class Rows:
    TABLE = block_table()

    def __init__(self, links, local):
        self.l, self.local = links, local

    @staticmethod
    def home(block):
        m, b = divmod(int(block), 12)
        return b // 3, m * 3 + b % 3

    @staticmethod
    def unit(slot):
        return 7 * slot if slot < 9 else NR // 8 + 7 * (slot - 9)

    def inward(self, held, rows, slots, base, do):
        l = self.l
        for me in range(4):

            @pl.when(l.z == me)
            def _():
                sent = 0
                for slot in slots:
                    for step in range(4):
                        dev = (me + step) % 4
                        owner, idx = self.home(self.TABLE[dev, slot])
                        if owner != me:
                            continue
                        dst = rows.at[pl.ds(self.unit(slot), 7)]
                        if dev == me:
                            if do != "drain":
                                c = pltpu.make_async_copy(held.at[idx], dst, self.local.at[base + slot])
                                c.start() if do == "start" else c.wait()
                            continue
                        sent += 1
                        if do == "wait":
                            continue
                        c = pltpu.make_async_remote_copy(
                            src_ref=held.at[idx], dst_ref=dst, send_sem=l.send.at[base + sent - 1],
                            recv_sem=l.recv.at[base + slot], device_id=l.zdev(dev), device_id_type=MESH,
                        )
                        c.start() if do == "start" else c.wait_send()
                    owner, idx = self.home(self.TABLE[me, slot])
                    if do == "wait" and owner != me:
                        pltpu.make_async_remote_copy(
                            src_ref=held.at[0], dst_ref=rows.at[pl.ds(self.unit(slot), 7)], send_sem=l.send.at[base],
                            recv_sem=l.recv.at[base + slot], device_id=l.zdev(owner), device_id_type=MESH,
                        ).wait_recv()

    def outward(self, rows, held, base, mine, do):
        l = self.l
        for me in range(4):

            @pl.when(l.z == me)
            def _():
                for slot in range(9):
                    owner, idx = self.home(self.TABLE[me, slot])
                    src = rows.at[pl.ds(7 * slot, 7)]
                    if owner == me:
                        if do != "drain":
                            c = pltpu.make_async_copy(src, held.at[idx], self.local.at[mine + slot])
                            c.start() if do == "start" else c.wait()
                    elif do != "wait":
                        c = pltpu.make_async_remote_copy(
                            src_ref=src, dst_ref=held.at[idx], send_sem=l.send.at[base + slot],
                            recv_sem=l.recv.at[base + idx], device_id=l.zdev(owner), device_id_type=MESH,
                        )
                        c.start() if do == "start" else c.wait_send()
                for dev in range(4):
                    for slot in range(9):
                        owner, idx = self.home(self.TABLE[dev, slot])
                        if do == "wait" and owner == me and dev != me:
                            pltpu.make_async_remote_copy(
                                src_ref=rows.at[pl.ds(0, 7)], dst_ref=held.at[idx], send_sem=l.send.at[base],
                                recv_sem=l.recv.at[base + idx], device_id=l.zdev(dev), device_id_type=MESH,
                            ).wait_recv()


XS, CS, BS = 0, 13, 22
AG0 = BS + 3
RET0 = AG0 + AG_SEMS
DX0 = RET0 + 9
SH0 = DX0 + 9
VS0 = SH0 + 3
RS0 = VS0 + 10
SEMS = RS0 + RS_SEMS
X_SLOTS = (0, 1, 2, 3, 4, 5, 6, 7, 9, 10, 11, 12)

ORD = (0, 1, 3, 2)
BACK = (2, 1, 3, 0)
BLOCKS = ((0, 0), (1, 0), (0, 1), (0, 3), (0, 2), (2, 0), (1, 1), (2, 1), (1, 3), (2, 3), (1, 2), (2, 2))


PLACES = (
    [("M", n, j) for n in range(4) for j in range(5)] + ["N"] + [("B", n, j) for n in range(4) for j in range(3)]
    + ["T0", "T1", "T2", "S0", "S1", "S2", "S3", "S4", "T3"]
)
TICKS = {1: ("F", 0, 0), 2: ("F", 0, 2), 3: ("F", 1, 1), 4: ("F", 2, 1), 5: ("F", 3, 1), 6: "L", 7: ("M", 0, 0), 8: ("M", 0, 4),
         9: ("M", 1, 1), 10: ("M", 1, 4), 11: ("M", 2, 1)}
MLP_LAGS = ((0, 6, 11), (1, 8, 12))
BWD_LAGS = (0, 3, 5)


def timetable():
    plan = {}

    def put(place, *event):
        plan.setdefault(place, []).append(event)

    for s, place in TICKS.items():
        put(place, "tick", s)
    for n in range(4):
        for k, lags in zip((2, 1), MLP_LAGS):
            made = PLACES.index(("M", n, 4)) + 1
            for stage, lag in zip((2, 3, 4), lags):
                put(PLACES[made + lag], "step", k, ORD[n], stage)
        made = PLACES.index(("B", n, 2)) + 1
        for stage, lag in zip((2, 3, 4), BWD_LAGS):
            put(PLACES[made + lag], "step", 0, BACK[n], stage)
    return plan


def whole_kernel(
    x_in, cot_in, shard, small, mask_ref, vec_ref, ktail_ref, fwd_ref, back_ref, tab_ref, tabt_ref,
    own, out_h, dx_h, vg_out, tg_out,
    w, r1, r2, r3, r4, x, cot, sm, ob, dx, gn, hid, gn2, gs, gsr, vg, tg, vr, tr,
    nrm, proj, qaug, kaug, vals, probs, att, nr2, act, gup, gml, dqkv, send, recv, local,
):
    links = Links(send, recv)
    z = links.z
    rows_of = Rows(links, local)
    ag = Gather(links, shard, w, local.at[pl.ds(40, 3)], AG0)
    rs = Scatter(links, w, r1, r2, r3, r4, RS0)
    g1, b1, pb, g2, b2, fb = (vec_ref[i : i + 1, :] for i in range(6))

    def rank(order, m):
        i = jnp.int32(order[3])
        for n in range(3):
            i = jnp.where(m == n, order[n], i)
        return (z + 4 - i) % 4

    def weight(k, t):
        return w[k, t].reshape(768, 768)

    def tick(s):
        if s + 2 < 12:
            ag.along(*BLOCKS[s + 2])
        if s + 1 < 12:
            ag.across(*BLOCKS[s + 1])
        ag.corner(*BLOCKS[s])

    def at(m, plan):
        for n, todo in plan.items():

            @pl.when(m == n)
            def _():
                for f in todo:
                    f()

    plan = timetable()

    def run(events):
        for what, *which in events:
            if what == "tick":
                tick(*which)
            else:
                rs.step(*which)

    def now(place):
        run(plan.get(place, ()))

    def hook(m, loop, j):
        for n in range(4):
            todo = plan.get((loop, n, j))
            if todo:

                @pl.when(m == n)
                def _():
                    run(todo)

    def stats(v):
        mu = jnp.mean(v, axis=-1, keepdims=True)
        c = v - mu
        var = jnp.mean(c * c, axis=-1, keepdims=True)
        return c, lax.rsqrt(var + 1e-6)

    x[63] = jnp.zeros((8, 768), BF)
    cot[63] = jnp.zeros((8, 768), BF)
    links.barrier()
    for b in (0, 1):
        ag.along(*BLOCKS[b])
    bias = [links.copy(small, sm.at[z], BS + d - 1, links.zdev((z + d) % 4)) for d in (1, 2, 3)]
    keep_bias = pltpu.make_async_copy(small, sm.at[z], local.at[43])
    keep_bias.start()
    for c in bias:
        c.start()
    rows_of.inward(x_in, x, X_SLOTS, XS, "start")
    ag.own_z(0)
    rows_of.inward(cot_in, cot, range(9), CS, "start")
    ag.own_z(1)

    vg[...] = jnp.zeros_like(vg)
    tg[...] = jnp.zeros_like(tg)
    rows_of.inward(x_in, x, X_SLOTS, XS, "wait")
    x[56:63] = x[pl.ds(NR // 8 + 7 * z, 7)]
    for c in bias:
        c.wait_recv()
    keep_bias.wait()

    for r0 in range(0, NE, 32):
        rows = slice(r0, r0 + 32)
        c, rstd = stats(x[r0 // 8 : r0 // 8 + 4].astype(F32).reshape(32, 768))
        nrm[rows, :] = (mask_ref[rows, :] * (c * rstd * g1 + b1)).astype(BF)

    ag.across(*BLOCKS[0])
    tick(0)
    ag.own_z(2)
    mix = gn.at[pl.ds(0, NR)]
    mix[...] = jnp.zeros_like(mix)

    def fwd_t(m, _):
        at(m, {n: [partial(ag.partner, 0, ORD[n])] for n in range(4)})
        t = rank(ORD, m)
        proj[...] = dotf(nrm[...], weight(0, t)[:, :576], NN) + sm[t][1:2, :576]
        for h in range(3):
            hh = 3 * t + h
            qs = (proj[:NR, 64 * h : 64 * h + 64].astype(BF) * BF(0.125)).astype(BF)
            rel = dotf(qs, tabt_ref[...], NN)
            lane = lax.broadcasted_iota(jnp.int32, (NR, 128), 1)
            got = jnp.take_along_axis(rel, fwd_ref[...], axis=1, mode="promise_in_bounds")
            hi = got.astype(BF).astype(F32)
            tail = jnp.where(lane < 92, hi, got - hi)
            tail = jnp.where(lane == 120, 1.0, jnp.where(lane < 120, tail, 0.0)).astype(BF)
            qa = jnp.concatenate([qs, tail[:, 64:]], axis=1)
            qaug[hh] = qa
            for wn in range(3):
                src = slice(wn * WR, wn * WR + WR) if wn < 2 else slice(NR, NE)
                k = proj[src, 192 + 64 * h : 256 + 64 * h].astype(BF)
                kaug[hh, wn] = jnp.concatenate([k, ktail_ref[:, 64:]], axis=1)
                vals[hh, wn] = proj[src, 384 + 64 * h : 448 + 64 * h].astype(BF)
        hook(m, "F", 0)
        for h in range(3):
            hh = 3 * t + h
            for wn in range(3):
                rows = slice(wn * WR, wn * WR + WR) if wn < 2 else slice(2 * WR, NR)
                s = dotf(qaug[hh, rows, :], kaug[hh, wn], NT)
                e = jnp.exp(s - jnp.max(s, axis=-1, keepdims=True))
                p = (e * (1.0 / jnp.sum(e, axis=-1, keepdims=True))).astype(BF)
                probs[hh, rows, :] = p
                att[t, rows, 64 * h : 64 * h + 64] = dotf(p, vals[hh, wn], NN).astype(BF)
            if h == 1:
                hook(m, "F", 1)
        mix[...] += dotf(att[t], weight(0, t)[:, 576:], NT)
        hook(m, "F", 2)
        return 0

    lax.fori_loop(0, 4, fwd_t, 0)
    rows_of.inward(cot_in, cot, range(9), CS, "wait")
    now("L")

    for r0 in range(0, NR, 32):
        rows = slice(r0, r0 + 32)
        xv = x[r0 // 8 : r0 // 8 + 4].astype(F32).reshape(32, 768)
        hv = xv + mask_ref[rows, :] * (mix[rows, :] + pb)
        hid[rows, :] = hv
        c, rstd = stats(hv)
        nr2[rows, :] = (c * rstd * g2 + b2).astype(BF)
        gm = mask_ref[rows, :] * cot[r0 // 8 : r0 // 8 + 4].astype(F32).reshape(32, 768)
        gml[rows, :] = gm.astype(BF)
    mix[...] = jnp.zeros_like(mix)
    gn2[...] = jnp.zeros_like(gn2)

    def mlp_t(m, _):
        at(m, {n: [partial(ag.partner, 1, ORD[n]), partial(ag.partner, 2, ORD[n])] for n in range(4)})
        t = rank(ORD, m)
        for f in range(3):
            cols = slice(256 * f, 256 * f + 256)
            for r0 in range(0, NR, 128):
                rows = slice(r0, r0 + 128)
                up = dotf(nr2[rows, :], weight(1, t)[:, cols], NN) + sm[t][0:1, cols]
                ga = dotf(gml[rows, :], weight(2, t)[:, cols], NN)
                cdf = 0.5 * (1.0 + lax.erf(up * (1.0 / math.sqrt(2.0))))
                pdf = jnp.exp(-0.5 * up * up) * (1.0 / math.sqrt(2.0 * math.pi))
                act[rows, cols] = (up * cdf).astype(BF)
                gup[rows, cols] = (ga * (cdf + up * pdf)).astype(BF)
            hook(m, "M", f)
        vg[0, pl.ds(8 + t, 1), :] = jnp.sum(gup[...].astype(F32), axis=0, keepdims=True)
        mix[...] += dotf(act[...], weight(2, t), NT)
        hook(m, "M", 3)
        gn2[...] += dotf(gup[...], weight(1, t), NT)
        hook(m, "M", 4)
        at(m, {n: [partial(ag.drain, 2, ORD[n])] for n in range(4)})
        w[2, t] = dotf(gml[...], act[...], TN).astype(BF).reshape(2, 2, 2, 96, 768)
        at(m, {n: [partial(rs.start, 2, ORD[n], 1), partial(ag.drain, 1, ORD[n])] for n in range(4)})
        w[1, t] = dotf(nr2[...], gup[...], TN).astype(BF).reshape(2, 2, 2, 96, 768)
        at(m, {n: [partial(rs.start, 1, ORD[n], 1)] for n in range(4)})
        return 0

    lax.fori_loop(0, 4, mlp_t, 0)
    now("N")

    sums = [jnp.zeros((8, 768), F32) for _ in range(4)]

    def fold(v):
        return jnp.sum(v.reshape(4, 8, 768), axis=0)

    gbl = act
    for r0 in range(0, NR, 32):
        rows = slice(r0, r0 + 32)
        mk = mask_ref[rows, :]
        gm = mk * cot[r0 // 8 : r0 // 8 + 4].astype(F32).reshape(32, 768)
        hv = hid[rows, :]
        ob[r0 // 8 : r0 // 8 + 4] = (mk * (hv + mix[rows, :] + fb)).reshape(4, 8, 768).astype(BF)
        c, rstd = stats(hv)
        xh = c * rstd
        gv = gn2[rows, :]
        e2 = gv * g2
        gh = gm + rstd * (e2 - jnp.mean(e2, axis=-1, keepdims=True) - xh * jnp.mean(e2 * xh, axis=-1, keepdims=True))
        gb = mk * gh
        hid[rows, :] = gh
        gbl[rows, :] = gb.astype(BF)
        for n, v in enumerate((gv * xh, gv, gb, gm)):
            sums[n] = sums[n] + fold(v)
    for n in range(4):
        vg[0, n : n + 1, :] = jnp.sum(sums[n], axis=0, keepdims=True)
    rows_of.outward(ob, out_h, RET0, 22, "start")
    gn[...] = jnp.zeros_like(gn)

    def bwd_t(m, _):
        t = rank(BACK, m)
        at(m, {n: [partial(ag.drain, 0, BACK[n])] for n in range(4)})
        att_w = att[t]
        proj[:NR, :192] = dotf(gbl[...], weight(0, t)[:, 576:], NN)
        dqkv[...] = jnp.zeros_like(dqkv)
        for h in range(3):
            hh = 3 * t + h
            lo = 64 * h
            for wn in range(3):
                rows = slice(wn * WR, wn * WR + WR) if wn < 2 else slice(2 * WR, NR)
                dst = rows if wn < 2 else slice(NR, NE)
                do = proj[rows, lo : lo + 64].astype(BF)
                p = probs[hh, rows, :]
                pf = p.astype(F32)
                dp = dotf(do, vals[hh, wn], NT)
                delta = jnp.sum(pf * dp, axis=-1, keepdims=True)
                ds = (pf * (dp - delta)).astype(BF)
                dq = dotf(ds, kaug[hh, wn], NN)
                qa = qaug[hh, rows, :]
                dqkv[dst, 192 + lo : 256 + lo] = dotf(ds, qa, TN)[:, :64].astype(BF)
                dqkv[dst, 384 + lo : 448 + lo] = dotf(p, do, TN).astype(BF)
                rel = jnp.take_along_axis(dq, back_ref[rows, :], axis=1, mode="promise_in_bounds").astype(BF)
                gq = dq[:, :64] * 0.125 + dotf(rel, tab_ref[...], NN)
                dqkv[rows, lo : lo + 64] = gq.astype(BF)
                tg[0] += dotf(rel, qa, TN)[:64]
            hook(m, "B", h)
        vg[0, pl.ds(12 + t, 1), 0:576] = jnp.sum(dqkv[...].astype(F32), axis=0, keepdims=True)
        gn[...] += dotf(dqkv[...], weight(0, t)[:, :576], NT)
        gw = jnp.concatenate([dotf(nrm[...], dqkv[...], TN).astype(BF), dotf(gbl[...], att_w, TN).astype(BF)], axis=1)
        w[0, t] = gw.reshape(2, 2, 2, 96, 768)
        at(m, {n: [partial(rs.start, 0, BACK[n], 1)] for n in range(4)})
        return 0

    lax.fori_loop(0, 4, bwd_t, 0)

    gs[...] = gn[NR:].reshape(WR // 8, 8, 768).astype(BF)
    sh = [
        links.copy(gs.at[pl.ds(7 * ((z + d) % 4), 7)], gsr.at[d - 1], SH0 + d - 1, links.zdev((z + d) % 4)) for d in (1, 2, 3)
    ]
    for c in sh:
        c.start()
    now("T0")
    for c in sh:
        c.wait_recv()
    now("T1")
    first_norm_back(links, x, mask_ref, vec_ref, gn, hid, gsr, dx, vg.at[0])
    rows_of.outward(dx, dx_h, DX0, 31, "start")
    now("T2")
    small_sums(links, vg, tg, vr, tr, now)
    now("T3")
    vg_out[...] = vg[5]
    tg_out[...] = tg[5]
    for k in (2, 1, 0):
        own[k] = rs.total(k)
    rows_of.outward(ob, out_h, RET0, 22, "wait")
    rows_of.outward(dx, dx_h, DX0, 31, "wait")
    rows_of.outward(ob, out_h, RET0, 22, "drain")
    rows_of.outward(dx, dx_h, DX0, 31, "drain")
    rows_of.inward(x_in, x, X_SLOTS, XS, "drain")
    rows_of.inward(cot_in, cot, range(9), CS, "drain")
    for c in sh + bias:
        c.wait_send()
    for k in range(3):
        for i in (1, 2, 3):
            ag.move(k, "z", i).wait_send()
    rs.drain()


def first_norm_back(links, x, mask_ref, gain_ref, gn_ref, gh_ref, gsr, dx, vg):
    own = gn_ref[pl.ds(pl.multiple_of(NR + 56 * links.z, 8), 56), :]
    for d in range(3):
        own = own + gsr[d].astype(F32).reshape(56, 768)
    quarter = gn_ref[2 * WR : 2 * WR + 56, :] + own
    g1 = gain_ref[0:1, :]
    s_gain = jnp.zeros((8, 768), F32)
    s_bias = jnp.zeros((8, 768), F32)
    for r0, n in [(r, 32) for r in range(0, 2 * WR, 32)] + [(2 * WR, 56)]:
        rows = slice(r0, r0 + n)
        v = x[r0 // 8 : (r0 + n) // 8].astype(F32).reshape(n, 768)
        c = v - jnp.mean(v, axis=-1, keepdims=True)
        rs = lax.rsqrt(jnp.mean(c * c, axis=-1, keepdims=True) + 1e-6)
        xh = c * rs
        gn = mask_ref[rows, :] * (gn_ref[rows, :] if n == 32 else quarter)
        e1 = gn * g1
        gx = gh_ref[rows, :] + rs * (
            e1 - jnp.mean(e1, axis=-1, keepdims=True) - xh * jnp.mean(e1 * xh, axis=-1, keepdims=True)
        )
        dx[r0 // 8 : (r0 + n) // 8] = gx.reshape(n // 8, 8, 768).astype(BF)
        s_gain = s_gain + jnp.sum((gn * xh).reshape(n // 8, 8, 768), axis=0)
        s_bias = s_bias + jnp.sum(gn.reshape(n // 8, 8, 768), axis=0)
    vg[4:5, :] = jnp.sum(s_gain, axis=0, keepdims=True)
    vg[5:6, :] = jnp.sum(s_bias, axis=0, keepdims=True)


def small_sums(links, vg, tg, vr, tr, now):
    l = links
    partners = [l.sib, l.xn, l.yn, l.zdev((l.z // 2) * 2 + 1 - l.z % 2), l.zdev((l.z + 2) % 4)]
    copies = []
    for n, dev in enumerate(partners):
        pair = [l.copy(vg.at[n], vr.at[n], VS0 + 2 * n, dev), l.copy(tg.at[n], tr.at[n], VS0 + 2 * n + 1, dev)]
        for c in pair:
            c.start()
        now(f"S{n}")
        for c in pair:
            c.wait_recv()
        vg[n + 1] = vg[n] + vr[n]
        tg[n + 1] = tg[n] + tr[n]
        copies += pair
    for c in copies:
        c.wait_send()


def whole_call(xh, coth, shard, small, mask, vec, ktail, fwd, back, tab, tabt):
    shp = jax.ShapeDtypeStruct
    vm = pl.BlockSpec(memory_space=pltpu.VMEM)
    hbm = pl.BlockSpec(memory_space=pl.ANY)
    V = pltpu.VMEM
    dma = pltpu.SemaphoreType.DMA
    return pl.pallas_call(
        whole_kernel,
        out_shape=(
            shp((3, 96, 768), F32), shp((9, 7, 8, 768), BF), shp((9, 7, 8, 768), BF), shp((16, 768), F32), shp((64, 128), F32),
        ),
        in_specs=[hbm, hbm] + [vm] * 9,
        out_specs=(vm, hbm, hbm, vm, vm),
        scratch_shapes=[
            V((3, 4, 2, 2, 2, 96, 768), BF), V((12, 2, 2, 96, 768), BF), V((12, 2, 2, 48, 768), BF), V((12, 2, 48, 768), BF),
            V((3, 3, 96, 768), BF), V((NE // 8, 8, 768), BF), V((NR // 8, 8, 768), BF), V((4, 8, 768), F32),
            V((NR // 8, 8, 768), BF), V((NR // 8, 8, 768), BF), V((NE, 768), F32), V((NR, 768), F32), V((NR, 768), F32),
            V((WR // 8, 8, 768), BF), V((3, 7, 8, 768), BF), V((6, 16, 768), F32), V((6, 64, 128), F32),
            V((5, 16, 768), F32), V((5, 64, 128), F32),
            V((NE, 768), BF), V((NE, 576), F32), V((HEADS, NR, 128), BF), V((HEADS, 3, WR, 128), BF), V((HEADS, 3, WR, 64), BF),
            V((HEADS, NR, WR), BF), V((4, NR, 192), BF), V((NR, 768), BF), V((NR, 768), BF), V((NR, 768), BF), V((NR, 768), BF),
            V((NE, 576), BF), dma((SEMS,)), dma((SEMS,)), dma((48,)),
        ],
        compiler_params=pltpu.CompilerParams(collective_id=0, has_side_effects=True, vmem_limit_bytes=67043328),
    )(xh, coth, shard, small, mask, vec, ktail, fwd, back, tab, tabt)


def plain_gather(xh, coth, shard):
    mine = lax.dynamic_index_in_dim(jnp.asarray(block_table()), lax.axis_index("tensor"), 0, keepdims=False)

    def spread(held, count):
        blocks = lax.all_gather(held.reshape(3, 3, 7, 8, 768), "tensor", axis=1).reshape(36, 7, 8, 768)
        got = jnp.take(blocks, mine[:count], axis=0).reshape(-1, 8, 768)
        return jnp.concatenate([got[:63], jnp.zeros((1, 8, 768), BF), got[63:]], axis=0)

    whole = lax.all_gather(lax.all_gather(shard, ("dp", "win"), axis=1, tiled=True), "tensor", axis=1)
    return spread(xh, 13), spread(coth, 9), whole


def plain_scatter(grads, x, mask, vec, gn, gh, vg, tg, out):
    shared = lax.psum_scatter(gn[NR:], "tensor", scatter_dimension=0, tiled=True)
    gn = mask * (gn[:NR] + jnp.pad(shared, ((2 * WR, QR - BP), (0, 0))))
    xf = x[: NR // 8].reshape(NR, 768).astype(F32)
    cen = xf - jnp.mean(xf, axis=-1, keepdims=True)
    rs = lax.rsqrt(jnp.mean(cen * cen, axis=-1, keepdims=True) + 1e-6)
    xh = cen * rs
    e1 = gn * vec[0]
    gx = gh + rs * (e1 - jnp.mean(e1, axis=-1, keepdims=True) - xh * jnp.mean(e1 * xh, axis=-1, keepdims=True))
    vg = vg.at[4].set(jnp.sum(gn * xh, axis=0)).at[5].set(jnp.sum(gn, axis=0))
    back_to = lax.dynamic_index_in_dim(jnp.asarray(home_table()), lax.axis_index("tensor"), 0, keepdims=False)

    def bring(rows):
        blocks = lax.all_gather(rows[:63].reshape(9, 7, 8, 768), "tensor", axis=0, tiled=True)
        return jnp.take(blocks, back_to, axis=0)

    own = lax.psum_scatter(grads.reshape(3, 4, 768, 768), "tensor", scatter_dimension=1, tiled=False)
    own = lax.psum_scatter(own, ("dp", "win"), scatter_dimension=1, tiled=True).astype(F32)
    vg, tg = lax.psum((vg, tg), ("dp", "win", "tensor"))
    return own, bring(out), bring(gx.astype(BF).reshape(NR // 8, 8, 768)), vg, tg


def per_device(
    links, tokens, window_ids, norm1_gain, norm1_bias, qkv_weight, qv_bias, rel_height, rel_width, proj_weight, proj_bias,
    norm2_gain, norm2_bias, fc1_weight, fc1_bias, fc2_weight, fc2_bias, out_grad,
):
    rank = lax.axis_index("tensor")

    def home_blocks(rows):
        return jnp.pad(rows.reshape(9, BT, 768), ((0, 0), (0, BP - BT), (0, 0))).reshape(9, 7, 8, 768)

    shard = jnp.stack(
        [
            jnp.concatenate([qkv_weight.reshape(-1, 576), proj_weight.T], axis=1),
            fc1_weight,
            fc2_weight.T,
        ]
    )
    xh, coth = home_blocks(tokens), home_blocks(out_grad)

    wi, wj, wv = token_positions()
    wi, wj, wv = jnp.asarray(wi, jnp.int32), jnp.asarray(wj, jnp.int32), jnp.asarray(wv)
    qi = jnp.pad(lax.dynamic_slice_in_dim(wi, rank * BP, BP), (0, QR - BP))
    qj = jnp.pad(lax.dynamic_slice_in_dim(wj, rank * BP, BP), (0, QR - BP))
    qv = jnp.pad(lax.dynamic_slice_in_dim(wv, rank * BP, BP), (0, QR - BP))
    ids = window_ids.reshape(9)
    slots = jnp.asarray([[m * 3 + s for m, s in WINDOWS_OF[dev]] + [4, 4] for dev in range(4)], jnp.int32)
    wid = jnp.take(ids, lax.dynamic_index_in_dim(slots, rank, 0, keepdims=False), axis=0)

    across = (GRID + WS - 1) // WS

    def valid(w, i, j, ok):
        return ok & (w < across * across) & ((w // across) * WS + i < GRID) & ((w % across) * WS + j < GRID)

    mask = jnp.concatenate(
        [valid(wid[0], wi, wj, wv), valid(wid[1], wi, wj, wv), valid(wid[2], qi, qj, qv), valid(wid[3], wi, wj, wv)]
    ).astype(F32)[:, None]
    ii = jnp.concatenate([wi, wi, qi])
    jj = jnp.concatenate([wj, wj, qj])
    fwd, back = pick_lanes(ii, jj)

    small = jnp.zeros((8, 768), F32).at[0].set(fc1_bias.astype(F32))
    small = small.at[1, :192].set(qv_bias[0].astype(F32)).at[1, 384:576].set(qv_bias[1].astype(F32))
    vec = jnp.stack(
        [norm1_gain, norm1_bias, proj_bias, norm2_gain, norm2_bias, fc2_bias, fc2_bias, fc2_bias]
    ).astype(F32)
    tab = jnp.zeros((128, 64), BF).at[0:27].set(rel_height).at[32:59].set(rel_width)
    tabt = (tab * BF(8)).T
    ktail = jnp.asarray(key_tail(), BF)

    if links:
        own, out, dx, vg, tg = whole_call(xh, coth, shard, small, mask, vec, ktail, fwd, back, tab, tabt)
    else:
        x, cot, whole = plain_gather(xh, coth, shard)
        small = lax.all_gather(small, "tensor", axis=0)
        out, gn, gh, grads, vg, tg = compute(
            x, cot, mask, whole.reshape(3, 4, 768, 768), vec, small[:, 1:2, :576], small[:, 0:1], ktail, fwd, back, tab, tabt
        )
        own, out, dx, vg, tg = plain_scatter(grads, x, mask[:NR], vec, gn, gh, vg, tg, out)

    def tokens_of(blocks):
        return blocks.reshape(9, BP, 768)[:, :BT].reshape(tokens.shape)

    output = tokens_of(out)
    grad_tokens = tokens_of(dx).astype(F32)
    g_qkv = own[0, :, :576].reshape(qkv_weight.shape)
    g_proj = own[0, :, 576:].T
    g_fc1 = own[1]
    g_fc2 = own[2].T
    g_qv = jnp.stack([vg[12:16, :192].reshape(-1), vg[12:16, 384:576].reshape(-1)])
    return (
        output, grad_tokens, vg[4], vg[5], g_qkv, g_qv, tg[0:27, :64] * 8.0, tg[32:59, :64] * 8.0, g_proj,
        vg[2], vg[0], vg[1], g_fc1, vg[8:12].reshape(-1), g_fc2, vg[3],
    )


def solution(mesh):
    in_specs = (
        P("dp", "win", "tensor", None), P("dp", "win", None), P(), P(), P(("dp", "win"), None, "tensor"),
        P(None, "tensor"), P(), P(), P("tensor", ("dp", "win")), P(), P(), P(), P(("dp", "win"), "tensor"), P("tensor"),
        P("tensor", ("dp", "win")), P(), P("dp", "win", "tensor", None),
    )
    out_specs = (
        P("dp", "win", "tensor", None), P("dp", "win", "tensor", None), P(), P(), P(("dp", "win"), None, "tensor"), P(),
        P(), P(), P("tensor", ("dp", "win")), P(), P(), P(), P(("dp", "win"), "tensor"), P(),
        P("tensor", ("dp", "win")), P(),
    )
    links = dict(mesh.shape) == {"dp": 2, "win": 4, "tensor": 4}
    return jax.shard_map(partial(per_device, links), mesh=mesh, in_specs=in_specs, out_specs=out_specs, check_vma=False)
```

```python
import math
from functools import partial

import jax
import jax.numpy as jnp
import numpy as np
from jax import lax
from jax.experimental import pallas as pl
from jax.experimental.pallas import tpu as pltpu
from jax.sharding import PartitionSpec as P

HEADS = 12
HD = 64
WS = 14
GRID = 64
WT = 196
BT = 49
BP = 56
WR = 4 * BP
QR = 64
NR = 2 * WR + QR
NE = NR + WR
BF = jnp.bfloat16
F32 = jnp.float32

WINDOWS_OF = (((0, 0), (1, 0)), ((2, 0), (0, 1)), ((2, 2), (2, 1)), ((0, 2), (1, 2)))
SHARED = (1, 1)


def block_table():
    rows = []
    for dev in range(4):
        row = []
        for m, s in WINDOWS_OF[dev]:
            row += [m * 12 + 4 * s + j for j in range(4)]
        row.append(SHARED[0] * 12 + 4 * SHARED[1] + dev)
        row += [SHARED[0] * 12 + 4 * SHARED[1] + j for j in range(4)]
        rows.append(row)
    return np.array(rows, np.int32)


def home_table():
    table = block_table()
    place = {}
    for dev in range(4):
        for slot in range(9):
            place[int(table[dev, slot])] = dev * 9 + slot
    return np.array([[place[m * 12 + 3 * dev + b] for m in range(3) for b in range(3)] for dev in range(4)], np.int32)


def token_positions():
    row = np.arange(WR)
    off = row % BP
    token = (row // BP) * BT + np.minimum(off, BT - 1)
    return token // WS, token % WS, off < BT


def key_tail():
    i, j, valid = token_positions()
    tail = np.zeros((WR, 128), np.float32)
    for m in range(WS):
        tail[:, 64 + m] = i == m
        tail[:, 78 + m] = j == m
    tail[:, 92:120] = tail[:, 64:92]
    tail[:, :120] *= valid[:, None]
    tail[:, 120] = np.where(valid, 0.0, -1e30)
    return tail


def pick_lanes(i, j):
    lane = np.arange(128)[None, :]
    m = np.clip((lane - 64) % 28, 0, 27)
    is_w = m >= 14
    fwd = jnp.where(is_w, 32 + j[:, None] - (m - 14) + 13, i[:, None] - m + 13)
    fwd = jnp.where((lane >= 64) & (lane < 120), fwd, 0)
    d = lane % 32
    pos = jnp.where(lane >= 32, j[:, None], i[:, None]) + 13 - d
    ok = (pos >= 0) & (pos < WS) & (lane < 64) & (d < 27)
    back = jnp.where(ok, pos + jnp.where(lane >= 32, 78, 64), 127)
    return fwd.astype(jnp.int32), back.astype(jnp.int32)


def dotf(a, b, dims):
    return lax.dot_general(a, b, (dims, ((), ())), preferred_element_type=F32)


NN = ((1,), (0,))
NT = ((1,), (1,))
TN = ((0,), (0,))


def compute_kernel(
    x_ref, cot_ref, mask_ref, w_ref, vec_ref, qkvb_ref, fc1b_ref, ktail_ref, fwd_ref, back_ref, tab_ref, tabt_ref,
    out_ref, gn_ref, gh_ref, g_ref, vg_ref, tg_ref,
    nrm, proj, qaug, kaug, vals, probs, att, hid, nr2, mix, gn2, act, gup, gml, gbl, dqkv,
):
    g1, b1, pb, g2, b2, fb = (vec_ref[i : i + 1, :] for i in range(6))

    def stats(v):
        mu = jnp.mean(v, axis=-1, keepdims=True)
        c = v - mu
        var = jnp.mean(c * c, axis=-1, keepdims=True)
        return c, lax.rsqrt(var + 1e-6)

    vg_ref[...] = jnp.zeros_like(vg_ref)

    for r0 in range(0, NE, 32):
        rows = slice(r0, r0 + 32)
        c, rs = stats(x_ref[r0 // 8 : r0 // 8 + 4].astype(F32).reshape(32, 768))
        nrm[rows, :] = (mask_ref[rows, :] * (c * rs * g1 + b1)).astype(BF)

    def fwd_t(t, _):
        proj[...] = dotf(nrm[...], w_ref[0, t][:, :576], NN) + qkvb_ref[t]
        for h in range(3):
            hh = 3 * t + h
            qs = (proj[:NR, 64 * h : 64 * h + 64].astype(BF) * BF(0.125)).astype(BF)
            rel = dotf(qs, tabt_ref[...], NN)
            lane = lax.broadcasted_iota(jnp.int32, (NR, 128), 1)
            got = jnp.take_along_axis(rel, fwd_ref[...], axis=1, mode="promise_in_bounds")
            hi = got.astype(BF).astype(F32)
            tail = jnp.where(lane < 92, hi, got - hi)
            tail = jnp.where(lane == 120, 1.0, jnp.where(lane < 120, tail, 0.0)).astype(BF)
            qa = jnp.concatenate([qs, tail[:, 64:]], axis=1)
            qaug[hh] = qa
            for w in range(3):
                src = slice(w * WR, w * WR + WR) if w < 2 else slice(NR, NE)
                k = proj[src, 192 + 64 * h : 256 + 64 * h].astype(BF)
                kaug[hh, w] = jnp.concatenate([k, ktail_ref[:, 64:]], axis=1)
                vals[hh, w] = proj[src, 384 + 64 * h : 448 + 64 * h].astype(BF)
        return 0

    lax.fori_loop(0, 4, fwd_t, 0)
    mix[...] = jnp.zeros_like(mix)

    def att_t(t, _):
        for h in range(3):
            hh = 3 * t + h
            for w in range(3):
                rows = slice(w * WR, w * WR + WR) if w < 2 else slice(2 * WR, NR)
                s = dotf(qaug[hh, rows, :], kaug[hh, w], NT)
                e = jnp.exp(s - jnp.max(s, axis=-1, keepdims=True))
                p = (e * (1.0 / jnp.sum(e, axis=-1, keepdims=True))).astype(BF)
                probs[hh, rows, :] = p
                att[t, rows, 64 * h : 64 * h + 64] = dotf(p, vals[hh, w], NN).astype(BF)
        mix[...] += dotf(att[t], w_ref[0, t][:, 576:], NT)
        return 0

    lax.fori_loop(0, 4, att_t, 0)

    for r0 in range(0, NR, 32):
        rows = slice(r0, r0 + 32)
        x = x_ref[r0 // 8 : r0 // 8 + 4].astype(F32).reshape(32, 768)
        hv = x + mask_ref[rows, :] * (mix[rows, :] + pb)
        hid[rows, :] = hv
        c, rs = stats(hv)
        nr2[rows, :] = (c * rs * g2 + b2).astype(BF)
        gm = mask_ref[rows, :] * cot_ref[r0 // 8 : r0 // 8 + 4].astype(F32).reshape(32, 768)
        gml[rows, :] = gm.astype(BF)
    mix[...] = jnp.zeros_like(mix)
    gn2[...] = jnp.zeros_like(gn2)

    def mlp_t(t, _):
        for f in range(3):
            cols = slice(256 * f, 256 * f + 256)
            for r0 in range(0, NR, 128):
                rows = slice(r0, r0 + 128)
                up = dotf(nr2[rows, :], w_ref[1, t][:, cols], NN) + fc1b_ref[t][:, cols]
                ga = dotf(gml[rows, :], w_ref[2, t][:, cols], NN)
                cdf = 0.5 * (1.0 + lax.erf(up * (1.0 / math.sqrt(2.0))))
                pdf = jnp.exp(-0.5 * up * up) * (1.0 / math.sqrt(2.0 * math.pi))
                act[rows, cols] = (up * cdf).astype(BF)
                gup[rows, cols] = (ga * (cdf + up * pdf)).astype(BF)
        vg_ref[pl.ds(8 + t, 1), :] = jnp.sum(gup[...].astype(F32), axis=0, keepdims=True)
        mix[...] += dotf(act[...], w_ref[2, t], NT)
        gn2[...] += dotf(gup[...], w_ref[1, t], NT)
        g_ref[2, t] = dotf(gml[...], act[...], TN).astype(BF)
        g_ref[1, t] = dotf(nr2[...], gup[...], TN).astype(BF)
        return 0

    lax.fori_loop(0, 4, mlp_t, 0)

    sums = [jnp.zeros((8, 768), F32) for _ in range(4)]

    def fold(v):
        return jnp.sum(v.reshape(4, 8, 768), axis=0)

    for r0 in range(0, NR, 32):
        rows = slice(r0, r0 + 32)
        mk = mask_ref[rows, :]
        gm = mk * cot_ref[r0 // 8 : r0 // 8 + 4].astype(F32).reshape(32, 768)
        hv = hid[rows, :]
        out_ref[r0 // 8 : r0 // 8 + 4] = (mk * (hv + mix[rows, :] + fb)).reshape(4, 8, 768).astype(BF)
        c, rs = stats(hv)
        xh = c * rs
        gn = gn2[rows, :]
        e2 = gn * g2
        gh = gm + rs * (e2 - jnp.mean(e2, axis=-1, keepdims=True) - xh * jnp.mean(e2 * xh, axis=-1, keepdims=True))
        gb = mk * gh
        gh_ref[rows, :] = gh
        gbl[rows, :] = gb.astype(BF)
        for n, v in enumerate((gn * xh, gn, gb, gm)):
            sums[n] = sums[n] + fold(v)
    for n in range(4):
        vg_ref[n : n + 1, :] = jnp.sum(sums[n], axis=0, keepdims=True)
    tg_ref[...] = jnp.zeros_like(tg_ref)
    gn_ref[...] = jnp.zeros_like(gn_ref)

    def bwd_t(t, _):
        att_w = att[t]
        g_ref[0, t, :, 576:] = dotf(gbl[...], att_w, TN).astype(BF)
        proj[:NR, :192] = dotf(gbl[...], w_ref[0, t][:, 576:], NN)
        dqkv[...] = jnp.zeros_like(dqkv)
        for h in range(3):
            hh = 3 * t + h
            lo = 64 * h
            for w in range(3):
                rows = slice(w * WR, w * WR + WR) if w < 2 else slice(2 * WR, NR)
                dst = rows if w < 2 else slice(NR, NE)
                do = proj[rows, lo : lo + 64].astype(BF)
                p = probs[hh, rows, :]
                pf = p.astype(F32)
                dp = dotf(do, vals[hh, w], NT)
                delta = jnp.sum(pf * dp, axis=-1, keepdims=True)
                ds = (pf * (dp - delta)).astype(BF)
                dq = dotf(ds, kaug[hh, w], NN)
                qa = qaug[hh, rows, :]
                dqkv[dst, 192 + lo : 256 + lo] = dotf(ds, qa, TN)[:, :64].astype(BF)
                dqkv[dst, 384 + lo : 448 + lo] = dotf(p, do, TN).astype(BF)
                rel = jnp.take_along_axis(dq, back_ref[rows, :], axis=1, mode="promise_in_bounds").astype(BF)
                gq = dq[:, :64] * 0.125 + dotf(rel, tab_ref[...], NN)
                dqkv[rows, lo : lo + 64] = gq.astype(BF)
                tg_ref[...] += dotf(rel, qa, TN)[:64]
        vg_ref[pl.ds(12 + t, 1), 0:576] = jnp.sum(dqkv[...].astype(F32), axis=0, keepdims=True)
        g_ref[0, t, :, :576] = dotf(nrm[...], dqkv[...], TN).astype(BF)
        gn_ref[...] += dotf(dqkv[...], w_ref[0, t][:, :576], NT)
        return 0

    lax.fori_loop(0, 4, bwd_t, 0)


def compute(x, cot, mask, w, vec, qkvb, fc1b, ktail, fwd, back, tab, tabt):
    shp = jax.ShapeDtypeStruct
    vm = pl.BlockSpec(memory_space=pltpu.VMEM)
    return pl.pallas_call(
        compute_kernel,
        out_shape=(
            shp((NR // 8, 8, 768), BF), shp((NE, 768), F32), shp((NR, 768), F32), shp((3, 4, 768, 768), BF),
            shp((16, 768), F32), shp((64, 128), F32),
        ),
        in_specs=[vm] * 12,
        out_specs=(vm,) * 6,
        scratch_shapes=[
            pltpu.VMEM((NE, 768), BF), pltpu.VMEM((NE, 576), F32), pltpu.VMEM((HEADS, NR, 128), BF),
            pltpu.VMEM((HEADS, 3, WR, 128), BF), pltpu.VMEM((HEADS, 3, WR, 64), BF), pltpu.VMEM((HEADS, NR, WR), BF),
            pltpu.VMEM((4, NR, 192), BF), pltpu.VMEM((NR, 768), F32), pltpu.VMEM((NR, 768), BF),
            pltpu.VMEM((NR, 768), F32), pltpu.VMEM((NR, 768), F32), pltpu.VMEM((NR, 768), BF), pltpu.VMEM((NR, 768), BF),
            pltpu.VMEM((NR, 768), BF), pltpu.VMEM((NR, 768), BF), pltpu.VMEM((NE, 576), BF),
        ],
        compiler_params=pltpu.CompilerParams(vmem_limit_bytes=67043328),
    )(x, cot, mask, w, vec, qkvb, fc1b, ktail, fwd, back, tab, tabt)


MESH = pl.DeviceIdType.MESH


class Links:
    def __init__(self, send, recv):
        self.send, self.recv = send, recv
        self.x = lax.axis_index("dp")
        win = lax.axis_index("win")
        self.y, self.c = win // 2, win % 2
        self.z = lax.axis_index("tensor")
        self.xn = (1 - self.x, win, self.z)
        self.yn = (self.x, (1 - self.y) * 2 + self.c, self.z)
        self.sib = (self.x, self.y * 2 + 1 - self.c, self.z)
        self.win = win

    def zdev(self, z):
        return (self.x, self.win, z)

    def barrier(self):
        sem = pltpu.get_barrier_semaphore()
        others = [self.xn, self.yn, self.sib] + [self.zdev((self.z + d) % 4) for d in (1, 2, 3)]
        for dev in others:
            pl.semaphore_signal(sem, inc=1, device_id=dev, device_id_type=MESH)
        pl.semaphore_wait(sem, len(others))

    def copy(self, src, dst, n, dev):
        return pltpu.make_async_remote_copy(
            src_ref=src, dst_ref=dst, send_sem=self.send.at[n], recv_sem=self.recv.at[n], device_id=dev,
            device_id_type=MESH,
        )


AG_SEMS = 3 * 39


class Gather:
    def __init__(self, links, shards, w, local, base):
        self.l, self.shards, self.w, self.local, self.base = links, shards, w, local, base

    def sem(self, k, kind, i):
        start = {"z": 0, "x": 3, "y": 7, "hx": 11, "hy": 15, "so": 19, "sx": 23, "sy": 27, "sa": 31, "sb": 35}[kind]
        return self.base + k * 39 + start + i

    def rank(self, i):
        return (self.l.z + 4 - i) % 4

    def piece(self, k, i, px, py, c, half=None):
        ref = self.w.at[k, self.rank(i), px, py, c]
        return ref if half is None else ref.at[pl.ds(48 * half, 48)]

    def move(self, k, kind, i):
        l = self.l
        if kind == "z":
            src = self.shards[k]
            return l.copy(src, self.piece(k, 0, l.x, l.y, l.c), self.sem(k, kind, i - 1), l.zdev((l.z + i) % 4))
        px, py, half, dev = {
            "x": (l.x, l.y, None, l.xn), "y": (l.x, l.y, None, l.yn),
            "hx": (l.x, 1 - l.y, 1, l.xn), "hy": (1 - l.x, l.y, 0, l.yn),
            "so": (l.x, l.y, None, l.sib), "sx": (1 - l.x, l.y, None, l.sib), "sy": (l.x, 1 - l.y, None, l.sib),
            "sa": (1 - l.x, 1 - l.y, 0, l.sib), "sb": (1 - l.x, 1 - l.y, 1, l.sib),
        }[kind]
        dst = self.piece(k, i, px, py, l.c, half)
        own = kind in ("x", "y", "so") and i == 0
        return l.copy(self.shards[k] if own else dst, dst, self.sem(k, kind, i), dev)

    def start(self, k, kind, i):
        self.move(k, kind, i).start()

    def arrived(self, k, kind, i):
        self.move(k, kind, i).wait_recv()

    def keep(self, k):
        l = self.l
        return pltpu.make_async_copy(self.shards[k], self.piece(k, 0, l.x, l.y, l.c), self.local.at[k])

    def own_z(self, k):
        for i in (1, 3, 2):
            self.start(k, "z", i)

    def along(self, k, i):
        if i:
            self.arrived(k, "z", i)
        else:
            self.keep(k).start()
        for kind in ("x", "y", "so"):
            self.start(k, kind, i)

    def across(self, k, i):
        self.arrived(k, "x", i)
        self.start(k, "hy", i)
        self.start(k, "sx", i)
        self.arrived(k, "y", i)
        self.start(k, "hx", i)
        self.start(k, "sy", i)

    def corner(self, k, i):
        self.arrived(k, "hy", i)
        self.start(k, "sa", i)
        self.arrived(k, "hx", i)
        self.start(k, "sb", i)

    def partner(self, k, i):
        for kind in ("so", "sx", "sy", "sa", "sb"):
            self.arrived(k, kind, i)
        if not i:
            self.keep(k).wait()

    def drain(self, k, i):
        for kind in ("x", "y", "hx", "hy", "so", "sx", "sy", "sa", "sb"):
            self.move(k, kind, i).wait_send()


RS_SEMS = 12 * 6


class Scatter:
    def __init__(self, links, w, r1, r2, r3, r4, base):
        self.l, self.w, self.r1, self.r2, self.r3, self.r4, self.base = links, w, r1, r2, r3, r4, base

    def g(self, k, i):
        return self.w.at[k, (self.l.z + 4 - i) % 4]

    def moves(self, k, i, stage):
        l, n = self.l, 4 * k + i
        s = self.base + 6 * n
        g = self.g(k, i)
        if stage == 1:
            return [l.copy(g.at[:, :, 1 - l.c], self.r1.at[n], s, l.sib)]
        if stage == 2:
            return [
                l.copy(g.at[:, 1 - l.y, l.c, 0:48], self.r2.at[n, 0], s + 1, l.yn),
                l.copy(g.at[1 - l.x, :, l.c, 48:96], self.r2.at[n, 1], s + 2, l.xn),
            ]
        if stage == 3:
            return [
                l.copy(g.at[1 - l.x, l.y, l.c, 0:48], self.r3.at[n, 0], s + 3, l.xn),
                l.copy(g.at[l.x, 1 - l.y, l.c, 48:96], self.r3.at[n, 1], s + 4, l.yn),
            ]
        return [l.copy(g.at[l.x, l.y, l.c], self.r4.at[k, i - 1], s + 5, l.zdev((l.z + 4 - i) % 4))] if i else []

    def start(self, k, i, stage):
        for m in self.moves(k, i, stage):
            m.start()

    def wait(self, k, i, stage):
        for m in self.moves(k, i, stage):
            m.wait_recv()

    def step(self, k, i, stage):
        l, g, n = self.l, self.g(k, i), 4 * k + i
        self.wait(k, i, stage - 1)
        if stage == 2:
            for a in range(2):
                for b in range(2):
                    ref = g.at[a, b, l.c]
                    ref[...] = ref[...] + self.r1[n, a, b]
        elif stage == 3:
            for a in range(2):
                ref = g.at[a, l.y, l.c, 0:48]
                ref[...] = ref[...] + self.r2[n, 0, a]
                ref = g.at[l.x, a, l.c, 48:96]
                ref[...] = ref[...] + self.r2[n, 1, a]
        else:
            for h in range(2):
                ref = g.at[l.x, l.y, l.c, pl.ds(48 * h, 48)]
                ref[...] = ref[...] + self.r3[n, h]
        self.start(k, i, stage)

    def total(self, k):
        l = self.l
        fin = self.g(k, 0)[l.x, l.y, l.c].astype(F32)
        for i in (1, 2, 3):
            self.wait(k, i, 4)
            fin = fin + self.r4[k, i - 1].astype(F32)
        return fin

    def drain(self):
        for k in range(3):
            for i in range(4):
                for stage in (1, 2, 3, 4):
                    for m in self.moves(k, i, stage):
                        m.wait_send()


class Rows:
    TABLE = block_table()

    def __init__(self, links, local):
        self.l, self.local = links, local

    @staticmethod
    def home(block):
        m, b = divmod(int(block), 12)
        return b // 3, m * 3 + b % 3

    @staticmethod
    def unit(slot):
        return 7 * slot if slot < 9 else NR // 8 + 7 * (slot - 9)

    def inward(self, held, rows, slots, base, do):
        l = self.l
        for me in range(4):

            @pl.when(l.z == me)
            def _():
                sent = 0
                for slot in slots:
                    for step in range(4):
                        dev = (me + step) % 4
                        owner, idx = self.home(self.TABLE[dev, slot])
                        if owner != me:
                            continue
                        dst = rows.at[pl.ds(self.unit(slot), 7)]
                        if dev == me:
                            if do != "drain":
                                c = pltpu.make_async_copy(held.at[idx], dst, self.local.at[base + slot])
                                c.start() if do == "start" else c.wait()
                            continue
                        sent += 1
                        if do == "wait":
                            continue
                        c = pltpu.make_async_remote_copy(
                            src_ref=held.at[idx], dst_ref=dst, send_sem=l.send.at[base + sent - 1],
                            recv_sem=l.recv.at[base + slot], device_id=l.zdev(dev), device_id_type=MESH,
                        )
                        c.start() if do == "start" else c.wait_send()
                    owner, idx = self.home(self.TABLE[me, slot])
                    if do == "wait" and owner != me:
                        pltpu.make_async_remote_copy(
                            src_ref=held.at[0], dst_ref=rows.at[pl.ds(self.unit(slot), 7)], send_sem=l.send.at[base],
                            recv_sem=l.recv.at[base + slot], device_id=l.zdev(owner), device_id_type=MESH,
                        ).wait_recv()

    def outward(self, rows, held, base, mine, do):
        l = self.l
        for me in range(4):

            @pl.when(l.z == me)
            def _():
                for slot in range(9):
                    owner, idx = self.home(self.TABLE[me, slot])
                    src = rows.at[pl.ds(7 * slot, 7)]
                    if owner == me:
                        if do != "drain":
                            c = pltpu.make_async_copy(src, held.at[idx], self.local.at[mine + slot])
                            c.start() if do == "start" else c.wait()
                    elif do != "wait":
                        c = pltpu.make_async_remote_copy(
                            src_ref=src, dst_ref=held.at[idx], send_sem=l.send.at[base + slot],
                            recv_sem=l.recv.at[base + idx], device_id=l.zdev(owner), device_id_type=MESH,
                        )
                        c.start() if do == "start" else c.wait_send()
                for dev in range(4):
                    for slot in range(9):
                        owner, idx = self.home(self.TABLE[dev, slot])
                        if do == "wait" and owner == me and dev != me:
                            pltpu.make_async_remote_copy(
                                src_ref=rows.at[pl.ds(0, 7)], dst_ref=held.at[idx], send_sem=l.send.at[base],
                                recv_sem=l.recv.at[base + idx], device_id=l.zdev(dev), device_id_type=MESH,
                            ).wait_recv()


XS, CS, BS = 0, 13, 22
AG0 = BS + 3
RET0 = AG0 + AG_SEMS
DX0 = RET0 + 9
SH0 = DX0 + 9
VS0 = SH0 + 3
RS0 = VS0 + 10
SEMS = RS0 + RS_SEMS
X_SLOTS = (0, 1, 2, 3, 4, 5, 6, 7, 9, 10, 11, 12)

ORD = (0, 1, 3, 2)
BACK = (2, 1, 3, 0)
BLOCKS = ((0, 0), (1, 0), (0, 1), (0, 3), (0, 2), (2, 0), (1, 1), (2, 1), (1, 3), (2, 3), (1, 2), (2, 2))


PLACES = (
    [("M", n, j) for n in range(4) for j in range(5)] + ["N"] + [("B", n, j) for n in range(4) for j in range(3)]
    + ["T0", "T1", "T2", "S0", "S1", "S2", "S3", "S4", "T3"]
)
TICKS = {1: ("F", 0, 0), 2: ("F", 0, 2), 3: ("F", 1, 1), 4: ("F", 2, 1), 5: ("F", 3, 1), 6: "L", 7: ("M", 0, 0), 8: ("M", 0, 4),
         9: ("M", 1, 1), 10: ("M", 1, 4), 11: ("M", 2, 1)}
MLP_LAGS = ((0, 6, 11), (1, 8, 12))
BWD_LAGS = (0, 3, 5)


def timetable():
    plan = {}

    def put(place, *event):
        plan.setdefault(place, []).append(event)

    for s, place in TICKS.items():
        put(place, "tick", s)
    for n in range(4):
        for k, lags in zip((2, 1), MLP_LAGS):
            made = PLACES.index(("M", n, 4)) + 1
            for stage, lag in zip((2, 3, 4), lags):
                put(PLACES[made + lag], "step", k, ORD[n], stage)
        made = PLACES.index(("B", n, 2)) + 1
        for stage, lag in zip((2, 3, 4), BWD_LAGS):
            put(PLACES[made + lag], "step", 0, BACK[n], stage)
    return plan


def places(rows, first):
    r = lax.broadcasted_iota(jnp.int32, (rows, 128), 0)
    blk = sum((r >= BP * n).astype(jnp.int32) for n in range(1, 4)) if rows == WR else jnp.zeros_like(r)
    off = r - BP * blk
    token = (blk + first) * BT + jnp.minimum(off, BT - 1)
    i = (token * 4682) >> 16
    return i, token - WS * i, off < BT


def lanes_of(i, j):
    lane = lax.broadcasted_iota(jnp.int32, i.shape, 1)
    m = lane - 64
    m = m - 28 * ((m >= 28).astype(jnp.int32) + (m >= 56).astype(jnp.int32))
    fwd = jnp.where(m >= 14, 32 + j - (m - 14) + 13, i - m + 13)
    fwd = jnp.where((lane >= 64) & (lane < 120), fwd, 0)
    d = lane & 31
    pos = jnp.where(lane >= 32, j, i) + 13 - d
    ok = (pos >= 0) & (pos < WS) & (lane < 64) & (d < 27)
    return fwd, jnp.where(ok, pos + jnp.where(lane >= 32, 78, 64), 127)


def fill_tables(z, ids, mask_ref, fwd_ref, back_ref):
    across = (GRID + WS - 1) // WS

    def valid(w, i, j, ok):
        a = lax.div(w, jnp.int32(across))
        hi = jnp.where(w < across * across, GRID - a * WS, 0)
        wi = GRID - (w - across * a) * WS
        return jnp.where(ok & (i < hi) & (j < wi), 1.0, 0.0)[:, :1]

    def window(n):
        m, s = (jnp.int32(v) for v in WINDOWS_OF[3][n])
        for dev in range(3):
            m = jnp.where(z == dev, WINDOWS_OF[dev][n][0], m)
            s = jnp.where(z == dev, WINDOWS_OF[dev][n][1], s)
        return ids[m, 0, s]

    i, j, ok = places(WR, 0)
    fwd, back = lanes_of(i, j)
    shared = ids[SHARED[0], 0, SHARED[1]]
    for n in range(2):
        rows = slice(n * WR, n * WR + WR)
        fwd_ref[rows, :] = fwd
        back_ref[rows, :] = back
        mask_ref[rows, :] = valid(window(n), i, j, ok)
    mask_ref[NR:NE, :] = valid(shared, i, j, ok)
    i, j, ok = places(QR, z)
    fwd, back = lanes_of(i, j)
    fwd_ref[2 * WR : NR, :] = fwd
    back_ref[2 * WR : NR, :] = back
    mask_ref[2 * WR : NR, :] = valid(shared, i, j, ok)


def whole_kernel(
    x_in, cot_in, ids, qkv_w, proj_w, fc1_w, fc2_w, vec_ref, ktail_ref, tab_ref,
    g_qkv, g_proj, g_fc1, g_fc2, out_h, dx_h, v0, v1, v2, v3, v4, v5, fc1b_out, qvb_out, relh_out, relw_out,
    shard0, small, mask_ref, fwd_ref, back_ref,
    w, r1, r2, r3, r4, x, cot, sm, ob, dx, gn, hid, gn2, gs, gsr, vg, tg, vr, tr,
    nrm, proj, qaug, kaug, vals, probs, att, nr2, act, gup, gml, dqkv, send, recv, local,
):
    links = Links(send, recv)
    z = links.z
    rows_of = Rows(links, local)
    ag = Gather(links, (shard0, fc1_w, fc2_w), w, local.at[pl.ds(40, 3)], AG0)
    rs = Scatter(links, w, r1, r2, r3, r4, RS0)
    g1, b1, pb, g2, b2, fb = (vec_ref[i : i + 1, :] for i in range(6))

    def rank(order, m):
        i = jnp.int32(order[3])
        for n in range(3):
            i = jnp.where(m == n, order[n], i)
        return (z + 4 - i) % 4

    def weight(k, t):
        return w[k, t].reshape(768, 768)

    def tick(s):
        if s + 2 < 12:
            ag.along(*BLOCKS[s + 2])
        if s + 1 < 12:
            ag.across(*BLOCKS[s + 1])
        ag.corner(*BLOCKS[s])

    def at(m, plan):
        for n, todo in plan.items():

            @pl.when(m == n)
            def _():
                for f in todo:
                    f()

    plan = timetable()

    def run(events):
        for what, *which in events:
            if what == "tick":
                tick(*which)
            else:
                rs.step(*which)

    def now(place):
        run(plan.get(place, ()))

    def hook(m, loop, j):
        for n in range(4):
            todo = plan.get((loop, n, j))
            if todo:

                @pl.when(m == n)
                def _():
                    run(todo)

    def stats(v):
        mu = jnp.mean(v, axis=-1, keepdims=True)
        c = v - mu
        var = jnp.mean(c * c, axis=-1, keepdims=True)
        return c, lax.rsqrt(var + 1e-6)

    for t in range(3):
        shard0[:, 192 * t : 192 * t + 192] = qkv_w[t]
    shard0[:, 576:] = proj_w[...].astype(F32).T.astype(BF)
    small[...] = jnp.zeros_like(small)
    small[0:1, :] = vec_ref[6:7, :]
    small[1:2, 0:192] = vec_ref[8:9, 0:192]
    small[1:2, 384:576] = vec_ref[9:10, 0:192]
    x[63] = jnp.zeros((8, 768), BF)
    cot[63] = jnp.zeros((8, 768), BF)
    links.barrier()
    for b in (0, 1):
        ag.along(*BLOCKS[b])
    bias = [links.copy(small, sm.at[z], BS + d - 1, links.zdev((z + d) % 4)) for d in (1, 2, 3)]
    keep_bias = pltpu.make_async_copy(small, sm.at[z], local.at[43])
    keep_bias.start()
    for c in bias:
        c.start()
    rows_of.inward(x_in, x, X_SLOTS, XS, "start")
    ag.own_z(0)
    rows_of.inward(cot_in, cot, range(9), CS, "start")
    ag.own_z(1)

    vg[...] = jnp.zeros_like(vg)
    tg[...] = jnp.zeros_like(tg)
    fill_tables(z, ids, mask_ref, fwd_ref, back_ref)
    rows_of.inward(x_in, x, X_SLOTS, XS, "wait")
    x[56:63] = x[pl.ds(NR // 8 + 7 * z, 7)]
    for c in bias:
        c.wait_recv()
    keep_bias.wait()

    for r0 in range(0, NE, 32):
        rows = slice(r0, r0 + 32)
        c, rstd = stats(x[r0 // 8 : r0 // 8 + 4].astype(F32).reshape(32, 768))
        nrm[rows, :] = (mask_ref[rows, :] * (c * rstd * g1 + b1)).astype(BF)

    ag.across(*BLOCKS[0])
    tick(0)
    ag.own_z(2)
    mix = gn.at[pl.ds(0, NR)]
    mix[...] = jnp.zeros_like(mix)

    def fwd_t(m, _):
        at(m, {n: [partial(ag.partner, 0, ORD[n])] for n in range(4)})
        t = rank(ORD, m)
        proj[...] = dotf(nrm[...], weight(0, t)[:, :576], NN) + sm[t][1:2, :576]
        for h in range(3):
            hh = 3 * t + h
            qs = (proj[:NR, 64 * h : 64 * h + 64].astype(BF) * BF(0.125)).astype(BF)
            rel = dotf(qs, tab_ref[...], NT) * 8.0
            lane = lax.broadcasted_iota(jnp.int32, (NR, 128), 1)
            got = jnp.take_along_axis(rel, fwd_ref[...], axis=1, mode="promise_in_bounds")
            hi = got.astype(BF).astype(F32)
            tail = jnp.where(lane < 92, hi, got - hi)
            tail = jnp.where(lane == 120, 1.0, jnp.where(lane < 120, tail, 0.0)).astype(BF)
            qa = jnp.concatenate([qs, tail[:, 64:]], axis=1)
            qaug[hh] = qa
            for wn in range(3):
                src = slice(wn * WR, wn * WR + WR) if wn < 2 else slice(NR, NE)
                k = proj[src, 192 + 64 * h : 256 + 64 * h].astype(BF)
                kaug[hh, wn] = jnp.concatenate([k, ktail_ref[:, 64:]], axis=1)
                vals[hh, wn] = proj[src, 384 + 64 * h : 448 + 64 * h].astype(BF)
        hook(m, "F", 0)
        for h in range(3):
            hh = 3 * t + h
            for wn in range(3):
                rows = slice(wn * WR, wn * WR + WR) if wn < 2 else slice(2 * WR, NR)
                s = dotf(qaug[hh, rows, :], kaug[hh, wn], NT)
                e = jnp.exp(s - jnp.max(s, axis=-1, keepdims=True))
                p = (e * (1.0 / jnp.sum(e, axis=-1, keepdims=True))).astype(BF)
                probs[hh, rows, :] = p
                att[t, rows, 64 * h : 64 * h + 64] = dotf(p, vals[hh, wn], NN).astype(BF)
            if h == 1:
                hook(m, "F", 1)
        mix[...] += dotf(att[t], weight(0, t)[:, 576:], NT)
        hook(m, "F", 2)
        return 0

    lax.fori_loop(0, 4, fwd_t, 0)
    rows_of.inward(cot_in, cot, range(9), CS, "wait")
    now("L")

    for r0 in range(0, NR, 32):
        rows = slice(r0, r0 + 32)
        xv = x[r0 // 8 : r0 // 8 + 4].astype(F32).reshape(32, 768)
        hv = xv + mask_ref[rows, :] * (mix[rows, :] + pb)
        hid[rows, :] = hv
        c, rstd = stats(hv)
        nr2[rows, :] = (c * rstd * g2 + b2).astype(BF)
        gm = mask_ref[rows, :] * cot[r0 // 8 : r0 // 8 + 4].astype(F32).reshape(32, 768)
        gml[rows, :] = gm.astype(BF)
    mix[...] = jnp.zeros_like(mix)
    gn2[...] = jnp.zeros_like(gn2)

    def mlp_t(m, _):
        at(m, {n: [partial(ag.partner, 1, ORD[n]), partial(ag.partner, 2, ORD[n])] for n in range(4)})
        t = rank(ORD, m)
        for f in range(3):
            cols = slice(256 * f, 256 * f + 256)
            for r0 in range(0, NR, 128):
                rows = slice(r0, r0 + 128)
                up = dotf(nr2[rows, :], weight(1, t)[:, cols], NN) + sm[t][0:1, cols]
                ga = dotf(gml[rows, :], weight(2, t)[:, cols], NN)
                cdf = 0.5 * (1.0 + lax.erf(up * (1.0 / math.sqrt(2.0))))
                pdf = jnp.exp(-0.5 * up * up) * (1.0 / math.sqrt(2.0 * math.pi))
                act[rows, cols] = (up * cdf).astype(BF)
                gup[rows, cols] = (ga * (cdf + up * pdf)).astype(BF)
            hook(m, "M", f)
        vg[0, pl.ds(8 + t, 1), :] = jnp.sum(gup[...].astype(F32), axis=0, keepdims=True)
        mix[...] += dotf(act[...], weight(2, t), NT)
        hook(m, "M", 3)
        gn2[...] += dotf(gup[...], weight(1, t), NT)
        hook(m, "M", 4)
        at(m, {n: [partial(ag.drain, 2, ORD[n])] for n in range(4)})
        w[2, t] = dotf(gml[...], act[...], TN).astype(BF).reshape(2, 2, 2, 96, 768)
        at(m, {n: [partial(rs.start, 2, ORD[n], 1), partial(ag.drain, 1, ORD[n])] for n in range(4)})
        w[1, t] = dotf(nr2[...], gup[...], TN).astype(BF).reshape(2, 2, 2, 96, 768)
        at(m, {n: [partial(rs.start, 1, ORD[n], 1)] for n in range(4)})
        return 0

    lax.fori_loop(0, 4, mlp_t, 0)
    now("N")

    sums = [jnp.zeros((8, 768), F32) for _ in range(4)]

    def fold(v):
        return jnp.sum(v.reshape(4, 8, 768), axis=0)

    gbl = act
    for r0 in range(0, NR, 32):
        rows = slice(r0, r0 + 32)
        mk = mask_ref[rows, :]
        gm = mk * cot[r0 // 8 : r0 // 8 + 4].astype(F32).reshape(32, 768)
        hv = hid[rows, :]
        ob[r0 // 8 : r0 // 8 + 4] = (mk * (hv + mix[rows, :] + fb)).reshape(4, 8, 768).astype(BF)
        c, rstd = stats(hv)
        xh = c * rstd
        gv = gn2[rows, :]
        e2 = gv * g2
        gh = gm + rstd * (e2 - jnp.mean(e2, axis=-1, keepdims=True) - xh * jnp.mean(e2 * xh, axis=-1, keepdims=True))
        gb = mk * gh
        hid[rows, :] = gh
        gbl[rows, :] = gb.astype(BF)
        for n, v in enumerate((gv * xh, gv, gb, gm)):
            sums[n] = sums[n] + fold(v)
    for n in range(4):
        vg[0, n : n + 1, :] = jnp.sum(sums[n], axis=0, keepdims=True)
    rows_of.outward(ob, out_h, RET0, 22, "start")
    gn[...] = jnp.zeros_like(gn)

    def bwd_t(m, _):
        t = rank(BACK, m)
        at(m, {n: [partial(ag.drain, 0, BACK[n])] for n in range(4)})
        att_w = att[t]
        proj[:NR, :192] = dotf(gbl[...], weight(0, t)[:, 576:], NN)
        dqkv[...] = jnp.zeros_like(dqkv)
        for h in range(3):
            hh = 3 * t + h
            lo = 64 * h
            for wn in range(3):
                rows = slice(wn * WR, wn * WR + WR) if wn < 2 else slice(2 * WR, NR)
                dst = rows if wn < 2 else slice(NR, NE)
                do = proj[rows, lo : lo + 64].astype(BF)
                p = probs[hh, rows, :]
                pf = p.astype(F32)
                dp = dotf(do, vals[hh, wn], NT)
                delta = jnp.sum(pf * dp, axis=-1, keepdims=True)
                ds = (pf * (dp - delta)).astype(BF)
                dq = dotf(ds, kaug[hh, wn], NN)
                qa = qaug[hh, rows, :]
                dqkv[dst, 192 + lo : 256 + lo] = dotf(ds, qa, TN)[:, :64].astype(BF)
                dqkv[dst, 384 + lo : 448 + lo] = dotf(p, do, TN).astype(BF)
                rel = jnp.take_along_axis(dq, back_ref[rows, :], axis=1, mode="promise_in_bounds").astype(BF)
                gq = dq[:, :64] * 0.125 + dotf(rel, tab_ref[...], NN)
                dqkv[rows, lo : lo + 64] = gq.astype(BF)
                tg[0] += dotf(rel, qa, TN)[:64]
            hook(m, "B", h)
        vg[0, pl.ds(12 + t, 1), 0:576] = jnp.sum(dqkv[...].astype(F32), axis=0, keepdims=True)
        gn[...] += dotf(dqkv[...], weight(0, t)[:, :576], NT)
        gw = jnp.concatenate([dotf(nrm[...], dqkv[...], TN).astype(BF), dotf(gbl[...], att_w, TN).astype(BF)], axis=1)
        w[0, t] = gw.reshape(2, 2, 2, 96, 768)
        at(m, {n: [partial(rs.start, 0, BACK[n], 1)] for n in range(4)})
        return 0

    lax.fori_loop(0, 4, bwd_t, 0)

    gs[...] = gn[NR:].reshape(WR // 8, 8, 768).astype(BF)
    sh = [
        links.copy(gs.at[pl.ds(7 * ((z + d) % 4), 7)], gsr.at[d - 1], SH0 + d - 1, links.zdev((z + d) % 4)) for d in (1, 2, 3)
    ]
    for c in sh:
        c.start()
    now("T0")
    for c in sh:
        c.wait_recv()
    now("T1")
    first_norm_back(links, x, mask_ref, vec_ref, gn, hid, gsr, dx, vg.at[0])
    rows_of.outward(dx, dx_h, DX0, 31, "start")
    now("T2")
    small_sums(links, vg, tg, vr, tr, now)
    now("T3")
    for n, ref in enumerate((v0, v1, v2, v3, v4, v5)):
        for c in range(6):
            ref[c : c + 1, :] = vg[5, n : n + 1, 128 * c : 128 * c + 128]
    for t in range(4):
        for c in range(6):
            fc1b_out[6 * t + c : 6 * t + c + 1, :] = vg[5, 8 + t : 9 + t, 128 * c : 128 * c + 128]
        qvb_out[0:1, 192 * t : 192 * t + 192] = vg[5, 12 + t : 13 + t, 0:192]
        qvb_out[1:2, 192 * t : 192 * t + 192] = vg[5, 12 + t : 13 + t, 384:576]
    relh_out[...] = tg[5, 0:27, :64] * 8.0
    relw_out[...] = tg[5, 32:59, :64] * 8.0
    g_fc2[...] = rs.total(2)
    g_fc1[...] = rs.total(1)
    fin = rs.total(0)
    for t in range(3):
        g_qkv[t] = fin[:, 192 * t : 192 * t + 192]
    g_proj[...] = fin[:, 576:].T
    rows_of.outward(ob, out_h, RET0, 22, "wait")
    rows_of.outward(dx, dx_h, DX0, 31, "wait")
    rows_of.outward(ob, out_h, RET0, 22, "drain")
    rows_of.outward(dx, dx_h, DX0, 31, "drain")
    rows_of.inward(x_in, x, X_SLOTS, XS, "drain")
    rows_of.inward(cot_in, cot, range(9), CS, "drain")
    for c in sh + bias:
        c.wait_send()
    for k in range(3):
        for i in (1, 2, 3):
            ag.move(k, "z", i).wait_send()
    rs.drain()


def first_norm_back(links, x, mask_ref, gain_ref, gn_ref, gh_ref, gsr, dx, vg):
    own = gn_ref[pl.ds(pl.multiple_of(NR + 56 * links.z, 8), 56), :]
    for d in range(3):
        own = own + gsr[d].astype(F32).reshape(56, 768)
    quarter = gn_ref[2 * WR : 2 * WR + 56, :] + own
    g1 = gain_ref[0:1, :]
    s_gain = jnp.zeros((8, 768), F32)
    s_bias = jnp.zeros((8, 768), F32)
    for r0, n in [(r, 32) for r in range(0, 2 * WR, 32)] + [(2 * WR, 56)]:
        rows = slice(r0, r0 + n)
        v = x[r0 // 8 : (r0 + n) // 8].astype(F32).reshape(n, 768)
        c = v - jnp.mean(v, axis=-1, keepdims=True)
        rs = lax.rsqrt(jnp.mean(c * c, axis=-1, keepdims=True) + 1e-6)
        xh = c * rs
        gn = mask_ref[rows, :] * (gn_ref[rows, :] if n == 32 else quarter)
        e1 = gn * g1
        gx = gh_ref[rows, :] + rs * (
            e1 - jnp.mean(e1, axis=-1, keepdims=True) - xh * jnp.mean(e1 * xh, axis=-1, keepdims=True)
        )
        dx[r0 // 8 : (r0 + n) // 8] = gx.reshape(n // 8, 8, 768).astype(BF)
        s_gain = s_gain + jnp.sum((gn * xh).reshape(n // 8, 8, 768), axis=0)
        s_bias = s_bias + jnp.sum(gn.reshape(n // 8, 8, 768), axis=0)
    vg[4:5, :] = jnp.sum(s_gain, axis=0, keepdims=True)
    vg[5:6, :] = jnp.sum(s_bias, axis=0, keepdims=True)


def small_sums(links, vg, tg, vr, tr, now):
    l = links
    partners = [l.sib, l.xn, l.yn, l.zdev((l.z // 2) * 2 + 1 - l.z % 2), l.zdev((l.z + 2) % 4)]
    copies = []
    for n, dev in enumerate(partners):
        pair = [l.copy(vg.at[n], vr.at[n], VS0 + 2 * n, dev), l.copy(tg.at[n], tr.at[n], VS0 + 2 * n + 1, dev)]
        for c in pair:
            c.start()
        now(f"S{n}")
        for c in pair:
            c.wait_recv()
        vg[n + 1] = vg[n] + vr[n]
        tg[n + 1] = tg[n] + tr[n]
        copies += pair
    for c in copies:
        c.wait_send()


def whole_call(xh, coth, ids, qkv_w, proj_w, fc1_w, fc2_w, vec, ktail, tab):
    shp = jax.ShapeDtypeStruct
    vm = pl.BlockSpec(memory_space=pltpu.VMEM)
    hbm = pl.BlockSpec(memory_space=pl.ANY)
    V = pltpu.VMEM
    dma = pltpu.SemaphoreType.DMA
    return pl.pallas_call(
        whole_kernel,
        out_shape=(
            shp((3, 96, 192), F32), shp((192, 96), F32), shp((96, 768), F32), shp((96, 768), F32),
            shp((9, 7, 8, 768), BF), shp((9, 7, 8, 768), BF), *[shp((6, 128), F32)] * 6, shp((24, 128), F32),
            shp((2, 768), F32), shp((27, 64), F32), shp((27, 64), F32),
        ),
        in_specs=[hbm, hbm, pl.BlockSpec(memory_space=pltpu.SMEM)] + [vm] * 7,
        out_specs=(vm, vm, vm, vm, hbm, hbm) + (vm,) * 10,
        scratch_shapes=[
            V((96, 768), BF), V((8, 768), F32), V((NE, 1), F32), V((NR, 128), jnp.int32), V((NR, 128), jnp.int32),
            V((3, 4, 2, 2, 2, 96, 768), BF), V((12, 2, 2, 96, 768), BF), V((12, 2, 2, 48, 768), BF), V((12, 2, 48, 768), BF),
            V((3, 3, 96, 768), BF), V((NE // 8, 8, 768), BF), V((NR // 8, 8, 768), BF), V((4, 8, 768), F32),
            V((NR // 8, 8, 768), BF), V((NR // 8, 8, 768), BF), V((NE, 768), F32), V((NR, 768), F32), V((NR, 768), F32),
            V((WR // 8, 8, 768), BF), V((3, 7, 8, 768), BF), V((6, 16, 768), F32), V((6, 64, 128), F32),
            V((5, 16, 768), F32), V((5, 64, 128), F32),
            V((NE, 768), BF), V((NE, 576), F32), V((HEADS, NR, 128), BF), V((HEADS, 3, WR, 128), BF), V((HEADS, 3, WR, 64), BF),
            V((HEADS, NR, WR), BF), V((4, NR, 192), BF), V((NR, 768), BF), V((NR, 768), BF), V((NR, 768), BF), V((NR, 768), BF),
            V((NE, 576), BF), dma((SEMS,)), dma((SEMS,)), dma((48,)),
        ],
        compiler_params=pltpu.CompilerParams(collective_id=0, has_side_effects=True, vmem_limit_bytes=67043328),
    )(xh, coth, ids, qkv_w, proj_w, fc1_w, fc2_w, vec, ktail, tab)


def plain_gather(xh, coth, shard):
    mine = lax.dynamic_index_in_dim(jnp.asarray(block_table()), lax.axis_index("tensor"), 0, keepdims=False)

    def spread(held, count):
        blocks = lax.all_gather(held.reshape(3, 3, 7, 8, 768), "tensor", axis=1).reshape(36, 7, 8, 768)
        got = jnp.take(blocks, mine[:count], axis=0).reshape(-1, 8, 768)
        return jnp.concatenate([got[:63], jnp.zeros((1, 8, 768), BF), got[63:]], axis=0)

    whole = lax.all_gather(lax.all_gather(shard, ("dp", "win"), axis=1, tiled=True), "tensor", axis=1)
    return spread(xh, 13), spread(coth, 9), whole


def plain_scatter(grads, x, mask, vec, gn, gh, vg, tg, out):
    shared = lax.psum_scatter(gn[NR:], "tensor", scatter_dimension=0, tiled=True)
    gn = mask * (gn[:NR] + jnp.pad(shared, ((2 * WR, QR - BP), (0, 0))))
    xf = x[: NR // 8].reshape(NR, 768).astype(F32)
    cen = xf - jnp.mean(xf, axis=-1, keepdims=True)
    rs = lax.rsqrt(jnp.mean(cen * cen, axis=-1, keepdims=True) + 1e-6)
    xh = cen * rs
    e1 = gn * vec[0]
    gx = gh + rs * (e1 - jnp.mean(e1, axis=-1, keepdims=True) - xh * jnp.mean(e1 * xh, axis=-1, keepdims=True))
    vg = vg.at[4].set(jnp.sum(gn * xh, axis=0)).at[5].set(jnp.sum(gn, axis=0))
    back_to = lax.dynamic_index_in_dim(jnp.asarray(home_table()), lax.axis_index("tensor"), 0, keepdims=False)

    def bring(rows):
        blocks = lax.all_gather(rows[:63].reshape(9, 7, 8, 768), "tensor", axis=0, tiled=True)
        return jnp.take(blocks, back_to, axis=0)

    own = lax.psum_scatter(grads.reshape(3, 4, 768, 768), "tensor", scatter_dimension=1, tiled=False)
    own = lax.psum_scatter(own, ("dp", "win"), scatter_dimension=1, tiled=True).astype(F32)
    vg, tg = lax.psum((vg, tg), ("dp", "win", "tensor"))
    return own, bring(out), bring(gx.astype(BF).reshape(NR // 8, 8, 768)), vg, tg


def per_device(
    links, tokens, window_ids, norm1_gain, norm1_bias, qkv_weight, qv_bias, rel_height, rel_width, proj_weight, proj_bias,
    norm2_gain, norm2_bias, fc1_weight, fc1_bias, fc2_weight, fc2_bias, out_grad,
):
    rank = lax.axis_index("tensor")

    def home_blocks(rows):
        return jnp.pad(rows.reshape(9, BT, 768), ((0, 0), (0, BP - BT), (0, 0))).reshape(9, 7, 8, 768)

    if links:
        vectors = (norm1_gain, norm1_bias, proj_bias, norm2_gain, norm2_bias, fc2_bias, fc1_bias)
        row = lax.broadcasted_iota(jnp.int32, (16, 768), 0)
        vec = jnp.pad(qv_bias.astype(F32), ((8, 6), (0, 576)))
        for n, v in enumerate(vectors):
            vec = jnp.where(row == n, v.astype(F32)[None, :], vec)
        tab = jnp.pad(rel_height, ((0, 101), (0, 0))) + jnp.pad(rel_width, ((32, 69), (0, 0)))

        def padded(rows):
            return jnp.pad(rows.reshape(9, BT, 768), ((0, 0), (0, BP - BT), (0, 0))).reshape(9, 7, 8, 768)

        def unpadded(blocks):
            return blocks.reshape(9, BP, 768)[:, :BT].reshape(tokens.shape)

        g_qkv, g_proj, g_fc1, g_fc2, out, dx, v0, v1, v2, v3, v4, v5, fc1b, qvb, relh, relw = whole_call(
            padded(tokens), padded(out_grad), jnp.transpose(window_ids, (1, 0, 2)), jnp.transpose(qkv_weight, (1, 0, 2)),
            proj_weight, fc1_weight, fc2_weight.T, vec, jnp.asarray(key_tail(), BF), tab,
        )
        v0, v1, v2, v3, v4, v5 = (v.reshape(768) for v in (v0, v1, v2, v3, v4, v5))
        return (
            unpadded(out), unpadded(dx).astype(F32), v4, v5, jnp.transpose(g_qkv, (1, 0, 2)), qvb, relh, relw, g_proj,
            v2, v0, v1, g_fc1, fc1b.reshape(-1), g_fc2.T, v3,
        )

    shard = jnp.stack(
        [
            jnp.concatenate([qkv_weight.reshape(-1, 576), proj_weight.T], axis=1),
            fc1_weight,
            fc2_weight.T,
        ]
    )
    xh, coth = home_blocks(tokens), home_blocks(out_grad)

    wi, wj, wv = token_positions()
    wi, wj, wv = jnp.asarray(wi, jnp.int32), jnp.asarray(wj, jnp.int32), jnp.asarray(wv)
    qi = jnp.pad(lax.dynamic_slice_in_dim(wi, rank * BP, BP), (0, QR - BP))
    qj = jnp.pad(lax.dynamic_slice_in_dim(wj, rank * BP, BP), (0, QR - BP))
    qv = jnp.pad(lax.dynamic_slice_in_dim(wv, rank * BP, BP), (0, QR - BP))
    ids = window_ids.reshape(9)
    slots = jnp.asarray([[m * 3 + s for m, s in WINDOWS_OF[dev]] + [4, 4] for dev in range(4)], jnp.int32)
    wid = jnp.take(ids, lax.dynamic_index_in_dim(slots, rank, 0, keepdims=False), axis=0)

    across = (GRID + WS - 1) // WS

    def valid(w, i, j, ok):
        return ok & (w < across * across) & ((w // across) * WS + i < GRID) & ((w % across) * WS + j < GRID)

    mask = jnp.concatenate(
        [valid(wid[0], wi, wj, wv), valid(wid[1], wi, wj, wv), valid(wid[2], qi, qj, qv), valid(wid[3], wi, wj, wv)]
    ).astype(F32)[:, None]
    ii = jnp.concatenate([wi, wi, qi])
    jj = jnp.concatenate([wj, wj, qj])
    fwd, back = pick_lanes(ii, jj)

    small = jnp.zeros((8, 768), F32).at[0].set(fc1_bias.astype(F32))
    small = small.at[1, :192].set(qv_bias[0].astype(F32)).at[1, 384:576].set(qv_bias[1].astype(F32))
    vec = jnp.stack(
        [norm1_gain, norm1_bias, proj_bias, norm2_gain, norm2_bias, fc2_bias, fc2_bias, fc2_bias]
    ).astype(F32)
    tab = jnp.zeros((128, 64), BF).at[0:27].set(rel_height).at[32:59].set(rel_width)
    tabt = (tab * BF(8)).T
    ktail = jnp.asarray(key_tail(), BF)

    x, cot, whole = plain_gather(xh, coth, shard)
    small = lax.all_gather(small, "tensor", axis=0)
    out, gn, gh, grads, vg, tg = compute(
        x, cot, mask, whole.reshape(3, 4, 768, 768), vec, small[:, 1:2, :576], small[:, 0:1], ktail, fwd, back, tab, tabt
    )
    own, out, dx, vg, tg = plain_scatter(grads, x, mask[:NR], vec, gn, gh, vg, tg, out)

    def tokens_of(blocks):
        return blocks.reshape(9, BP, 768)[:, :BT].reshape(tokens.shape)

    output = tokens_of(out)
    grad_tokens = tokens_of(dx).astype(F32)
    g_qkv = own[0, :, :576].reshape(qkv_weight.shape)
    g_proj = own[0, :, 576:].T
    g_fc1 = own[1]
    g_fc2 = own[2].T
    g_qv = jnp.stack([vg[12:16, :192].reshape(-1), vg[12:16, 384:576].reshape(-1)])
    return (
        output, grad_tokens, vg[4], vg[5], g_qkv, g_qv, tg[0:27, :64] * 8.0, tg[32:59, :64] * 8.0, g_proj,
        vg[2], vg[0], vg[1], g_fc1, vg[8:12].reshape(-1), g_fc2, vg[3],
    )


def solution(mesh):
    in_specs = (
        P("dp", "win", "tensor", None), P("dp", "win", None), P(), P(), P(("dp", "win"), None, "tensor"),
        P(None, "tensor"), P(), P(), P("tensor", ("dp", "win")), P(), P(), P(), P(("dp", "win"), "tensor"), P("tensor"),
        P("tensor", ("dp", "win")), P(), P("dp", "win", "tensor", None),
    )
    out_specs = (
        P("dp", "win", "tensor", None), P("dp", "win", "tensor", None), P(), P(), P(("dp", "win"), None, "tensor"), P(),
        P(), P(), P("tensor", ("dp", "win")), P(), P(), P(), P(("dp", "win"), "tensor"), P(),
        P("tensor", ("dp", "win")), P(),
    )
    links = dict(mesh.shape) == {"dp": 2, "win": 4, "tensor": 4}
    return jax.shard_map(partial(per_device, links), mesh=mesh, in_specs=in_specs, out_specs=out_specs, check_vma=False)
```

```python
import math
from functools import partial

import jax
import jax.numpy as jnp
import numpy as np
from jax import lax
from jax.experimental import pallas as pl
from jax.experimental.pallas import tpu as pltpu
from jax.sharding import PartitionSpec as P

HEADS = 12
HD = 64
WS = 14
GRID = 64
WT = 196
BT = 49
BP = 56
WR = 4 * BP
QR = 64
NR = 2 * WR + QR
NE = NR + WR
BF = jnp.bfloat16
F32 = jnp.float32

WINDOWS_OF = (((0, 0), (1, 0)), ((2, 0), (0, 1)), ((2, 2), (2, 1)), ((0, 2), (1, 2)))
SHARED = (1, 1)


def block_table():
    rows = []
    for dev in range(4):
        row = []
        for m, s in WINDOWS_OF[dev]:
            row += [m * 12 + 4 * s + j for j in range(4)]
        row.append(SHARED[0] * 12 + 4 * SHARED[1] + dev)
        row += [SHARED[0] * 12 + 4 * SHARED[1] + j for j in range(4)]
        rows.append(row)
    return np.array(rows, np.int32)


def home_table():
    table = block_table()
    place = {}
    for dev in range(4):
        for slot in range(9):
            place[int(table[dev, slot])] = dev * 9 + slot
    return np.array([[place[m * 12 + 3 * dev + b] for m in range(3) for b in range(3)] for dev in range(4)], np.int32)


def token_positions():
    row = np.arange(WR)
    off = row % BP
    token = (row // BP) * BT + np.minimum(off, BT - 1)
    return token // WS, token % WS, off < BT


def key_tail():
    i, j, valid = token_positions()
    tail = np.zeros((WR, 128), np.float32)
    for m in range(WS):
        tail[:, 64 + m] = i == m
        tail[:, 78 + m] = j == m
    tail[:, 92:120] = tail[:, 64:92]
    tail[:, :120] *= valid[:, None]
    tail[:, 120] = np.where(valid, 0.0, -1e30)
    return tail


def pick_lanes(i, j):
    lane = np.arange(128)[None, :]
    m = np.clip((lane - 64) % 28, 0, 27)
    is_w = m >= 14
    fwd = jnp.where(is_w, 32 + j[:, None] - (m - 14) + 13, i[:, None] - m + 13)
    fwd = jnp.where((lane >= 64) & (lane < 120), fwd, 0)
    d = lane % 32
    pos = jnp.where(lane >= 32, j[:, None], i[:, None]) + 13 - d
    ok = (pos >= 0) & (pos < WS) & (lane < 64) & (d < 27)
    back = jnp.where(ok, pos + jnp.where(lane >= 32, 78, 64), 127)
    return fwd.astype(jnp.int32), back.astype(jnp.int32)


def dotf(a, b, dims):
    return lax.dot_general(a, b, (dims, ((), ())), preferred_element_type=F32)


NN = ((1,), (0,))
NT = ((1,), (1,))
TN = ((0,), (0,))


def compute_kernel(
    x_ref, cot_ref, mask_ref, w_ref, vec_ref, qkvb_ref, fc1b_ref, ktail_ref, fwd_ref, back_ref, tab_ref, tabt_ref,
    out_ref, gn_ref, gh_ref, g_ref, vg_ref, tg_ref,
    nrm, proj, qaug, kaug, vals, probs, att, hid, nr2, mix, gn2, act, gup, gml, gbl, dqkv,
):
    g1, b1, pb, g2, b2, fb = (vec_ref[i : i + 1, :] for i in range(6))

    def stats(v):
        mu = jnp.mean(v, axis=-1, keepdims=True)
        c = v - mu
        var = jnp.mean(c * c, axis=-1, keepdims=True)
        return c, lax.rsqrt(var + 1e-6)

    vg_ref[...] = jnp.zeros_like(vg_ref)

    for r0 in range(0, NE, 32):
        rows = slice(r0, r0 + 32)
        c, rs = stats(x_ref[r0 // 8 : r0 // 8 + 4].astype(F32).reshape(32, 768))
        nrm[rows, :] = (mask_ref[rows, :] * (c * rs * g1 + b1)).astype(BF)

    def fwd_t(t, _):
        proj[...] = dotf(nrm[...], w_ref[0, t][:, :576], NN) + qkvb_ref[t]
        for h in range(3):
            hh = 3 * t + h
            qs = (proj[:NR, 64 * h : 64 * h + 64].astype(BF) * BF(0.125)).astype(BF)
            rel = dotf(qs, tabt_ref[...], NN)
            lane = lax.broadcasted_iota(jnp.int32, (NR, 128), 1)
            got = jnp.take_along_axis(rel, fwd_ref[...], axis=1, mode="promise_in_bounds")
            hi = got.astype(BF).astype(F32)
            tail = jnp.where(lane < 92, hi, got - hi)
            tail = jnp.where(lane == 120, 1.0, jnp.where(lane < 120, tail, 0.0)).astype(BF)
            qa = jnp.concatenate([qs, tail[:, 64:]], axis=1)
            qaug[hh] = qa
            for w in range(3):
                src = slice(w * WR, w * WR + WR) if w < 2 else slice(NR, NE)
                k = proj[src, 192 + 64 * h : 256 + 64 * h].astype(BF)
                kaug[hh, w] = jnp.concatenate([k, ktail_ref[:, 64:]], axis=1)
                vals[hh, w] = proj[src, 384 + 64 * h : 448 + 64 * h].astype(BF)
        return 0

    lax.fori_loop(0, 4, fwd_t, 0)
    mix[...] = jnp.zeros_like(mix)

    def att_t(t, _):
        for h in range(3):
            hh = 3 * t + h
            for w in range(3):
                rows = slice(w * WR, w * WR + WR) if w < 2 else slice(2 * WR, NR)
                s = dotf(qaug[hh, rows, :], kaug[hh, w], NT)
                e = jnp.exp(s - jnp.max(s, axis=-1, keepdims=True))
                p = (e * (1.0 / jnp.sum(e, axis=-1, keepdims=True))).astype(BF)
                probs[hh, rows, :] = p
                att[t, rows, 64 * h : 64 * h + 64] = dotf(p, vals[hh, w], NN).astype(BF)
        mix[...] += dotf(att[t], w_ref[0, t][:, 576:], NT)
        return 0

    lax.fori_loop(0, 4, att_t, 0)

    for r0 in range(0, NR, 32):
        rows = slice(r0, r0 + 32)
        x = x_ref[r0 // 8 : r0 // 8 + 4].astype(F32).reshape(32, 768)
        hv = x + mask_ref[rows, :] * (mix[rows, :] + pb)
        hid[rows, :] = hv
        c, rs = stats(hv)
        nr2[rows, :] = (c * rs * g2 + b2).astype(BF)
        gm = mask_ref[rows, :] * cot_ref[r0 // 8 : r0 // 8 + 4].astype(F32).reshape(32, 768)
        gml[rows, :] = gm.astype(BF)
    mix[...] = jnp.zeros_like(mix)
    gn2[...] = jnp.zeros_like(gn2)

    def mlp_t(t, _):
        for f in range(3):
            cols = slice(256 * f, 256 * f + 256)
            for r0 in range(0, NR, 128):
                rows = slice(r0, r0 + 128)
                up = dotf(nr2[rows, :], w_ref[1, t][:, cols], NN) + fc1b_ref[t][:, cols]
                ga = dotf(gml[rows, :], w_ref[2, t][:, cols], NN)
                cdf = 0.5 * (1.0 + lax.erf(up * (1.0 / math.sqrt(2.0))))
                pdf = jnp.exp(-0.5 * up * up) * (1.0 / math.sqrt(2.0 * math.pi))
                act[rows, cols] = (up * cdf).astype(BF)
                gup[rows, cols] = (ga * (cdf + up * pdf)).astype(BF)
        vg_ref[pl.ds(8 + t, 1), :] = jnp.sum(gup[...].astype(F32), axis=0, keepdims=True)
        mix[...] += dotf(act[...], w_ref[2, t], NT)
        gn2[...] += dotf(gup[...], w_ref[1, t], NT)
        g_ref[2, t] = dotf(gml[...], act[...], TN).astype(BF)
        g_ref[1, t] = dotf(nr2[...], gup[...], TN).astype(BF)
        return 0

    lax.fori_loop(0, 4, mlp_t, 0)

    sums = [jnp.zeros((8, 768), F32) for _ in range(4)]

    def fold(v):
        return jnp.sum(v.reshape(4, 8, 768), axis=0)

    for r0 in range(0, NR, 32):
        rows = slice(r0, r0 + 32)
        mk = mask_ref[rows, :]
        gm = mk * cot_ref[r0 // 8 : r0 // 8 + 4].astype(F32).reshape(32, 768)
        hv = hid[rows, :]
        out_ref[r0 // 8 : r0 // 8 + 4] = (mk * (hv + mix[rows, :] + fb)).reshape(4, 8, 768).astype(BF)
        c, rs = stats(hv)
        xh = c * rs
        gn = gn2[rows, :]
        e2 = gn * g2
        gh = gm + rs * (e2 - jnp.mean(e2, axis=-1, keepdims=True) - xh * jnp.mean(e2 * xh, axis=-1, keepdims=True))
        gb = mk * gh
        gh_ref[rows, :] = gh
        gbl[rows, :] = gb.astype(BF)
        for n, v in enumerate((gn * xh, gn, gb, gm)):
            sums[n] = sums[n] + fold(v)
    for n in range(4):
        vg_ref[n : n + 1, :] = jnp.sum(sums[n], axis=0, keepdims=True)
    tg_ref[...] = jnp.zeros_like(tg_ref)
    gn_ref[...] = jnp.zeros_like(gn_ref)

    def bwd_t(t, _):
        att_w = att[t]
        g_ref[0, t, :, 576:] = dotf(gbl[...], att_w, TN).astype(BF)
        proj[:NR, :192] = dotf(gbl[...], w_ref[0, t][:, 576:], NN)
        dqkv[...] = jnp.zeros_like(dqkv)
        for h in range(3):
            hh = 3 * t + h
            lo = 64 * h
            for w in range(3):
                rows = slice(w * WR, w * WR + WR) if w < 2 else slice(2 * WR, NR)
                dst = rows if w < 2 else slice(NR, NE)
                do = proj[rows, lo : lo + 64].astype(BF)
                p = probs[hh, rows, :]
                pf = p.astype(F32)
                dp = dotf(do, vals[hh, w], NT)
                delta = jnp.sum(pf * dp, axis=-1, keepdims=True)
                ds = (pf * (dp - delta)).astype(BF)
                dq = dotf(ds, kaug[hh, w], NN)
                qa = qaug[hh, rows, :]
                dqkv[dst, 192 + lo : 256 + lo] = dotf(ds, qa, TN)[:, :64].astype(BF)
                dqkv[dst, 384 + lo : 448 + lo] = dotf(p, do, TN).astype(BF)
                rel = jnp.take_along_axis(dq, back_ref[rows, :], axis=1, mode="promise_in_bounds").astype(BF)
                gq = dq[:, :64] * 0.125 + dotf(rel, tab_ref[...], NN)
                dqkv[rows, lo : lo + 64] = gq.astype(BF)
                tg_ref[...] += dotf(rel, qa, TN)[:64]
        vg_ref[pl.ds(12 + t, 1), 0:576] = jnp.sum(dqkv[...].astype(F32), axis=0, keepdims=True)
        g_ref[0, t, :, :576] = dotf(nrm[...], dqkv[...], TN).astype(BF)
        gn_ref[...] += dotf(dqkv[...], w_ref[0, t][:, :576], NT)
        return 0

    lax.fori_loop(0, 4, bwd_t, 0)


def compute(x, cot, mask, w, vec, qkvb, fc1b, ktail, fwd, back, tab, tabt):
    shp = jax.ShapeDtypeStruct
    vm = pl.BlockSpec(memory_space=pltpu.VMEM)
    return pl.pallas_call(
        compute_kernel,
        out_shape=(
            shp((NR // 8, 8, 768), BF), shp((NE, 768), F32), shp((NR, 768), F32), shp((3, 4, 768, 768), BF),
            shp((16, 768), F32), shp((64, 128), F32),
        ),
        in_specs=[vm] * 12,
        out_specs=(vm,) * 6,
        scratch_shapes=[
            pltpu.VMEM((NE, 768), BF), pltpu.VMEM((NE, 576), F32), pltpu.VMEM((HEADS, NR, 128), BF),
            pltpu.VMEM((HEADS, 3, WR, 128), BF), pltpu.VMEM((HEADS, 3, WR, 64), BF), pltpu.VMEM((HEADS, NR, WR), BF),
            pltpu.VMEM((4, NR, 192), BF), pltpu.VMEM((NR, 768), F32), pltpu.VMEM((NR, 768), BF),
            pltpu.VMEM((NR, 768), F32), pltpu.VMEM((NR, 768), F32), pltpu.VMEM((NR, 768), BF), pltpu.VMEM((NR, 768), BF),
            pltpu.VMEM((NR, 768), BF), pltpu.VMEM((NR, 768), BF), pltpu.VMEM((NE, 576), BF),
        ],
        compiler_params=pltpu.CompilerParams(vmem_limit_bytes=67043328),
    )(x, cot, mask, w, vec, qkvb, fc1b, ktail, fwd, back, tab, tabt)


MESH = pl.DeviceIdType.MESH


class Links:
    def __init__(self, send, recv):
        self.send, self.recv = send, recv
        self.x = lax.axis_index("dp")
        win = lax.axis_index("win")
        self.y, self.c = win // 2, win % 2
        self.z = lax.axis_index("tensor")
        self.xn = (1 - self.x, win, self.z)
        self.yn = (self.x, (1 - self.y) * 2 + self.c, self.z)
        self.sib = (self.x, self.y * 2 + 1 - self.c, self.z)
        self.win = win

    def zdev(self, z):
        return (self.x, self.win, z)

    def barrier(self):
        sem = pltpu.get_barrier_semaphore()
        others = [self.xn, self.yn, self.sib] + [self.zdev((self.z + d) % 4) for d in (1, 2, 3)]
        for dev in others:
            pl.semaphore_signal(sem, inc=1, device_id=dev, device_id_type=MESH)
        pl.semaphore_wait(sem, len(others))

    def copy(self, src, dst, n, dev):
        return pltpu.make_async_remote_copy(
            src_ref=src, dst_ref=dst, send_sem=self.send.at[n], recv_sem=self.recv.at[n], device_id=dev,
            device_id_type=MESH,
        )


AG_SEMS = 3 * 39


class Gather:
    def __init__(self, links, shards, w, local, base):
        self.l, self.shards, self.w, self.local, self.base = links, shards, w, local, base

    def sem(self, k, kind, i):
        start = {"z": 0, "x": 3, "y": 7, "hx": 11, "hy": 15, "so": 19, "sx": 23, "sy": 27, "sa": 31, "sb": 35}[kind]
        return self.base + k * 39 + start + i

    def rank(self, i):
        return (self.l.z + 4 - i) % 4

    def piece(self, k, i, px, py, c, half=None):
        ref = self.w.at[k, self.rank(i), px, py, c]
        return ref if half is None else ref.at[pl.ds(48 * half, 48)]

    def move(self, k, kind, i):
        l = self.l
        if kind == "z":
            src = self.shards[k]
            return l.copy(src, self.piece(k, 0, l.x, l.y, l.c), self.sem(k, kind, i - 1), l.zdev((l.z + i) % 4))
        px, py, half, dev = {
            "x": (l.x, l.y, None, l.xn), "y": (l.x, l.y, None, l.yn),
            "hx": (l.x, 1 - l.y, 1, l.xn), "hy": (1 - l.x, l.y, 0, l.yn),
            "so": (l.x, l.y, None, l.sib), "sx": (1 - l.x, l.y, None, l.sib), "sy": (l.x, 1 - l.y, None, l.sib),
            "sa": (1 - l.x, 1 - l.y, 0, l.sib), "sb": (1 - l.x, 1 - l.y, 1, l.sib),
        }[kind]
        dst = self.piece(k, i, px, py, l.c, half)
        own = kind in ("x", "y", "so") and i == 0
        return l.copy(self.shards[k] if own else dst, dst, self.sem(k, kind, i), dev)

    def start(self, k, kind, i):
        self.move(k, kind, i).start()

    def arrived(self, k, kind, i):
        self.move(k, kind, i).wait_recv()

    def keep(self, k):
        l = self.l
        return pltpu.make_async_copy(self.shards[k], self.piece(k, 0, l.x, l.y, l.c), self.local.at[k])

    def own_z(self, k):
        for i in (1, 3, 2):
            self.start(k, "z", i)

    def along(self, k, i):
        if i:
            self.arrived(k, "z", i)
        else:
            self.keep(k).start()
        for kind in ("x", "y", "so"):
            self.start(k, kind, i)

    def across(self, k, i):
        self.arrived(k, "x", i)
        self.start(k, "hy", i)
        self.start(k, "sx", i)
        self.arrived(k, "y", i)
        self.start(k, "hx", i)
        self.start(k, "sy", i)

    def corner(self, k, i):
        self.arrived(k, "hy", i)
        self.start(k, "sa", i)
        self.arrived(k, "hx", i)
        self.start(k, "sb", i)

    def partner(self, k, i):
        for kind in ("so", "sx", "sy", "sa", "sb"):
            self.arrived(k, kind, i)
        if not i:
            self.keep(k).wait()

    def drain(self, k, i):
        for kind in ("x", "y", "hx", "hy", "so", "sx", "sy", "sa", "sb"):
            self.move(k, kind, i).wait_send()


RS_SEMS = 12 * 6


class Scatter:
    def __init__(self, links, w, r1, r2, r3, r4, base):
        self.l, self.w, self.r1, self.r2, self.r3, self.r4, self.base = links, w, r1, r2, r3, r4, base

    def g(self, k, i):
        return self.w.at[k, (self.l.z + 4 - i) % 4]

    def moves(self, k, i, stage):
        l, n = self.l, 4 * k + i
        s = self.base + 6 * n
        g = self.g(k, i)
        if stage == 1:
            return [l.copy(g.at[:, :, 1 - l.c], self.r1.at[n], s, l.sib)]
        if stage == 2:
            return [
                l.copy(g.at[:, 1 - l.y, l.c, 0:48], self.r2.at[n, 0], s + 1, l.yn),
                l.copy(g.at[1 - l.x, :, l.c, 48:96], self.r2.at[n, 1], s + 2, l.xn),
            ]
        if stage == 3:
            return [
                l.copy(g.at[1 - l.x, l.y, l.c, 0:48], self.r3.at[n, 0], s + 3, l.xn),
                l.copy(g.at[l.x, 1 - l.y, l.c, 48:96], self.r3.at[n, 1], s + 4, l.yn),
            ]
        return [l.copy(g.at[l.x, l.y, l.c], self.r4.at[k, i - 1], s + 5, l.zdev((l.z + 4 - i) % 4))] if i else []

    def start(self, k, i, stage):
        for m in self.moves(k, i, stage):
            m.start()

    def wait(self, k, i, stage):
        for m in self.moves(k, i, stage):
            m.wait_recv()

    def step(self, k, i, stage):
        l, g, n = self.l, self.g(k, i), 4 * k + i
        self.wait(k, i, stage - 1)
        if stage == 2:
            for a in range(2):
                for b in range(2):
                    ref = g.at[a, b, l.c]
                    ref[...] = ref[...] + self.r1[n, a, b]
        elif stage == 3:
            for a in range(2):
                ref = g.at[a, l.y, l.c, 0:48]
                ref[...] = ref[...] + self.r2[n, 0, a]
                ref = g.at[l.x, a, l.c, 48:96]
                ref[...] = ref[...] + self.r2[n, 1, a]
        else:
            for h in range(2):
                ref = g.at[l.x, l.y, l.c, pl.ds(48 * h, 48)]
                ref[...] = ref[...] + self.r3[n, h]
        self.start(k, i, stage)

    def total(self, k):
        l = self.l
        fin = self.g(k, 0)[l.x, l.y, l.c].astype(F32)
        for i in (1, 2, 3):
            self.wait(k, i, 4)
            fin = fin + self.r4[k, i - 1].astype(F32)
        return fin

    def drain(self):
        for k in range(3):
            for i in range(4):
                for stage in (1, 2, 3, 4):
                    for m in self.moves(k, i, stage):
                        m.wait_send()


class Rows:
    TABLE = block_table()

    def __init__(self, links, local):
        self.l, self.local = links, local

    @staticmethod
    def home(block):
        m, b = divmod(int(block), 12)
        return b // 3, m * 3 + b % 3

    @staticmethod
    def unit(slot):
        return 7 * slot if slot < 9 else NR // 8 + 7 * (slot - 9)

    def inward(self, held, rows, slots, base, do):
        l = self.l
        for me in range(4):

            @pl.when(l.z == me)
            def _():
                sent = 0
                for slot in slots:
                    for step in range(4):
                        dev = (me + step) % 4
                        owner, idx = self.home(self.TABLE[dev, slot])
                        if owner != me:
                            continue
                        dst = rows.at[pl.ds(self.unit(slot), 7)]
                        if dev == me:
                            if do != "drain":
                                c = pltpu.make_async_copy(held.at[idx], dst, self.local.at[base + slot])
                                c.start() if do == "start" else c.wait()
                            continue
                        sent += 1
                        if do == "wait":
                            continue
                        c = pltpu.make_async_remote_copy(
                            src_ref=held.at[idx], dst_ref=dst, send_sem=l.send.at[base + sent - 1],
                            recv_sem=l.recv.at[base + slot], device_id=l.zdev(dev), device_id_type=MESH,
                        )
                        c.start() if do == "start" else c.wait_send()
                    owner, idx = self.home(self.TABLE[me, slot])
                    if do == "wait" and owner != me:
                        pltpu.make_async_remote_copy(
                            src_ref=held.at[0], dst_ref=rows.at[pl.ds(self.unit(slot), 7)], send_sem=l.send.at[base],
                            recv_sem=l.recv.at[base + slot], device_id=l.zdev(owner), device_id_type=MESH,
                        ).wait_recv()

    def outward(self, rows, held, base, mine, do):
        l = self.l
        for me in range(4):

            @pl.when(l.z == me)
            def _():
                for slot in range(9):
                    owner, idx = self.home(self.TABLE[me, slot])
                    src = rows.at[pl.ds(7 * slot, 7)]
                    if owner == me:
                        if do != "drain":
                            c = pltpu.make_async_copy(src, held.at[idx], self.local.at[mine + slot])
                            c.start() if do == "start" else c.wait()
                    elif do != "wait":
                        c = pltpu.make_async_remote_copy(
                            src_ref=src, dst_ref=held.at[idx], send_sem=l.send.at[base + slot],
                            recv_sem=l.recv.at[base + idx], device_id=l.zdev(owner), device_id_type=MESH,
                        )
                        c.start() if do == "start" else c.wait_send()
                for dev in range(4):
                    for slot in range(9):
                        owner, idx = self.home(self.TABLE[dev, slot])
                        if do == "wait" and owner == me and dev != me:
                            pltpu.make_async_remote_copy(
                                src_ref=rows.at[pl.ds(0, 7)], dst_ref=held.at[idx], send_sem=l.send.at[base],
                                recv_sem=l.recv.at[base + idx], device_id=l.zdev(dev), device_id_type=MESH,
                            ).wait_recv()


XS, CS, BS = 0, 13, 22
AG0 = BS + 3
RET0 = AG0 + AG_SEMS
DX0 = RET0 + 9
SH0 = DX0 + 9
VS0 = SH0 + 3
RS0 = VS0 + 10
SEMS = RS0 + RS_SEMS
X_SLOTS = (0, 1, 2, 3, 4, 5, 6, 7, 9, 10, 11, 12)

ORD = (0, 1, 3, 2)
BACK = (2, 1, 3, 0)
BLOCKS = ((0, 0), (1, 0), (0, 1), (0, 3), (0, 2), (2, 0), (1, 1), (2, 1), (1, 3), (2, 3), (1, 2), (2, 2))


PLACES = (
    [("M", n, j) for n in range(4) for j in range(5)] + ["N"] + [("B", n, j) for n in range(4) for j in range(3)]
    + ["T0", "T1", "T2", "S0", "S1", "S2", "S3", "S4", "T3"]
)
TICKS = {1: ("F", 0, 0), 2: ("F", 0, 2), 3: ("F", 1, 1), 4: ("F", 2, 1), 5: ("F", 3, 1), 6: "L", 7: ("M", 0, 0), 8: ("M", 0, 4),
         9: ("M", 1, 1), 10: ("M", 1, 4), 11: ("M", 2, 1)}
MLP_LAGS = ((0, 6, 11), (1, 8, 12))
BWD_LAGS = (0, 3, 5)


def timetable():
    plan = {}

    def put(place, *event):
        plan.setdefault(place, []).append(event)

    for s, place in TICKS.items():
        put(place, "tick", s)
    for n in range(4):
        for k, lags in zip((2, 1), MLP_LAGS):
            made = PLACES.index(("M", n, 4)) + 1
            for stage, lag in zip((2, 3, 4), lags):
                put(PLACES[made + lag], "step", k, ORD[n], stage)
        made = PLACES.index(("B", n, 2)) + 1
        for stage, lag in zip((2, 3, 4), BWD_LAGS):
            put(PLACES[made + lag], "step", 0, BACK[n], stage)
    return plan


def places(rows, first):
    r = lax.broadcasted_iota(jnp.int32, (rows, 128), 0)
    blk = sum((r >= BP * n).astype(jnp.int32) for n in range(1, 4)) if rows == WR else jnp.zeros_like(r)
    off = r - BP * blk
    token = (blk + first) * BT + jnp.minimum(off, BT - 1)
    i = (token * 4682) >> 16
    return i, token - WS * i, off < BT


def lanes_of(i, j):
    lane = lax.broadcasted_iota(jnp.int32, i.shape, 1)
    m = lane - 64
    m = m - 28 * ((m >= 28).astype(jnp.int32) + (m >= 56).astype(jnp.int32))
    fwd = jnp.where(m >= 14, 32 + j - (m - 14) + 13, i - m + 13)
    fwd = jnp.where((lane >= 64) & (lane < 120), fwd, 0)
    d = lane & 31
    pos = jnp.where(lane >= 32, j, i) + 13 - d
    ok = (pos >= 0) & (pos < WS) & (lane < 64) & (d < 27)
    return fwd, jnp.where(ok, pos + jnp.where(lane >= 32, 78, 64), 127)


def fill_tables(z, ids, mask_ref, fwd_ref, back_ref):
    across = (GRID + WS - 1) // WS

    def valid(w, i, j, ok):
        a = lax.div(w, jnp.int32(across))
        hi = jnp.where(w < across * across, GRID - a * WS, 0)
        wi = GRID - (w - across * a) * WS
        return jnp.where(ok & (i < hi) & (j < wi), 1.0, 0.0)[:, :1]

    def window(n):
        m, s = (jnp.int32(v) for v in WINDOWS_OF[3][n])
        for dev in range(3):
            m = jnp.where(z == dev, WINDOWS_OF[dev][n][0], m)
            s = jnp.where(z == dev, WINDOWS_OF[dev][n][1], s)
        return ids[m, 0, s]

    i, j, ok = places(WR, 0)
    fwd, back = lanes_of(i, j)
    shared = ids[SHARED[0], 0, SHARED[1]]
    for n in range(2):
        rows = slice(n * WR, n * WR + WR)
        fwd_ref[rows, :] = fwd
        back_ref[rows, :] = back
        mask_ref[rows, :] = valid(window(n), i, j, ok)
    mask_ref[NR:NE, :] = valid(shared, i, j, ok)
    i, j, ok = places(QR, z)
    fwd, back = lanes_of(i, j)
    fwd_ref[2 * WR : NR, :] = fwd
    back_ref[2 * WR : NR, :] = back
    mask_ref[2 * WR : NR, :] = valid(shared, i, j, ok)


def whole_kernel(
    x_raw, cot_raw, ids, qkv_w, proj_w, fc1_w, fc2_w, u0, u1, u2, u3, u4, u5, u6, qvb_in, relh_in, relw_in, ktail_ref,
    own, out_h, dx_h, vg_out, tg_out,
    shard0, small, mask_ref, fwd_ref, back_ref, vec_ref, tab_ref, tabf,
    w, r1, r2, r3, r4, x, cot, sm, raw, dx, gn, hid, gn2, gs, gsr, vg, tg, vr, tr,
    nrm, proj, qaug, kaug, vals, probs, att, nr2, act, gup, gml, dqkv, send, recv, local,
):
    links = Links(send, recv)
    z = links.z
    rows_of = Rows(links, local)
    ag = Gather(links, (shard0, fc1_w, fc2_w), w, local.at[pl.ds(40, 3)], AG0)
    rs = Scatter(links, w, r1, r2, r3, r4, RS0)

    def rank(order, m):
        i = jnp.int32(order[3])
        for n in range(3):
            i = jnp.where(m == n, order[n], i)
        return (z + 4 - i) % 4

    def weight(k, t):
        return w[k, t].reshape(768, 768)

    def tick(s):
        if s + 2 < 12:
            ag.along(*BLOCKS[s + 2])
        if s + 1 < 12:
            ag.across(*BLOCKS[s + 1])
        ag.corner(*BLOCKS[s])

    def at(m, plan):
        for n, todo in plan.items():

            @pl.when(m == n)
            def _():
                for f in todo:
                    f()

    plan = timetable()

    def run(events):
        for what, *which in events:
            if what == "tick":
                tick(*which)
            else:
                rs.step(*which)

    def now(place):
        run(plan.get(place, ()))

    def hook(m, loop, j):
        for n in range(4):
            todo = plan.get((loop, n, j))
            if todo:

                @pl.when(m == n)
                def _():
                    run(todo)

    def stats(v):
        mu = jnp.mean(v, axis=-1, keepdims=True)
        c = v - mu
        var = jnp.mean(c * c, axis=-1, keepdims=True)
        return c, lax.rsqrt(var + 1e-6)

    read_x = pltpu.make_async_copy(x_raw, raw, local.at[44])
    read_x.start()
    for t in range(3):
        shard0[:, 192 * t : 192 * t + 192] = qkv_w[t]
    shard0[:, 576:] = proj_w[...].astype(F32).T.astype(BF)
    x[63] = jnp.zeros((8, 768), BF)
    cot[63] = jnp.zeros((8, 768), BF)
    links.barrier()
    for b in (0, 1):
        ag.along(*BLOCKS[b])
    small[...] = jnp.zeros_like(small)
    for n, u in enumerate((u0, u1, u2, u3, u4, u5, u6)):
        ref, row = (vec_ref, n) if n < 6 else (small, 0)
        uf = u[...].astype(F32)
        for c in range(6):
            ref[row : row + 1, 128 * c : 128 * c + 128] = uf[c : c + 1, :]
    qvb = qvb_in[...].astype(F32)
    small[1:2, 0:192] = qvb[0:1]
    small[1:2, 384:576] = qvb[1:2]
    bias = [links.copy(small, sm.at[z], BS + d - 1, links.zdev((z + d) % 4)) for d in (1, 2, 3)]
    keep_bias = pltpu.make_async_copy(small, sm.at[z], local.at[43])
    keep_bias.start()
    for c in bias:
        c.start()
    ag.own_z(0)

    def pad_blocks(held):
        for m in range(3):
            gn2[0:147, :] = raw[m].astype(F32)
            for b in range(3):
                v = gn2[BT * b : BT * b + BP, :]
                v = jnp.where(lax.broadcasted_iota(jnp.int32, v.shape, 0) < BT, v, 0.0)
                held[3 * m + b] = v.astype(BF).reshape(7, 8, 768)

    held = dx.at[pl.ds(0, 63)].reshape(9, 7, 8, 768)
    read_x.wait()
    pad_blocks(held)
    rows_of.inward(held, x, X_SLOTS, XS, "start")
    read_cot = pltpu.make_async_copy(cot_raw, raw, local.at[44])
    read_cot.start()
    ag.own_z(1)
    tabf[...] = jnp.zeros_like(tabf)
    tabf[0:27, :] = relh_in[...].astype(F32)
    tabf[32:59, :] = relw_in[...].astype(F32)
    tab_ref[...] = tabf[...].astype(BF)

    vg[...] = jnp.zeros_like(vg)
    tg[...] = jnp.zeros_like(tg)
    fill_tables(z, ids, mask_ref, fwd_ref, back_ref)
    rows_of.inward(held, x, X_SLOTS, XS, "wait")
    x[56:63] = x[pl.ds(NR // 8 + 7 * z, 7)]
    for c in bias:
        c.wait_recv()
    keep_bias.wait()

    g1, b1, pb, g2, b2, fb = (vec_ref[i : i + 1, :] for i in range(6))

    for r0 in range(0, NE, 32):
        rows = slice(r0, r0 + 32)
        c, rstd = stats(x[r0 // 8 : r0 // 8 + 4].astype(F32).reshape(32, 768))
        nrm[rows, :] = (mask_ref[rows, :] * (c * rstd * g1 + b1)).astype(BF)

    ag.across(*BLOCKS[0])
    tick(0)
    ag.own_z(2)
    rows_of.inward(held, x, X_SLOTS, XS, "drain")
    read_cot.wait()
    pad_blocks(held)
    rows_of.inward(held, cot, range(9), CS, "start")
    mix = gn.at[pl.ds(0, NR)]
    mix[...] = jnp.zeros_like(mix)

    def fwd_t(m, _):
        at(m, {n: [partial(ag.partner, 0, ORD[n])] for n in range(4)})
        t = rank(ORD, m)
        proj[...] = dotf(nrm[...], weight(0, t)[:, :576], NN) + sm[t][1:2, :576]
        for h in range(3):
            hh = 3 * t + h
            qs = (proj[:NR, 64 * h : 64 * h + 64].astype(BF) * BF(0.125)).astype(BF)
            rel = dotf(qs, tab_ref[...], NT) * 8.0
            lane = lax.broadcasted_iota(jnp.int32, (NR, 128), 1)
            got = jnp.take_along_axis(rel, fwd_ref[...], axis=1, mode="promise_in_bounds")
            hi = got.astype(BF).astype(F32)
            tail = jnp.where(lane < 92, hi, got - hi)
            tail = jnp.where(lane == 120, 1.0, jnp.where(lane < 120, tail, 0.0)).astype(BF)
            qa = jnp.concatenate([qs, tail[:, 64:]], axis=1)
            qaug[hh] = qa
            for wn in range(3):
                src = slice(wn * WR, wn * WR + WR) if wn < 2 else slice(NR, NE)
                k = proj[src, 192 + 64 * h : 256 + 64 * h].astype(BF)
                kaug[hh, wn] = jnp.concatenate([k, ktail_ref[:, 64:]], axis=1)
                vals[hh, wn] = proj[src, 384 + 64 * h : 448 + 64 * h].astype(BF)
        hook(m, "F", 0)
        for h in range(3):
            hh = 3 * t + h
            for wn in range(3):
                rows = slice(wn * WR, wn * WR + WR) if wn < 2 else slice(2 * WR, NR)
                s = dotf(qaug[hh, rows, :], kaug[hh, wn], NT)
                e = jnp.exp(s - jnp.max(s, axis=-1, keepdims=True))
                p = (e * (1.0 / jnp.sum(e, axis=-1, keepdims=True))).astype(BF)
                probs[hh, rows, :] = p
                att[t, rows, 64 * h : 64 * h + 64] = dotf(p, vals[hh, wn], NN).astype(BF)
            if h == 1:
                hook(m, "F", 1)
        mix[...] += dotf(att[t], weight(0, t)[:, 576:], NT)
        hook(m, "F", 2)
        return 0

    lax.fori_loop(0, 4, fwd_t, 0)
    rows_of.inward(held, cot, range(9), CS, "wait")
    now("L")

    for r0 in range(0, NR, 32):
        rows = slice(r0, r0 + 32)
        xv = x[r0 // 8 : r0 // 8 + 4].astype(F32).reshape(32, 768)
        hv = xv + mask_ref[rows, :] * (mix[rows, :] + pb)
        hid[rows, :] = hv
        c, rstd = stats(hv)
        nr2[rows, :] = (c * rstd * g2 + b2).astype(BF)
        gm = mask_ref[rows, :] * cot[r0 // 8 : r0 // 8 + 4].astype(F32).reshape(32, 768)
        gml[rows, :] = gm.astype(BF)
    mix[...] = jnp.zeros_like(mix)
    gn2[...] = jnp.zeros_like(gn2)

    def mlp_t(m, _):
        at(m, {n: [partial(ag.partner, 1, ORD[n]), partial(ag.partner, 2, ORD[n])] for n in range(4)})
        t = rank(ORD, m)
        for f in range(3):
            cols = slice(256 * f, 256 * f + 256)
            for r0 in range(0, NR, 128):
                rows = slice(r0, r0 + 128)
                up = dotf(nr2[rows, :], weight(1, t)[:, cols], NN) + sm[t][0:1, cols]
                ga = dotf(gml[rows, :], weight(2, t)[:, cols], NN)
                cdf = 0.5 * (1.0 + lax.erf(up * (1.0 / math.sqrt(2.0))))
                pdf = jnp.exp(-0.5 * up * up) * (1.0 / math.sqrt(2.0 * math.pi))
                act[rows, cols] = (up * cdf).astype(BF)
                gup[rows, cols] = (ga * (cdf + up * pdf)).astype(BF)
            hook(m, "M", f)
        vg[0, pl.ds(8 + t, 1), :] = jnp.sum(gup[...].astype(F32), axis=0, keepdims=True)
        mix[...] += dotf(act[...], weight(2, t), NT)
        hook(m, "M", 3)
        gn2[...] += dotf(gup[...], weight(1, t), NT)
        hook(m, "M", 4)
        at(m, {n: [partial(ag.drain, 2, ORD[n])] for n in range(4)})
        w[2, t] = dotf(gml[...], act[...], TN).astype(BF).reshape(2, 2, 2, 96, 768)
        at(m, {n: [partial(rs.start, 2, ORD[n], 1), partial(ag.drain, 1, ORD[n])] for n in range(4)})
        w[1, t] = dotf(nr2[...], gup[...], TN).astype(BF).reshape(2, 2, 2, 96, 768)
        at(m, {n: [partial(rs.start, 1, ORD[n], 1)] for n in range(4)})
        return 0

    lax.fori_loop(0, 4, mlp_t, 0)
    now("N")

    sums = [jnp.zeros((8, 768), F32) for _ in range(4)]

    def fold(v):
        return jnp.sum(v.reshape(4, 8, 768), axis=0)

    gbl = act
    rows_of.inward(held, cot, range(9), CS, "drain")
    ob = cot
    for r0 in range(0, NR, 32):
        rows = slice(r0, r0 + 32)
        mk = mask_ref[rows, :]
        gm = gml[rows, :].astype(F32)
        hv = hid[rows, :]
        ob[r0 // 8 : r0 // 8 + 4] = (mk * (hv + mix[rows, :] + fb)).reshape(4, 8, 768).astype(BF)
        c, rstd = stats(hv)
        xh = c * rstd
        gv = gn2[rows, :]
        e2 = gv * g2
        gh = gm + rstd * (e2 - jnp.mean(e2, axis=-1, keepdims=True) - xh * jnp.mean(e2 * xh, axis=-1, keepdims=True))
        gb = mk * gh
        hid[rows, :] = gh
        gbl[rows, :] = gb.astype(BF)
        for n, v in enumerate((gv * xh, gv, gb, gm)):
            sums[n] = sums[n] + fold(v)
    for n in range(4):
        vg[0, n : n + 1, :] = jnp.sum(sums[n], axis=0, keepdims=True)
    rows_of.outward(ob, out_h, RET0, 22, "start")
    gn[...] = jnp.zeros_like(gn)

    def bwd_t(m, _):
        t = rank(BACK, m)
        at(m, {n: [partial(ag.drain, 0, BACK[n])] for n in range(4)})
        att_w = att[t]
        proj[:NR, :192] = dotf(gbl[...], weight(0, t)[:, 576:], NN)
        dqkv[...] = jnp.zeros_like(dqkv)
        for h in range(3):
            hh = 3 * t + h
            lo = 64 * h
            for wn in range(3):
                rows = slice(wn * WR, wn * WR + WR) if wn < 2 else slice(2 * WR, NR)
                dst = rows if wn < 2 else slice(NR, NE)
                do = proj[rows, lo : lo + 64].astype(BF)
                p = probs[hh, rows, :]
                pf = p.astype(F32)
                dp = dotf(do, vals[hh, wn], NT)
                delta = jnp.sum(pf * dp, axis=-1, keepdims=True)
                ds = (pf * (dp - delta)).astype(BF)
                dq = dotf(ds, kaug[hh, wn], NN)
                qa = qaug[hh, rows, :]
                dqkv[dst, 192 + lo : 256 + lo] = dotf(ds, qa, TN)[:, :64].astype(BF)
                dqkv[dst, 384 + lo : 448 + lo] = dotf(p, do, TN).astype(BF)
                rel = jnp.take_along_axis(dq, back_ref[rows, :], axis=1, mode="promise_in_bounds").astype(BF)
                gq = dq[:, :64] * 0.125 + dotf(rel, tab_ref[...], NN)
                dqkv[rows, lo : lo + 64] = gq.astype(BF)
                tg[0] += dotf(rel, qa, TN)[:64]
            hook(m, "B", h)
        vg[0, pl.ds(12 + t, 1), 0:576] = jnp.sum(dqkv[...].astype(F32), axis=0, keepdims=True)
        gn[...] += dotf(dqkv[...], weight(0, t)[:, :576], NT)
        gw = jnp.concatenate([dotf(nrm[...], dqkv[...], TN).astype(BF), dotf(gbl[...], att_w, TN).astype(BF)], axis=1)
        w[0, t] = gw.reshape(2, 2, 2, 96, 768)
        at(m, {n: [partial(rs.start, 0, BACK[n], 1)] for n in range(4)})
        return 0

    lax.fori_loop(0, 4, bwd_t, 0)

    gs[...] = gn[NR:].reshape(WR // 8, 8, 768).astype(BF)
    sh = [
        links.copy(gs.at[pl.ds(7 * ((z + d) % 4), 7)], gsr.at[d - 1], SH0 + d - 1, links.zdev((z + d) % 4)) for d in (1, 2, 3)
    ]
    for c in sh:
        c.start()
    now("T0")
    for c in sh:
        c.wait_recv()
    now("T1")
    first_norm_back(links, x, mask_ref, vec_ref, gn, hid, gsr, dx, vg.at[0])
    rows_of.outward(dx, dx_h, DX0, 31, "start")
    now("T2")
    small_sums(links, vg, tg, vr, tr, now)
    now("T3")
    vg_out[...] = vg[5]
    tg_out[...] = tg[5]
    for k in (2, 1, 0):
        own[k] = rs.total(k)
    rows_of.outward(ob, out_h, RET0, 22, "wait")
    rows_of.outward(dx, dx_h, DX0, 31, "wait")
    rows_of.outward(ob, out_h, RET0, 22, "drain")
    rows_of.outward(dx, dx_h, DX0, 31, "drain")
    for c in sh + bias:
        c.wait_send()
    for k in range(3):
        for i in (1, 2, 3):
            ag.move(k, "z", i).wait_send()
    rs.drain()


def first_norm_back(links, x, mask_ref, gain_ref, gn_ref, gh_ref, gsr, dx, vg):
    own = gn_ref[pl.ds(pl.multiple_of(NR + 56 * links.z, 8), 56), :]
    for d in range(3):
        own = own + gsr[d].astype(F32).reshape(56, 768)
    quarter = gn_ref[2 * WR : 2 * WR + 56, :] + own
    g1 = gain_ref[0:1, :]
    s_gain = jnp.zeros((8, 768), F32)
    s_bias = jnp.zeros((8, 768), F32)
    for r0, n in [(r, 32) for r in range(0, 2 * WR, 32)] + [(2 * WR, 56)]:
        rows = slice(r0, r0 + n)
        v = x[r0 // 8 : (r0 + n) // 8].astype(F32).reshape(n, 768)
        c = v - jnp.mean(v, axis=-1, keepdims=True)
        rs = lax.rsqrt(jnp.mean(c * c, axis=-1, keepdims=True) + 1e-6)
        xh = c * rs
        gn = mask_ref[rows, :] * (gn_ref[rows, :] if n == 32 else quarter)
        e1 = gn * g1
        gx = gh_ref[rows, :] + rs * (
            e1 - jnp.mean(e1, axis=-1, keepdims=True) - xh * jnp.mean(e1 * xh, axis=-1, keepdims=True)
        )
        dx[r0 // 8 : (r0 + n) // 8] = gx.reshape(n // 8, 8, 768).astype(BF)
        s_gain = s_gain + jnp.sum((gn * xh).reshape(n // 8, 8, 768), axis=0)
        s_bias = s_bias + jnp.sum(gn.reshape(n // 8, 8, 768), axis=0)
    vg[4:5, :] = jnp.sum(s_gain, axis=0, keepdims=True)
    vg[5:6, :] = jnp.sum(s_bias, axis=0, keepdims=True)


def small_sums(links, vg, tg, vr, tr, now):
    l = links
    partners = [l.sib, l.xn, l.yn, l.zdev((l.z // 2) * 2 + 1 - l.z % 2), l.zdev((l.z + 2) % 4)]
    copies = []
    for n, dev in enumerate(partners):
        pair = [l.copy(vg.at[n], vr.at[n], VS0 + 2 * n, dev), l.copy(tg.at[n], tr.at[n], VS0 + 2 * n + 1, dev)]
        for c in pair:
            c.start()
        now(f"S{n}")
        for c in pair:
            c.wait_recv()
        vg[n + 1] = vg[n] + vr[n]
        tg[n + 1] = tg[n] + tr[n]
        copies += pair
    for c in copies:
        c.wait_send()


def final_kernel(
    own, out_h, dx_h, vg, tg, out, dx, g_qkv, g_proj, g_fc1, g_fc2, v0, v1, v2, v3, v4, v5, fc1b_out, qvb_out, relh_out, relw_out,
    rows,
):
    for m in range(3):
        for b in range(3):
            dx[m, BT * b : BT * b + BT, :] = dx_h[3 * m + b].astype(F32).reshape(BP, 768)[:BT]
            rows[BT * b : BT * b + BT, :] = out_h[3 * m + b].astype(F32).reshape(BP, 768)[:BT]
        out[m] = rows[...].astype(BF)
    for n, ref in enumerate((v0, v1, v2, v3, v4, v5)):
        for c in range(6):
            ref[c : c + 1, :] = vg[n : n + 1, 128 * c : 128 * c + 128]
    for t in range(4):
        for c in range(6):
            fc1b_out[6 * t + c : 6 * t + c + 1, :] = vg[8 + t : 9 + t, 128 * c : 128 * c + 128]
        qvb_out[0:1, 192 * t : 192 * t + 192] = vg[12 + t : 13 + t, 0:192]
        qvb_out[1:2, 192 * t : 192 * t + 192] = vg[12 + t : 13 + t, 384:576]
    relh_out[...] = tg[0:27, :64] * 8.0
    relw_out[...] = tg[32:59, :64] * 8.0
    for t in range(3):
        g_qkv[t] = own[0, :, 192 * t : 192 * t + 192]
    g_proj[...] = own[0, :, 576:].T
    g_fc1[...] = own[1]
    g_fc2[...] = own[2]


def final_call(*arrays):
    shp = jax.ShapeDtypeStruct
    vm = pl.BlockSpec(memory_space=pltpu.VMEM)
    return pl.pallas_call(
        final_kernel,
        out_shape=(
            shp((3, 147, 768), BF), shp((3, 147, 768), F32), shp((3, 96, 192), F32), shp((192, 96), F32), shp((96, 768), F32),
            shp((96, 768), F32), *[shp((6, 128), F32)] * 6, shp((24, 128), F32), shp((2, 768), F32), shp((27, 64), F32),
            shp((27, 64), F32),
        ),
        in_specs=[vm] * 5,
        out_specs=(vm,) * 16,
        scratch_shapes=[pltpu.VMEM((147, 768), F32)],
    )(*arrays)


def whole_call(*arrays):
    shp = jax.ShapeDtypeStruct
    vm = pl.BlockSpec(memory_space=pltpu.VMEM)
    hbm = pl.BlockSpec(memory_space=pl.ANY)
    V = pltpu.VMEM
    dma = pltpu.SemaphoreType.DMA
    return pl.pallas_call(
        whole_kernel,
        out_shape=(
            shp((3, 96, 768), F32), shp((9, 7, 8, 768), BF), shp((9, 7, 8, 768), BF), shp((16, 768), F32), shp((64, 128), F32),
        ),
        in_specs=[hbm, hbm, pl.BlockSpec(memory_space=pltpu.SMEM)] + [vm] * 15,
        out_specs=(vm, hbm, hbm, vm, vm),
        scratch_shapes=[
            V((96, 768), BF), V((8, 768), F32), V((NE, 1), F32), V((NR, 128), jnp.int32), V((NR, 128), jnp.int32),
            V((8, 768), F32), V((128, 64), BF), V((128, 64), F32),
            V((3, 4, 2, 2, 2, 96, 768), BF), V((12, 2, 2, 96, 768), BF), V((12, 2, 2, 48, 768), BF), V((12, 2, 48, 768), BF),
            V((3, 3, 96, 768), BF), V((NE // 8, 8, 768), BF), V((NR // 8, 8, 768), BF), V((4, 8, 768), F32),
            V((3, 147, 768), BF), V((NR // 8, 8, 768), BF), V((NE, 768), F32), V((NR, 768), F32), V((NR, 768), F32),
            V((WR // 8, 8, 768), BF), V((3, 7, 8, 768), BF), V((6, 16, 768), F32), V((6, 64, 128), F32),
            V((5, 16, 768), F32), V((5, 64, 128), F32),
            V((NE, 768), BF), V((NE, 576), F32), V((HEADS, NR, 128), BF), V((HEADS, 3, WR, 128), BF), V((HEADS, 3, WR, 64), BF),
            V((HEADS, NR, WR), BF), V((4, NR, 192), BF), V((NR, 768), BF), V((NR, 768), BF), V((NR, 768), BF), V((NR, 768), BF),
            V((NE, 576), BF), dma((SEMS,)), dma((SEMS,)), dma((48,)),
        ],
        compiler_params=pltpu.CompilerParams(collective_id=0, has_side_effects=True, vmem_limit_bytes=67043328),
    )(*arrays)


def plain_gather(xh, coth, shard):
    mine = lax.dynamic_index_in_dim(jnp.asarray(block_table()), lax.axis_index("tensor"), 0, keepdims=False)

    def spread(held, count):
        blocks = lax.all_gather(held.reshape(3, 3, 7, 8, 768), "tensor", axis=1).reshape(36, 7, 8, 768)
        got = jnp.take(blocks, mine[:count], axis=0).reshape(-1, 8, 768)
        return jnp.concatenate([got[:63], jnp.zeros((1, 8, 768), BF), got[63:]], axis=0)

    whole = lax.all_gather(lax.all_gather(shard, ("dp", "win"), axis=1, tiled=True), "tensor", axis=1)
    return spread(xh, 13), spread(coth, 9), whole


def plain_scatter(grads, x, mask, vec, gn, gh, vg, tg, out):
    shared = lax.psum_scatter(gn[NR:], "tensor", scatter_dimension=0, tiled=True)
    gn = mask * (gn[:NR] + jnp.pad(shared, ((2 * WR, QR - BP), (0, 0))))
    xf = x[: NR // 8].reshape(NR, 768).astype(F32)
    cen = xf - jnp.mean(xf, axis=-1, keepdims=True)
    rs = lax.rsqrt(jnp.mean(cen * cen, axis=-1, keepdims=True) + 1e-6)
    xh = cen * rs
    e1 = gn * vec[0]
    gx = gh + rs * (e1 - jnp.mean(e1, axis=-1, keepdims=True) - xh * jnp.mean(e1 * xh, axis=-1, keepdims=True))
    vg = vg.at[4].set(jnp.sum(gn * xh, axis=0)).at[5].set(jnp.sum(gn, axis=0))
    back_to = lax.dynamic_index_in_dim(jnp.asarray(home_table()), lax.axis_index("tensor"), 0, keepdims=False)

    def bring(rows):
        blocks = lax.all_gather(rows[:63].reshape(9, 7, 8, 768), "tensor", axis=0, tiled=True)
        return jnp.take(blocks, back_to, axis=0)

    own = lax.psum_scatter(grads.reshape(3, 4, 768, 768), "tensor", scatter_dimension=1, tiled=False)
    own = lax.psum_scatter(own, ("dp", "win"), scatter_dimension=1, tiled=True).astype(F32)
    vg, tg = lax.psum((vg, tg), ("dp", "win", "tensor"))
    return own, bring(out), bring(gx.astype(BF).reshape(NR // 8, 8, 768)), vg, tg


def per_device(
    links, tokens, window_ids, norm1_gain, norm1_bias, qkv_weight, qv_bias, rel_height, rel_width, proj_weight, proj_bias,
    norm2_gain, norm2_bias, fc1_weight, fc1_bias, fc2_weight, fc2_bias, out_grad,
):
    rank = lax.axis_index("tensor")

    def home_blocks(rows):
        return jnp.pad(rows.reshape(9, BT, 768), ((0, 0), (0, BP - BT), (0, 0))).reshape(9, 7, 8, 768)

    if links:
        vectors = (norm1_gain, norm1_bias, proj_bias, norm2_gain, norm2_bias, fc2_bias, fc1_bias)
        done = whole_call(
            tokens[0], out_grad[0], jnp.transpose(window_ids, (1, 0, 2)), jnp.transpose(qkv_weight, (1, 0, 2)), proj_weight,
            fc1_weight, fc2_weight.T, *(v.reshape(6, 128) for v in vectors), qv_bias, rel_height, rel_width,
            jnp.asarray(key_tail(), BF),
        )
        out, dx, g_qkv, g_proj, g_fc1, g_fc2, v0, v1, v2, v3, v4, v5, fc1b, qvb, relh, relw = final_call(*done)
        v0, v1, v2, v3, v4, v5 = (v.reshape(768) for v in (v0, v1, v2, v3, v4, v5))
        return (
            out[None], dx[None], v4, v5, jnp.transpose(g_qkv, (1, 0, 2)), qvb, relh, relw, g_proj, v2, v0, v1, g_fc1,
            fc1b.reshape(-1), g_fc2.T, v3,
        )

    shard = jnp.stack(
        [
            jnp.concatenate([qkv_weight.reshape(-1, 576), proj_weight.T], axis=1),
            fc1_weight,
            fc2_weight.T,
        ]
    )
    xh, coth = home_blocks(tokens), home_blocks(out_grad)

    wi, wj, wv = token_positions()
    wi, wj, wv = jnp.asarray(wi, jnp.int32), jnp.asarray(wj, jnp.int32), jnp.asarray(wv)
    qi = jnp.pad(lax.dynamic_slice_in_dim(wi, rank * BP, BP), (0, QR - BP))
    qj = jnp.pad(lax.dynamic_slice_in_dim(wj, rank * BP, BP), (0, QR - BP))
    qv = jnp.pad(lax.dynamic_slice_in_dim(wv, rank * BP, BP), (0, QR - BP))
    ids = window_ids.reshape(9)
    slots = jnp.asarray([[m * 3 + s for m, s in WINDOWS_OF[dev]] + [4, 4] for dev in range(4)], jnp.int32)
    wid = jnp.take(ids, lax.dynamic_index_in_dim(slots, rank, 0, keepdims=False), axis=0)

    across = (GRID + WS - 1) // WS

    def valid(w, i, j, ok):
        return ok & (w < across * across) & ((w // across) * WS + i < GRID) & ((w % across) * WS + j < GRID)

    mask = jnp.concatenate(
        [valid(wid[0], wi, wj, wv), valid(wid[1], wi, wj, wv), valid(wid[2], qi, qj, qv), valid(wid[3], wi, wj, wv)]
    ).astype(F32)[:, None]
    ii = jnp.concatenate([wi, wi, qi])
    jj = jnp.concatenate([wj, wj, qj])
    fwd, back = pick_lanes(ii, jj)

    small = jnp.zeros((8, 768), F32).at[0].set(fc1_bias.astype(F32))
    small = small.at[1, :192].set(qv_bias[0].astype(F32)).at[1, 384:576].set(qv_bias[1].astype(F32))
    vec = jnp.stack(
        [norm1_gain, norm1_bias, proj_bias, norm2_gain, norm2_bias, fc2_bias, fc2_bias, fc2_bias]
    ).astype(F32)
    tab = jnp.zeros((128, 64), BF).at[0:27].set(rel_height).at[32:59].set(rel_width)
    tabt = (tab * BF(8)).T
    ktail = jnp.asarray(key_tail(), BF)

    x, cot, whole = plain_gather(xh, coth, shard)
    small = lax.all_gather(small, "tensor", axis=0)
    out, gn, gh, grads, vg, tg = compute(
        x, cot, mask, whole.reshape(3, 4, 768, 768), vec, small[:, 1:2, :576], small[:, 0:1], ktail, fwd, back, tab, tabt
    )
    own, out, dx, vg, tg = plain_scatter(grads, x, mask[:NR], vec, gn, gh, vg, tg, out)

    def tokens_of(blocks):
        return blocks.reshape(9, BP, 768)[:, :BT].reshape(tokens.shape)

    output = tokens_of(out)
    grad_tokens = tokens_of(dx).astype(F32)
    g_qkv = own[0, :, :576].reshape(qkv_weight.shape)
    g_proj = own[0, :, 576:].T
    g_fc1 = own[1]
    g_fc2 = own[2].T
    g_qv = jnp.stack([vg[12:16, :192].reshape(-1), vg[12:16, 384:576].reshape(-1)])
    return (
        output, grad_tokens, vg[4], vg[5], g_qkv, g_qv, tg[0:27, :64] * 8.0, tg[32:59, :64] * 8.0, g_proj,
        vg[2], vg[0], vg[1], g_fc1, vg[8:12].reshape(-1), g_fc2, vg[3],
    )


def solution(mesh):
    in_specs = (
        P("dp", "win", "tensor", None), P("dp", "win", None), P(), P(), P(("dp", "win"), None, "tensor"),
        P(None, "tensor"), P(), P(), P("tensor", ("dp", "win")), P(), P(), P(), P(("dp", "win"), "tensor"), P("tensor"),
        P("tensor", ("dp", "win")), P(), P("dp", "win", "tensor", None),
    )
    out_specs = (
        P("dp", "win", "tensor", None), P("dp", "win", "tensor", None), P(), P(), P(("dp", "win"), None, "tensor"), P(),
        P(), P(), P("tensor", ("dp", "win")), P(), P(), P(), P(("dp", "win"), "tensor"), P(),
        P("tensor", ("dp", "win")), P(),
    )
    links = dict(mesh.shape) == {"dp": 2, "win": 4, "tensor": 4}
    return jax.shard_map(partial(per_device, links), mesh=mesh, in_specs=in_specs, out_specs=out_specs, check_vma=False)
```

```python
import math
from functools import partial

import jax
import jax.numpy as jnp
import numpy as np
from jax import lax
from jax.experimental import pallas as pl
from jax.experimental.pallas import tpu as pltpu
from jax.sharding import PartitionSpec as P

HEADS = 12
HD = 64
WS = 14
GRID = 64
WT = 196
BT = 49
BP = 56
WR = 4 * BP
QR = 64
NR = 2 * WR + QR
NE = NR + WR
BF = jnp.bfloat16
F32 = jnp.float32

WINDOWS_OF = (((0, 0), (1, 0)), ((2, 0), (0, 1)), ((2, 2), (2, 1)), ((0, 2), (1, 2)))
SHARED = (1, 1)


def block_table():
    rows = []
    for dev in range(4):
        row = []
        for m, s in WINDOWS_OF[dev]:
            row += [m * 12 + 4 * s + j for j in range(4)]
        row.append(SHARED[0] * 12 + 4 * SHARED[1] + dev)
        row += [SHARED[0] * 12 + 4 * SHARED[1] + j for j in range(4)]
        rows.append(row)
    return np.array(rows, np.int32)


def home_table():
    table = block_table()
    place = {}
    for dev in range(4):
        for slot in range(9):
            place[int(table[dev, slot])] = dev * 9 + slot
    return np.array([[place[m * 12 + 3 * dev + b] for m in range(3) for b in range(3)] for dev in range(4)], np.int32)


def token_positions():
    row = np.arange(WR)
    off = row % BP
    token = (row // BP) * BT + np.minimum(off, BT - 1)
    return token // WS, token % WS, off < BT


def key_tail():
    i, j, valid = token_positions()
    tail = np.zeros((WR, 128), np.float32)
    for m in range(WS):
        tail[:, 64 + m] = i == m
        tail[:, 78 + m] = j == m
    tail[:, 92:120] = tail[:, 64:92]
    tail[:, :120] *= valid[:, None]
    tail[:, 120] = np.where(valid, 0.0, -1e30)
    return tail


def pick_lanes(i, j):
    lane = np.arange(128)[None, :]
    m = np.clip((lane - 64) % 28, 0, 27)
    is_w = m >= 14
    fwd = jnp.where(is_w, 32 + j[:, None] - (m - 14) + 13, i[:, None] - m + 13)
    fwd = jnp.where((lane >= 64) & (lane < 120), fwd, 0)
    d = lane % 32
    pos = jnp.where(lane >= 32, j[:, None], i[:, None]) + 13 - d
    ok = (pos >= 0) & (pos < WS) & (lane < 64) & (d < 27)
    back = jnp.where(ok, pos + jnp.where(lane >= 32, 78, 64), 127)
    return fwd.astype(jnp.int32), back.astype(jnp.int32)


def dotf(a, b, dims):
    return lax.dot_general(a, b, (dims, ((), ())), preferred_element_type=F32)


NN = ((1,), (0,))
NT = ((1,), (1,))
TN = ((0,), (0,))


def compute_kernel(
    x_ref, cot_ref, mask_ref, w_ref, vec_ref, qkvb_ref, fc1b_ref, ktail_ref, fwd_ref, back_ref, tab_ref, tabt_ref,
    out_ref, gn_ref, gh_ref, g_ref, vg_ref, tg_ref,
    nrm, proj, qaug, kaug, vals, probs, att, hid, nr2, mix, gn2, act, gup, gml, gbl, dqkv,
):
    g1, b1, pb, g2, b2, fb = (vec_ref[i : i + 1, :] for i in range(6))

    def stats(v):
        mu = jnp.mean(v, axis=-1, keepdims=True)
        c = v - mu
        var = jnp.mean(c * c, axis=-1, keepdims=True)
        return c, lax.rsqrt(var + 1e-6)

    vg_ref[...] = jnp.zeros_like(vg_ref)

    for r0 in range(0, NE, 32):
        rows = slice(r0, r0 + 32)
        c, rs = stats(x_ref[r0 // 8 : r0 // 8 + 4].astype(F32).reshape(32, 768))
        nrm[rows, :] = (mask_ref[rows, :] * (c * rs * g1 + b1)).astype(BF)

    def fwd_t(t, _):
        proj[...] = dotf(nrm[...], w_ref[0, t][:, :576], NN) + qkvb_ref[t]
        for h in range(3):
            hh = 3 * t + h
            qs = (proj[:NR, 64 * h : 64 * h + 64].astype(BF) * BF(0.125)).astype(BF)
            rel = dotf(qs, tabt_ref[...], NN)
            lane = lax.broadcasted_iota(jnp.int32, (NR, 128), 1)
            got = jnp.take_along_axis(rel, fwd_ref[...], axis=1, mode="promise_in_bounds")
            hi = got.astype(BF).astype(F32)
            tail = jnp.where(lane < 92, hi, got - hi)
            tail = jnp.where(lane == 120, 1.0, jnp.where(lane < 120, tail, 0.0)).astype(BF)
            qa = jnp.concatenate([qs, tail[:, 64:]], axis=1)
            qaug[hh] = qa
            for w in range(3):
                src = slice(w * WR, w * WR + WR) if w < 2 else slice(NR, NE)
                k = proj[src, 192 + 64 * h : 256 + 64 * h].astype(BF)
                kaug[hh, w] = jnp.concatenate([k, ktail_ref[:, 64:]], axis=1)
                vals[hh, w] = proj[src, 384 + 64 * h : 448 + 64 * h].astype(BF)
        return 0

    lax.fori_loop(0, 4, fwd_t, 0)
    mix[...] = jnp.zeros_like(mix)

    def att_t(t, _):
        for h in range(3):
            hh = 3 * t + h
            for w in range(3):
                rows = slice(w * WR, w * WR + WR) if w < 2 else slice(2 * WR, NR)
                s = dotf(qaug[hh, rows, :], kaug[hh, w], NT)
                e = jnp.exp(s - jnp.max(s, axis=-1, keepdims=True))
                p = (e * (1.0 / jnp.sum(e, axis=-1, keepdims=True))).astype(BF)
                probs[hh, rows, :] = p
                att[t, rows, 64 * h : 64 * h + 64] = dotf(p, vals[hh, w], NN).astype(BF)
        mix[...] += dotf(att[t], w_ref[0, t][:, 576:], NT)
        return 0

    lax.fori_loop(0, 4, att_t, 0)

    for r0 in range(0, NR, 32):
        rows = slice(r0, r0 + 32)
        x = x_ref[r0 // 8 : r0 // 8 + 4].astype(F32).reshape(32, 768)
        hv = x + mask_ref[rows, :] * (mix[rows, :] + pb)
        hid[rows, :] = hv
        c, rs = stats(hv)
        nr2[rows, :] = (c * rs * g2 + b2).astype(BF)
        gm = mask_ref[rows, :] * cot_ref[r0 // 8 : r0 // 8 + 4].astype(F32).reshape(32, 768)
        gml[rows, :] = gm.astype(BF)
    mix[...] = jnp.zeros_like(mix)
    gn2[...] = jnp.zeros_like(gn2)

    def mlp_t(t, _):
        for f in range(3):
            cols = slice(256 * f, 256 * f + 256)
            for r0 in range(0, NR, 128):
                rows = slice(r0, r0 + 128)
                up = dotf(nr2[rows, :], w_ref[1, t][:, cols], NN) + fc1b_ref[t][:, cols]
                ga = dotf(gml[rows, :], w_ref[2, t][:, cols], NN)
                cdf = 0.5 * (1.0 + lax.erf(up * (1.0 / math.sqrt(2.0))))
                pdf = jnp.exp(-0.5 * up * up) * (1.0 / math.sqrt(2.0 * math.pi))
                act[rows, cols] = (up * cdf).astype(BF)
                gup[rows, cols] = (ga * (cdf + up * pdf)).astype(BF)
        vg_ref[pl.ds(8 + t, 1), :] = jnp.sum(gup[...].astype(F32), axis=0, keepdims=True)
        mix[...] += dotf(act[...], w_ref[2, t], NT)
        gn2[...] += dotf(gup[...], w_ref[1, t], NT)
        g_ref[2, t] = dotf(gml[...], act[...], TN).astype(BF)
        g_ref[1, t] = dotf(nr2[...], gup[...], TN).astype(BF)
        return 0

    lax.fori_loop(0, 4, mlp_t, 0)

    sums = [jnp.zeros((8, 768), F32) for _ in range(4)]

    def fold(v):
        return jnp.sum(v.reshape(4, 8, 768), axis=0)

    for r0 in range(0, NR, 32):
        rows = slice(r0, r0 + 32)
        mk = mask_ref[rows, :]
        gm = mk * cot_ref[r0 // 8 : r0 // 8 + 4].astype(F32).reshape(32, 768)
        hv = hid[rows, :]
        out_ref[r0 // 8 : r0 // 8 + 4] = (mk * (hv + mix[rows, :] + fb)).reshape(4, 8, 768).astype(BF)
        c, rs = stats(hv)
        xh = c * rs
        gn = gn2[rows, :]
        e2 = gn * g2
        gh = gm + rs * (e2 - jnp.mean(e2, axis=-1, keepdims=True) - xh * jnp.mean(e2 * xh, axis=-1, keepdims=True))
        gb = mk * gh
        gh_ref[rows, :] = gh
        gbl[rows, :] = gb.astype(BF)
        for n, v in enumerate((gn * xh, gn, gb, gm)):
            sums[n] = sums[n] + fold(v)
    for n in range(4):
        vg_ref[n : n + 1, :] = jnp.sum(sums[n], axis=0, keepdims=True)
    tg_ref[...] = jnp.zeros_like(tg_ref)
    gn_ref[...] = jnp.zeros_like(gn_ref)

    def bwd_t(t, _):
        att_w = att[t]
        g_ref[0, t, :, 576:] = dotf(gbl[...], att_w, TN).astype(BF)
        proj[:NR, :192] = dotf(gbl[...], w_ref[0, t][:, 576:], NN)
        dqkv[...] = jnp.zeros_like(dqkv)
        for h in range(3):
            hh = 3 * t + h
            lo = 64 * h
            for w in range(3):
                rows = slice(w * WR, w * WR + WR) if w < 2 else slice(2 * WR, NR)
                dst = rows if w < 2 else slice(NR, NE)
                do = proj[rows, lo : lo + 64].astype(BF)
                p = probs[hh, rows, :]
                pf = p.astype(F32)
                dp = dotf(do, vals[hh, w], NT)
                delta = jnp.sum(pf * dp, axis=-1, keepdims=True)
                ds = (pf * (dp - delta)).astype(BF)
                dq = dotf(ds, kaug[hh, w], NN)
                qa = qaug[hh, rows, :]
                dqkv[dst, 192 + lo : 256 + lo] = dotf(ds, qa, TN)[:, :64].astype(BF)
                dqkv[dst, 384 + lo : 448 + lo] = dotf(p, do, TN).astype(BF)
                rel = jnp.take_along_axis(dq, back_ref[rows, :], axis=1, mode="promise_in_bounds").astype(BF)
                gq = dq[:, :64] * 0.125 + dotf(rel, tab_ref[...], NN)
                dqkv[rows, lo : lo + 64] = gq.astype(BF)
                tg_ref[...] += dotf(rel, qa, TN)[:64]
        vg_ref[pl.ds(12 + t, 1), 0:576] = jnp.sum(dqkv[...].astype(F32), axis=0, keepdims=True)
        g_ref[0, t, :, :576] = dotf(nrm[...], dqkv[...], TN).astype(BF)
        gn_ref[...] += dotf(dqkv[...], w_ref[0, t][:, :576], NT)
        return 0

    lax.fori_loop(0, 4, bwd_t, 0)


def compute(x, cot, mask, w, vec, qkvb, fc1b, ktail, fwd, back, tab, tabt):
    shp = jax.ShapeDtypeStruct
    vm = pl.BlockSpec(memory_space=pltpu.VMEM)
    return pl.pallas_call(
        compute_kernel,
        out_shape=(
            shp((NR // 8, 8, 768), BF), shp((NE, 768), F32), shp((NR, 768), F32), shp((3, 4, 768, 768), BF),
            shp((16, 768), F32), shp((64, 128), F32),
        ),
        in_specs=[vm] * 12,
        out_specs=(vm,) * 6,
        scratch_shapes=[
            pltpu.VMEM((NE, 768), BF), pltpu.VMEM((NE, 576), F32), pltpu.VMEM((HEADS, NR, 128), BF),
            pltpu.VMEM((HEADS, 3, WR, 128), BF), pltpu.VMEM((HEADS, 3, WR, 64), BF), pltpu.VMEM((HEADS, NR, WR), BF),
            pltpu.VMEM((4, NR, 192), BF), pltpu.VMEM((NR, 768), F32), pltpu.VMEM((NR, 768), BF),
            pltpu.VMEM((NR, 768), F32), pltpu.VMEM((NR, 768), F32), pltpu.VMEM((NR, 768), BF), pltpu.VMEM((NR, 768), BF),
            pltpu.VMEM((NR, 768), BF), pltpu.VMEM((NR, 768), BF), pltpu.VMEM((NE, 576), BF),
        ],
        compiler_params=pltpu.CompilerParams(vmem_limit_bytes=67043328),
    )(x, cot, mask, w, vec, qkvb, fc1b, ktail, fwd, back, tab, tabt)


MESH = pl.DeviceIdType.MESH


class Links:
    def __init__(self, send, recv):
        self.send, self.recv = send, recv
        self.x = lax.axis_index("dp")
        win = lax.axis_index("win")
        self.y, self.c = win // 2, win % 2
        self.z = lax.axis_index("tensor")
        self.xn = (1 - self.x, win, self.z)
        self.yn = (self.x, (1 - self.y) * 2 + self.c, self.z)
        self.sib = (self.x, self.y * 2 + 1 - self.c, self.z)
        self.win = win

    def zdev(self, z):
        return (self.x, self.win, z)

    def barrier(self):
        sem = pltpu.get_barrier_semaphore()
        others = [self.xn, self.yn, self.sib] + [self.zdev((self.z + d) % 4) for d in (1, 2, 3)]
        for dev in others:
            pl.semaphore_signal(sem, inc=1, device_id=dev, device_id_type=MESH)
        pl.semaphore_wait(sem, len(others))

    def copy(self, src, dst, n, dev):
        return pltpu.make_async_remote_copy(
            src_ref=src, dst_ref=dst, send_sem=self.send.at[n], recv_sem=self.recv.at[n], device_id=dev,
            device_id_type=MESH,
        )


AG_SEMS = 3 * 39


class Gather:
    def __init__(self, links, shards, w, local, base):
        self.l, self.shards, self.w, self.local, self.base = links, shards, w, local, base

    def sem(self, k, kind, i):
        start = {"z": 0, "x": 3, "y": 7, "hx": 11, "hy": 15, "so": 19, "sx": 23, "sy": 27, "sa": 31, "sb": 35}[kind]
        return self.base + k * 39 + start + i

    def rank(self, i):
        return (self.l.z + 4 - i) % 4

    def piece(self, k, i, px, py, c, half=None):
        ref = self.w.at[k, self.rank(i), px, py, c]
        return ref if half is None else ref.at[pl.ds(48 * half, 48)]

    def move(self, k, kind, i):
        l = self.l
        if kind == "z":
            src = self.shards[k]
            return l.copy(src, self.piece(k, 0, l.x, l.y, l.c), self.sem(k, kind, i - 1), l.zdev((l.z + i) % 4))
        px, py, half, dev = {
            "x": (l.x, l.y, None, l.xn), "y": (l.x, l.y, None, l.yn),
            "hx": (l.x, 1 - l.y, 1, l.xn), "hy": (1 - l.x, l.y, 0, l.yn),
            "so": (l.x, l.y, None, l.sib), "sx": (1 - l.x, l.y, None, l.sib), "sy": (l.x, 1 - l.y, None, l.sib),
            "sa": (1 - l.x, 1 - l.y, 0, l.sib), "sb": (1 - l.x, 1 - l.y, 1, l.sib),
        }[kind]
        dst = self.piece(k, i, px, py, l.c, half)
        own = kind in ("x", "y", "so") and i == 0
        return l.copy(self.shards[k] if own else dst, dst, self.sem(k, kind, i), dev)

    def start(self, k, kind, i):
        self.move(k, kind, i).start()

    def arrived(self, k, kind, i):
        self.move(k, kind, i).wait_recv()

    def keep(self, k):
        l = self.l
        return pltpu.make_async_copy(self.shards[k], self.piece(k, 0, l.x, l.y, l.c), self.local.at[k])

    def own_z(self, k):
        for i in (1, 3, 2):
            self.start(k, "z", i)

    def along(self, k, i):
        if i:
            self.arrived(k, "z", i)
        else:
            self.keep(k).start()
        for kind in ("x", "y", "so"):
            self.start(k, kind, i)

    def across(self, k, i):
        self.arrived(k, "x", i)
        self.start(k, "hy", i)
        self.start(k, "sx", i)
        self.arrived(k, "y", i)
        self.start(k, "hx", i)
        self.start(k, "sy", i)

    def corner(self, k, i):
        self.arrived(k, "hy", i)
        self.start(k, "sa", i)
        self.arrived(k, "hx", i)
        self.start(k, "sb", i)

    def partner(self, k, i):
        for kind in ("so", "sx", "sy", "sa", "sb"):
            self.arrived(k, kind, i)
        if not i:
            self.keep(k).wait()

    def drain(self, k, i):
        for kind in ("x", "y", "hx", "hy", "so", "sx", "sy", "sa", "sb"):
            self.move(k, kind, i).wait_send()


RS_SEMS = 12 * 6


class Scatter:
    def __init__(self, links, w, r1, r2, r3, r4, base):
        self.l, self.w, self.r1, self.r2, self.r3, self.r4, self.base = links, w, r1, r2, r3, r4, base

    def g(self, k, i):
        return self.w.at[k, (self.l.z + 4 - i) % 4]

    def moves(self, k, i, stage):
        l, n = self.l, 4 * k + i
        s = self.base + 6 * n
        g = self.g(k, i)
        if stage == 1:
            return [l.copy(g.at[:, :, 1 - l.c], self.r1.at[n], s, l.sib)]
        if stage == 2:
            return [
                l.copy(g.at[:, 1 - l.y, l.c, 0:48], self.r2.at[n, 0], s + 1, l.yn),
                l.copy(g.at[1 - l.x, :, l.c, 48:96], self.r2.at[n, 1], s + 2, l.xn),
            ]
        if stage == 3:
            return [
                l.copy(g.at[1 - l.x, l.y, l.c, 0:48], self.r3.at[n, 0], s + 3, l.xn),
                l.copy(g.at[l.x, 1 - l.y, l.c, 48:96], self.r3.at[n, 1], s + 4, l.yn),
            ]
        return [l.copy(g.at[l.x, l.y, l.c], self.r4.at[k, i - 1], s + 5, l.zdev((l.z + 4 - i) % 4))] if i else []

    def start(self, k, i, stage):
        for m in self.moves(k, i, stage):
            m.start()

    def wait(self, k, i, stage):
        for m in self.moves(k, i, stage):
            m.wait_recv()

    def step(self, k, i, stage):
        l, g, n = self.l, self.g(k, i), 4 * k + i
        self.wait(k, i, stage - 1)
        if stage == 2:
            for a in range(2):
                for b in range(2):
                    ref = g.at[a, b, l.c]
                    ref[...] = ref[...] + self.r1[n, a, b]
        elif stage == 3:
            for a in range(2):
                ref = g.at[a, l.y, l.c, 0:48]
                ref[...] = ref[...] + self.r2[n, 0, a]
                ref = g.at[l.x, a, l.c, 48:96]
                ref[...] = ref[...] + self.r2[n, 1, a]
        else:
            for h in range(2):
                ref = g.at[l.x, l.y, l.c, pl.ds(48 * h, 48)]
                ref[...] = ref[...] + self.r3[n, h]
        self.start(k, i, stage)

    def total(self, k):
        l = self.l
        fin = self.g(k, 0)[l.x, l.y, l.c].astype(F32)
        for i in (1, 2, 3):
            self.wait(k, i, 4)
            fin = fin + self.r4[k, i - 1].astype(F32)
        return fin

    def drain(self):
        for k in range(3):
            for i in range(4):
                for stage in (1, 2, 3, 4):
                    for m in self.moves(k, i, stage):
                        m.wait_send()


class Rows:
    TABLE = block_table()

    def __init__(self, links, local):
        self.l, self.local = links, local

    @staticmethod
    def home(block):
        m, b = divmod(int(block), 12)
        return b // 3, m * 3 + b % 3

    @staticmethod
    def unit(slot):
        return 7 * slot if slot < 9 else NR // 8 + 7 * (slot - 9)

    def inward(self, held, rows, slots, base, do):
        l = self.l
        for me in range(4):

            @pl.when(l.z == me)
            def _():
                sent = 0
                for slot in slots:
                    for step in range(4):
                        dev = (me + step) % 4
                        owner, idx = self.home(self.TABLE[dev, slot])
                        if owner != me:
                            continue
                        dst = rows.at[pl.ds(self.unit(slot), 7)]
                        if dev == me:
                            if do != "drain":
                                c = pltpu.make_async_copy(held.at[idx], dst, self.local.at[base + slot])
                                c.start() if do == "start" else c.wait()
                            continue
                        sent += 1
                        if do == "wait":
                            continue
                        c = pltpu.make_async_remote_copy(
                            src_ref=held.at[idx], dst_ref=dst, send_sem=l.send.at[base + sent - 1],
                            recv_sem=l.recv.at[base + slot], device_id=l.zdev(dev), device_id_type=MESH,
                        )
                        c.start() if do == "start" else c.wait_send()
                    owner, idx = self.home(self.TABLE[me, slot])
                    if do == "wait" and owner != me:
                        pltpu.make_async_remote_copy(
                            src_ref=held.at[0], dst_ref=rows.at[pl.ds(self.unit(slot), 7)], send_sem=l.send.at[base],
                            recv_sem=l.recv.at[base + slot], device_id=l.zdev(owner), device_id_type=MESH,
                        ).wait_recv()

    def outward(self, rows, held, base, mine, do):
        l = self.l
        for me in range(4):

            @pl.when(l.z == me)
            def _():
                for slot in range(9):
                    owner, idx = self.home(self.TABLE[me, slot])
                    src = rows.at[pl.ds(7 * slot, 7)]
                    if owner == me:
                        if do != "drain":
                            c = pltpu.make_async_copy(src, held.at[idx], self.local.at[mine + slot])
                            c.start() if do == "start" else c.wait()
                    elif do != "wait":
                        c = pltpu.make_async_remote_copy(
                            src_ref=src, dst_ref=held.at[idx], send_sem=l.send.at[base + slot],
                            recv_sem=l.recv.at[base + idx], device_id=l.zdev(owner), device_id_type=MESH,
                        )
                        c.start() if do == "start" else c.wait_send()
                for dev in range(4):
                    for slot in range(9):
                        owner, idx = self.home(self.TABLE[dev, slot])
                        if do == "wait" and owner == me and dev != me:
                            pltpu.make_async_remote_copy(
                                src_ref=rows.at[pl.ds(0, 7)], dst_ref=held.at[idx], send_sem=l.send.at[base],
                                recv_sem=l.recv.at[base + idx], device_id=l.zdev(dev), device_id_type=MESH,
                            ).wait_recv()


XS, CS, BS = 0, 13, 22
AG0 = BS + 3
RET0 = AG0 + AG_SEMS
DX0 = RET0 + 9
SH0 = DX0 + 9
VS0 = SH0 + 3
RS0 = VS0 + 10
SEMS = RS0 + RS_SEMS
X_SLOTS = (0, 1, 2, 3, 4, 5, 6, 7, 9, 10, 11, 12)

ORD = (0, 1, 3, 2)
BACK = (2, 1, 3, 0)
BLOCKS = ((0, 0), (1, 0), (0, 1), (0, 3), (0, 2), (2, 0), (1, 1), (2, 1), (1, 3), (2, 3), (1, 2), (2, 2))


PLACES = (
    [("M", n, j) for n in range(4) for j in range(5)] + ["N"] + [("B", n, j) for n in range(4) for j in range(3)]
    + ["T0", "T1", "T2", "S0", "S1", "S2", "S3", "S4", "T3"]
)
TICKS = {1: ("F", 0, 0), 2: ("F", 0, 3), 3: ("F", 1, 2), 4: ("F", 2, 2), 5: ("F", 3, 2), 6: "L", 7: ("M", 0, 0), 8: ("M", 0, 4),
         9: ("M", 1, 1), 10: ("M", 1, 4), 11: ("M", 2, 1)}
MLP_LAGS = ((1, 9, 15), (3, 11, 17))
BWD_LAGS = (0, 3, 5)


def timetable():
    plan = {}

    def put(place, *event):
        plan.setdefault(place, []).append(event)

    for s, place in TICKS.items():
        put(place, "tick", s)
    for n in range(4):
        for k, lags in zip((2, 1), MLP_LAGS):
            made = PLACES.index(("M", n, 4)) + 1
            for stage, lag in zip((2, 3, 4), lags):
                put(PLACES[made + lag], "step", k, ORD[n], stage)
        made = PLACES.index(("B", n, 2)) + 1
        for stage, lag in zip((2, 3, 4), BWD_LAGS):
            put(PLACES[made + lag], "step", 0, BACK[n], stage)
    return plan


def places(rows, first):
    r = lax.broadcasted_iota(jnp.int32, (rows, 128), 0)
    blk = sum((r >= BP * n).astype(jnp.int32) for n in range(1, 4)) if rows == WR else jnp.zeros_like(r)
    off = r - BP * blk
    token = (blk + first) * BT + jnp.minimum(off, BT - 1)
    i = (token * 4682) >> 16
    return i, token - WS * i, off < BT


def lanes_of(i, j):
    lane = lax.broadcasted_iota(jnp.int32, i.shape, 1)
    m = lane - 64
    m = m - 28 * ((m >= 28).astype(jnp.int32) + (m >= 56).astype(jnp.int32))
    fwd = jnp.where(m >= 14, 32 + j - (m - 14) + 13, i - m + 13)
    fwd = jnp.where((lane >= 64) & (lane < 120), fwd, 0)
    d = lane & 31
    pos = jnp.where(lane >= 32, j, i) + 13 - d
    ok = (pos >= 0) & (pos < WS) & (lane < 64) & (d < 27)
    return fwd, jnp.where(ok, pos + jnp.where(lane >= 32, 78, 64), 127)


def fill_tables(z, ids, mask_ref, fwd_ref, back_ref):
    across = (GRID + WS - 1) // WS

    def valid(w, i, j, ok):
        a = lax.div(w, jnp.int32(across))
        hi = jnp.where(w < across * across, GRID - a * WS, 0)
        wi = GRID - (w - across * a) * WS
        return jnp.where(ok & (i < hi) & (j < wi), 1.0, 0.0)[:, :1]

    def window(n):
        m, s = (jnp.int32(v) for v in WINDOWS_OF[3][n])
        for dev in range(3):
            m = jnp.where(z == dev, WINDOWS_OF[dev][n][0], m)
            s = jnp.where(z == dev, WINDOWS_OF[dev][n][1], s)
        return ids[m, 0, s]

    i, j, ok = places(WR, 0)
    fwd, back = lanes_of(i, j)
    shared = ids[SHARED[0], 0, SHARED[1]]
    for n in range(2):
        rows = slice(n * WR, n * WR + WR)
        fwd_ref[rows, :] = fwd
        back_ref[rows, :] = back
        mask_ref[rows, :] = valid(window(n), i, j, ok)
    mask_ref[NR:NE, :] = valid(shared, i, j, ok)
    i, j, ok = places(QR, z)
    fwd, back = lanes_of(i, j)
    fwd_ref[2 * WR : NR, :] = fwd
    back_ref[2 * WR : NR, :] = back
    mask_ref[2 * WR : NR, :] = valid(shared, i, j, ok)


def whole_kernel(
    x_raw, cot_raw, ids, *refs,
):
    given, refs, held_in, load = refs[:15], refs[15:-16], refs[-16:-1], refs[-1]
    qkv_w, proj_w, fc1_w, fc2_w, u0, u1, u2, u3, u4, u5, u6, qvb_in, relh_in, relw_in, ktail_ref = held_in
    (
        own, out_h, dx_h, vg_out, tg_out, shard0, small, mask_ref, fwd_ref, back_ref, vec_ref, tab_ref, tabf, w, r1,
        r2, r3, r4, x, cot, sm, raw, dx, gn, hid, gn2, gs, gsr, vg, tg, vr, tr, nrm, proj, qaug, kaug, vals, probs,
        att, nr2, act, gup, gml, dqkv, send, recv, local,
    ) = refs
    links = Links(send, recv)
    z = links.z
    rows_of = Rows(links, local)
    ag = Gather(links, (shard0, fc1_w, fc2_w), w, local.at[pl.ds(40, 3)], AG0)
    rs = Scatter(links, w, r1, r2, r3, r4, RS0)

    def rank(order, m):
        i = jnp.int32(order[3])
        for n in range(3):
            i = jnp.where(m == n, order[n], i)
        return (z + 4 - i) % 4

    def weight(k, t):
        return w[k, t].reshape(768, 768)

    def tick(s):
        if s + 2 < 12:
            ag.along(*BLOCKS[s + 2])
        if s + 1 < 12:
            ag.across(*BLOCKS[s + 1])
        ag.corner(*BLOCKS[s])

    def at(m, plan):
        for n, todo in plan.items():

            @pl.when(m == n)
            def _():
                for f in todo:
                    f()

    plan = timetable()

    def run(events):
        for what, *which in events:
            if what == "tick":
                tick(*which)
            else:
                rs.step(*which)

    def now(place):
        run(plan.get(place, ()))

    def hook(m, loop, j):
        for n in range(4):
            todo = plan.get((loop, n, j))
            if todo:

                @pl.when(m == n)
                def _():
                    run(todo)

    def stats(v):
        mu = jnp.mean(v, axis=-1, keepdims=True)
        c = v - mu
        var = jnp.mean(c * c, axis=-1, keepdims=True)
        return c, lax.rsqrt(var + 1e-6)

    read_x = pltpu.make_async_copy(x_raw, raw, local.at[44])
    read_x.start()
    loads = [pltpu.make_async_copy(a, b, load.at[n]) for n, (a, b) in enumerate(zip(given, held_in))]
    for c in loads:
        c.start()
    loads[0].wait()
    loads[1].wait()
    for t in range(3):
        shard0[:, 192 * t : 192 * t + 192] = qkv_w[t]
    shard0[:, 576:] = proj_w[...].astype(F32).T.astype(BF)
    x[63] = jnp.zeros((8, 768), BF)
    cot[63] = jnp.zeros((8, 768), BF)
    links.barrier()
    for c in loads[2:]:
        c.wait()
    for b in (0, 1):
        ag.along(*BLOCKS[b])
    small[...] = jnp.zeros_like(small)
    for n, u in enumerate((u0, u1, u2, u3, u4, u5, u6)):
        ref, row = (vec_ref, n) if n < 6 else (small, 0)
        uf = u[...].astype(F32)
        for c in range(6):
            ref[row : row + 1, 128 * c : 128 * c + 128] = uf[c : c + 1, :]
    qvb = qvb_in[...].astype(F32)
    small[1:2, 0:192] = qvb[0:1]
    small[1:2, 384:576] = qvb[1:2]
    bias = [links.copy(small, sm.at[z], BS + d - 1, links.zdev((z + d) % 4)) for d in (1, 2, 3)]
    keep_bias = pltpu.make_async_copy(small, sm.at[z], local.at[43])
    keep_bias.start()
    for c in bias:
        c.start()

    def pad_blocks(held):
        for m in range(3):
            gn2[0:147, :] = raw[m].astype(F32)
            for b in range(3):
                v = gn2[BT * b : BT * b + BP, :]
                v = jnp.where(lax.broadcasted_iota(jnp.int32, v.shape, 0) < BT, v, 0.0)
                held[3 * m + b] = v.astype(BF).reshape(7, 8, 768)

    held = dx.at[pl.ds(0, 63)].reshape(9, 7, 8, 768)
    read_x.wait()
    pad_blocks(held)
    rows_of.inward(held, x, X_SLOTS, XS, "start")
    ag.own_z(0)
    read_cot = pltpu.make_async_copy(cot_raw, raw, local.at[44])
    read_cot.start()
    ag.own_z(1)
    tabf[...] = jnp.zeros_like(tabf)
    tabf[0:27, :] = relh_in[...].astype(F32)
    tabf[32:59, :] = relw_in[...].astype(F32)
    tab_ref[...] = tabf[...].astype(BF)

    vg[...] = jnp.zeros_like(vg)
    tg[...] = jnp.zeros_like(tg)
    fill_tables(z, ids, mask_ref, fwd_ref, back_ref)
    rows_of.inward(held, x, X_SLOTS, XS, "wait")
    x[56:63] = x[pl.ds(NR // 8 + 7 * z, 7)]
    for c in bias:
        c.wait_recv()
    keep_bias.wait()

    g1, b1, pb, g2, b2, fb = (vec_ref[i : i + 1, :] for i in range(6))

    for r0 in range(0, NE, 32):
        rows = slice(r0, r0 + 32)
        c, rstd = stats(x[r0 // 8 : r0 // 8 + 4].astype(F32).reshape(32, 768))
        nrm[rows, :] = (mask_ref[rows, :] * (c * rstd * g1 + b1)).astype(BF)

    ag.across(*BLOCKS[0])
    tick(0)
    ag.own_z(2)
    rows_of.inward(held, x, X_SLOTS, XS, "drain")
    read_cot.wait()
    pad_blocks(held)
    rows_of.inward(held, cot, range(9), CS, "start")
    mix = gn.at[pl.ds(0, NR)]
    mix[...] = jnp.zeros_like(mix)

    def fwd_t(m, _):
        at(m, {n: [partial(ag.partner, 0, ORD[n])] for n in range(4)})
        t = rank(ORD, m)
        proj[...] = dotf(nrm[...], weight(0, t)[:, :576], NN) + sm[t][1:2, :576]
        for h in range(3):
            hh = 3 * t + h
            qs = (proj[:NR, 64 * h : 64 * h + 64].astype(BF) * BF(0.125)).astype(BF)
            rel = dotf(qs, tab_ref[...], NT) * 8.0
            lane = lax.broadcasted_iota(jnp.int32, (NR, 128), 1)
            got = jnp.take_along_axis(rel, fwd_ref[...], axis=1, mode="promise_in_bounds")
            hi = got.astype(BF).astype(F32)
            tail = jnp.where(lane < 92, hi, got - hi)
            tail = jnp.where(lane == 120, 1.0, jnp.where(lane < 120, tail, 0.0)).astype(BF)
            qa = jnp.concatenate([qs, tail[:, 64:]], axis=1)
            qaug[hh] = qa
            for wn in range(3):
                src = slice(wn * WR, wn * WR + WR) if wn < 2 else slice(NR, NE)
                k = proj[src, 192 + 64 * h : 256 + 64 * h].astype(BF)
                kaug[hh, wn] = jnp.concatenate([k, ktail_ref[:, 64:]], axis=1)
                vals[hh, wn] = proj[src, 384 + 64 * h : 448 + 64 * h].astype(BF)
        hook(m, "F", 0)
        for h in range(3):
            hh = 3 * t + h
            for wn in range(3):
                rows = slice(wn * WR, wn * WR + WR) if wn < 2 else slice(2 * WR, NR)
                s = dotf(qaug[hh, rows, :], kaug[hh, wn], NT)
                e = jnp.exp(s - jnp.max(s, axis=-1, keepdims=True))
                p = (e * (1.0 / jnp.sum(e, axis=-1, keepdims=True))).astype(BF)
                probs[hh, rows, :] = p
                att[t, rows, 64 * h : 64 * h + 64] = dotf(p, vals[hh, wn], NN).astype(BF)
            if h < 2:
                hook(m, "F", 1 + h)
        mix[...] += dotf(att[t], weight(0, t)[:, 576:], NT)
        hook(m, "F", 3)
        return 0

    lax.fori_loop(0, 4, fwd_t, 0)
    rows_of.inward(held, cot, range(9), CS, "wait")
    now("L")

    for r0 in range(0, NR, 32):
        rows = slice(r0, r0 + 32)
        xv = x[r0 // 8 : r0 // 8 + 4].astype(F32).reshape(32, 768)
        hv = xv + mask_ref[rows, :] * (mix[rows, :] + pb)
        hid[rows, :] = hv
        c, rstd = stats(hv)
        nr2[rows, :] = (c * rstd * g2 + b2).astype(BF)
        gm = mask_ref[rows, :] * cot[r0 // 8 : r0 // 8 + 4].astype(F32).reshape(32, 768)
        gml[rows, :] = gm.astype(BF)
    mix[...] = jnp.zeros_like(mix)
    gn2[...] = jnp.zeros_like(gn2)

    def mlp_t(m, _):
        at(m, {n: [partial(ag.partner, 1, ORD[n]), partial(ag.partner, 2, ORD[n])] for n in range(4)})
        t = rank(ORD, m)
        for f in range(3):
            cols = slice(256 * f, 256 * f + 256)
            for r0 in range(0, NR, 128):
                rows = slice(r0, r0 + 128)
                up = dotf(nr2[rows, :], weight(1, t)[:, cols], NN) + sm[t][0:1, cols]
                ga = dotf(gml[rows, :], weight(2, t)[:, cols], NN)
                cdf = 0.5 * (1.0 + lax.erf(up * (1.0 / math.sqrt(2.0))))
                pdf = jnp.exp(-0.5 * up * up) * (1.0 / math.sqrt(2.0 * math.pi))
                act[rows, cols] = (up * cdf).astype(BF)
                gup[rows, cols] = (ga * (cdf + up * pdf)).astype(BF)
            hook(m, "M", f)
        vg[0, pl.ds(8 + t, 1), :] = jnp.sum(gup[...].astype(F32), axis=0, keepdims=True)
        mix[...] += dotf(act[...], weight(2, t), NT)
        hook(m, "M", 3)
        gn2[...] += dotf(gup[...], weight(1, t), NT)
        hook(m, "M", 4)
        at(m, {n: [partial(ag.drain, 2, ORD[n])] for n in range(4)})
        w[2, t] = dotf(gml[...], act[...], TN).astype(BF).reshape(2, 2, 2, 96, 768)
        at(m, {n: [partial(rs.start, 2, ORD[n], 1), partial(ag.drain, 1, ORD[n])] for n in range(4)})
        w[1, t] = dotf(nr2[...], gup[...], TN).astype(BF).reshape(2, 2, 2, 96, 768)
        at(m, {n: [partial(rs.start, 1, ORD[n], 1)] for n in range(4)})
        return 0

    lax.fori_loop(0, 4, mlp_t, 0)
    now("N")

    sums = [jnp.zeros((8, 768), F32) for _ in range(4)]

    def fold(v):
        return jnp.sum(v.reshape(4, 8, 768), axis=0)

    gbl = act
    rows_of.inward(held, cot, range(9), CS, "drain")
    ob = cot
    for r0 in range(0, NR, 32):
        rows = slice(r0, r0 + 32)
        mk = mask_ref[rows, :]
        gm = gml[rows, :].astype(F32)
        hv = hid[rows, :]
        ob[r0 // 8 : r0 // 8 + 4] = (mk * (hv + mix[rows, :] + fb)).reshape(4, 8, 768).astype(BF)
        c, rstd = stats(hv)
        xh = c * rstd
        gv = gn2[rows, :]
        e2 = gv * g2
        gh = gm + rstd * (e2 - jnp.mean(e2, axis=-1, keepdims=True) - xh * jnp.mean(e2 * xh, axis=-1, keepdims=True))
        gb = mk * gh
        hid[rows, :] = gh
        gbl[rows, :] = gb.astype(BF)
        for n, v in enumerate((gv * xh, gv, gb, gm)):
            sums[n] = sums[n] + fold(v)
    for n in range(4):
        vg[0, n : n + 1, :] = jnp.sum(sums[n], axis=0, keepdims=True)
    rows_of.outward(ob, out_h, RET0, 22, "start")
    gn[...] = jnp.zeros_like(gn)

    def bwd_t(m, _):
        t = rank(BACK, m)
        at(m, {n: [partial(ag.drain, 0, BACK[n])] for n in range(4)})
        att_w = att[t]
        proj[:NR, :192] = dotf(gbl[...], weight(0, t)[:, 576:], NN)
        dqkv[...] = jnp.zeros_like(dqkv)
        for h in range(3):
            hh = 3 * t + h
            lo = 64 * h
            for wn in range(3):
                rows = slice(wn * WR, wn * WR + WR) if wn < 2 else slice(2 * WR, NR)
                dst = rows if wn < 2 else slice(NR, NE)
                do = proj[rows, lo : lo + 64].astype(BF)
                p = probs[hh, rows, :]
                pf = p.astype(F32)
                dp = dotf(do, vals[hh, wn], NT)
                delta = jnp.sum(pf * dp, axis=-1, keepdims=True)
                ds = (pf * (dp - delta)).astype(BF)
                dq = dotf(ds, kaug[hh, wn], NN)
                qa = qaug[hh, rows, :]
                dqkv[dst, 192 + lo : 256 + lo] = dotf(ds, qa, TN)[:, :64].astype(BF)
                dqkv[dst, 384 + lo : 448 + lo] = dotf(p, do, TN).astype(BF)
                rel = jnp.take_along_axis(dq, back_ref[rows, :], axis=1, mode="promise_in_bounds").astype(BF)
                gq = dq[:, :64] * 0.125 + dotf(rel, tab_ref[...], NN)
                dqkv[rows, lo : lo + 64] = gq.astype(BF)
                tg[0] += dotf(rel, qa, TN)[:64]
            hook(m, "B", h)
        vg[0, pl.ds(12 + t, 1), 0:576] = jnp.sum(dqkv[...].astype(F32), axis=0, keepdims=True)
        gn[...] += dotf(dqkv[...], weight(0, t)[:, :576], NT)
        gw = jnp.concatenate([dotf(nrm[...], dqkv[...], TN).astype(BF), dotf(gbl[...], att_w, TN).astype(BF)], axis=1)
        w[0, t] = gw.reshape(2, 2, 2, 96, 768)
        at(m, {n: [partial(rs.start, 0, BACK[n], 1)] for n in range(4)})
        return 0

    lax.fori_loop(0, 4, bwd_t, 0)

    gs[...] = gn[NR:].reshape(WR // 8, 8, 768).astype(BF)
    sh = [
        links.copy(gs.at[pl.ds(7 * ((z + d) % 4), 7)], gsr.at[d - 1], SH0 + d - 1, links.zdev((z + d) % 4)) for d in (1, 2, 3)
    ]
    for c in sh:
        c.start()
    now("T0")
    for c in sh:
        c.wait_recv()
    now("T1")
    first_norm_back(links, x, mask_ref, vec_ref, gn, hid, gsr, dx, vg.at[0])
    rows_of.outward(dx, dx_h, DX0, 31, "start")
    now("T2")
    small_sums(links, vg, tg, vr, tr, now)
    now("T3")
    vg_out[...] = vg[5]
    tg_out[...] = tg[5]
    for k in (2, 1, 0):
        own[k] = rs.total(k)
    rows_of.outward(ob, out_h, RET0, 22, "wait")
    rows_of.outward(dx, dx_h, DX0, 31, "wait")
    rows_of.outward(ob, out_h, RET0, 22, "drain")
    rows_of.outward(dx, dx_h, DX0, 31, "drain")
    for c in sh + bias:
        c.wait_send()
    for k in range(3):
        for i in (1, 2, 3):
            ag.move(k, "z", i).wait_send()
    rs.drain()


def first_norm_back(links, x, mask_ref, gain_ref, gn_ref, gh_ref, gsr, dx, vg):
    own = gn_ref[pl.ds(pl.multiple_of(NR + 56 * links.z, 8), 56), :]
    for d in range(3):
        own = own + gsr[d].astype(F32).reshape(56, 768)
    quarter = gn_ref[2 * WR : 2 * WR + 56, :] + own
    g1 = gain_ref[0:1, :]
    s_gain = jnp.zeros((8, 768), F32)
    s_bias = jnp.zeros((8, 768), F32)
    for r0, n in [(r, 32) for r in range(0, 2 * WR, 32)] + [(2 * WR, 56)]:
        rows = slice(r0, r0 + n)
        v = x[r0 // 8 : (r0 + n) // 8].astype(F32).reshape(n, 768)
        c = v - jnp.mean(v, axis=-1, keepdims=True)
        rs = lax.rsqrt(jnp.mean(c * c, axis=-1, keepdims=True) + 1e-6)
        xh = c * rs
        gn = mask_ref[rows, :] * (gn_ref[rows, :] if n == 32 else quarter)
        e1 = gn * g1
        gx = gh_ref[rows, :] + rs * (
            e1 - jnp.mean(e1, axis=-1, keepdims=True) - xh * jnp.mean(e1 * xh, axis=-1, keepdims=True)
        )
        dx[r0 // 8 : (r0 + n) // 8] = gx.reshape(n // 8, 8, 768).astype(BF)
        s_gain = s_gain + jnp.sum((gn * xh).reshape(n // 8, 8, 768), axis=0)
        s_bias = s_bias + jnp.sum(gn.reshape(n // 8, 8, 768), axis=0)
    vg[4:5, :] = jnp.sum(s_gain, axis=0, keepdims=True)
    vg[5:6, :] = jnp.sum(s_bias, axis=0, keepdims=True)


def small_sums(links, vg, tg, vr, tr, now):
    l = links
    partners = [l.sib, l.xn, l.yn, l.zdev((l.z // 2) * 2 + 1 - l.z % 2), l.zdev((l.z + 2) % 4)]
    copies = []
    for n, dev in enumerate(partners):
        pair = [l.copy(vg.at[n], vr.at[n], VS0 + 2 * n, dev), l.copy(tg.at[n], tr.at[n], VS0 + 2 * n + 1, dev)]
        for c in pair:
            c.start()
        now(f"S{n}")
        for c in pair:
            c.wait_recv()
        vg[n + 1] = vg[n] + vr[n]
        tg[n + 1] = tg[n] + tr[n]
        copies += pair
    for c in copies:
        c.wait_send()


def final_kernel(
    own, out_h, dx_h, vg, tg, out, dx, g_qkv, g_proj, g_fc1, g_fc2, v0, v1, v2, v3, v4, v5, fc1b_out, qvb_out, relh_out, relw_out,
    rows,
):
    for m in range(3):
        for b in range(3):
            n = BT * (3 * m + b)
            dx[n : n + BT, 0, :] = dx_h[3 * m + b].astype(F32).reshape(BP, 768)[:BT]
            rows[BT * b : BT * b + BT, :] = out_h[3 * m + b].astype(F32).reshape(BP, 768)[:BT]
        out[m] = rows[...].astype(BF)
    for n, ref in enumerate((v0, v1, v2, v3, v4, v5)):
        for c in range(6):
            ref[c : c + 1, :] = vg[n : n + 1, 128 * c : 128 * c + 128]
    for t in range(4):
        for c in range(6):
            fc1b_out[6 * t + c : 6 * t + c + 1, :] = vg[8 + t : 9 + t, 128 * c : 128 * c + 128]
        qvb_out[0:1, 192 * t : 192 * t + 192] = vg[12 + t : 13 + t, 0:192]
        qvb_out[1:2, 192 * t : 192 * t + 192] = vg[12 + t : 13 + t, 384:576]
    relh_out[...] = tg[0:27, :64] * 8.0
    relw_out[...] = tg[32:59, :64] * 8.0
    for t in range(3):
        g_qkv[t] = own[0, :, 192 * t : 192 * t + 192]
    g_proj[...] = own[0, :, 576:].T
    g_fc1[...] = own[1]
    g_fc2[...] = own[2]


def final_call(*arrays):
    shp = jax.ShapeDtypeStruct
    vm = pl.BlockSpec(memory_space=pltpu.VMEM)
    return pl.pallas_call(
        final_kernel,
        out_shape=(
            shp((3, 147, 768), BF), shp((441, 1, 768), F32), shp((3, 96, 192), F32), shp((192, 96), F32), shp((96, 768), F32),
            shp((96, 768), F32), *[shp((6, 128), F32)] * 6, shp((24, 128), F32), shp((2, 768), F32), shp((27, 64), F32),
            shp((27, 64), F32),
        ),
        in_specs=[vm] * 5,
        out_specs=(vm,) * 16,
        scratch_shapes=[pltpu.VMEM((147, 768), F32)],
    )(*arrays)


def whole_call(*arrays):
    shp = jax.ShapeDtypeStruct
    vm = pl.BlockSpec(memory_space=pltpu.VMEM)
    hbm = pl.BlockSpec(memory_space=pl.ANY)
    V = pltpu.VMEM
    dma = pltpu.SemaphoreType.DMA
    return pl.pallas_call(
        whole_kernel,
        out_shape=(
            shp((3, 96, 768), F32), shp((9, 7, 8, 768), BF), shp((9, 7, 8, 768), BF), shp((16, 768), F32), shp((64, 128), F32),
        ),
        in_specs=[hbm, hbm, pl.BlockSpec(memory_space=pltpu.SMEM)] + [hbm] * 15,
        out_specs=(vm, hbm, hbm, vm, vm),
        scratch_shapes=[
            V((96, 768), BF), V((8, 768), F32), V((NE, 1), F32), V((NR, 128), jnp.int32), V((NR, 128), jnp.int32),
            V((8, 768), F32), V((128, 64), BF), V((128, 64), F32),
            V((3, 4, 2, 2, 2, 96, 768), BF), V((12, 2, 2, 96, 768), BF), V((12, 2, 2, 48, 768), BF), V((12, 2, 48, 768), BF),
            V((3, 3, 96, 768), BF), V((NE // 8, 8, 768), BF), V((NR // 8, 8, 768), BF), V((4, 8, 768), F32),
            V((3, 147, 768), BF), V((NR // 8, 8, 768), BF), V((NE, 768), F32), V((NR, 768), F32), V((NR, 768), F32),
            V((WR // 8, 8, 768), BF), V((3, 7, 8, 768), BF), V((6, 16, 768), F32), V((6, 64, 128), F32),
            V((5, 16, 768), F32), V((5, 64, 128), F32),
            V((NE, 768), BF), V((NE, 576), F32), V((HEADS, NR, 128), BF), V((HEADS, 3, WR, 128), BF), V((HEADS, 3, WR, 64), BF),
            V((HEADS, NR, WR), BF), V((4, NR, 192), BF), V((NR, 768), BF), V((NR, 768), BF), V((NR, 768), BF), V((NR, 768), BF),
            V((NE, 576), BF), dma((SEMS,)), dma((SEMS,)), dma((48,)),
            *[V(a.shape, a.dtype) for a in arrays[3:]], dma((15,)),
        ],
        compiler_params=pltpu.CompilerParams(collective_id=0, has_side_effects=True, vmem_limit_bytes=67043328),
    )(*arrays)


def plain_gather(xh, coth, shard):
    mine = lax.dynamic_index_in_dim(jnp.asarray(block_table()), lax.axis_index("tensor"), 0, keepdims=False)

    def spread(held, count):
        blocks = lax.all_gather(held.reshape(3, 3, 7, 8, 768), "tensor", axis=1).reshape(36, 7, 8, 768)
        got = jnp.take(blocks, mine[:count], axis=0).reshape(-1, 8, 768)
        return jnp.concatenate([got[:63], jnp.zeros((1, 8, 768), BF), got[63:]], axis=0)

    whole = lax.all_gather(lax.all_gather(shard, ("dp", "win"), axis=1, tiled=True), "tensor", axis=1)
    return spread(xh, 13), spread(coth, 9), whole


def plain_scatter(grads, x, mask, vec, gn, gh, vg, tg, out):
    shared = lax.psum_scatter(gn[NR:], "tensor", scatter_dimension=0, tiled=True)
    gn = mask * (gn[:NR] + jnp.pad(shared, ((2 * WR, QR - BP), (0, 0))))
    xf = x[: NR // 8].reshape(NR, 768).astype(F32)
    cen = xf - jnp.mean(xf, axis=-1, keepdims=True)
    rs = lax.rsqrt(jnp.mean(cen * cen, axis=-1, keepdims=True) + 1e-6)
    xh = cen * rs
    e1 = gn * vec[0]
    gx = gh + rs * (e1 - jnp.mean(e1, axis=-1, keepdims=True) - xh * jnp.mean(e1 * xh, axis=-1, keepdims=True))
    vg = vg.at[4].set(jnp.sum(gn * xh, axis=0)).at[5].set(jnp.sum(gn, axis=0))
    back_to = lax.dynamic_index_in_dim(jnp.asarray(home_table()), lax.axis_index("tensor"), 0, keepdims=False)

    def bring(rows):
        blocks = lax.all_gather(rows[:63].reshape(9, 7, 8, 768), "tensor", axis=0, tiled=True)
        return jnp.take(blocks, back_to, axis=0)

    own = lax.psum_scatter(grads.reshape(3, 4, 768, 768), "tensor", scatter_dimension=1, tiled=False)
    own = lax.psum_scatter(own, ("dp", "win"), scatter_dimension=1, tiled=True).astype(F32)
    vg, tg = lax.psum((vg, tg), ("dp", "win", "tensor"))
    return own, bring(out), bring(gx.astype(BF).reshape(NR // 8, 8, 768)), vg, tg


def per_device(
    links, tokens, window_ids, norm1_gain, norm1_bias, qkv_weight, qv_bias, rel_height, rel_width, proj_weight, proj_bias,
    norm2_gain, norm2_bias, fc1_weight, fc1_bias, fc2_weight, fc2_bias, out_grad,
):
    rank = lax.axis_index("tensor")

    def home_blocks(rows):
        return jnp.pad(rows.reshape(9, BT, 768), ((0, 0), (0, BP - BT), (0, 0))).reshape(9, 7, 8, 768)

    if links:
        vectors = (norm1_gain, norm1_bias, proj_bias, norm2_gain, norm2_bias, fc2_bias, fc1_bias)
        done = whole_call(
            tokens[0], out_grad[0], jnp.transpose(window_ids, (1, 0, 2)), jnp.transpose(qkv_weight, (1, 0, 2)), proj_weight,
            fc1_weight, fc2_weight.T, *(v.reshape(6, 128) for v in vectors), qv_bias, rel_height, rel_width,
            jnp.asarray(key_tail(), BF),
        )
        out, dx, g_qkv, g_proj, g_fc1, g_fc2, v0, v1, v2, v3, v4, v5, fc1b, qvb, relh, relw = final_call(*done)
        v0, v1, v2, v3, v4, v5 = (v.reshape(768) for v in (v0, v1, v2, v3, v4, v5))
        return (
            out[None], dx.reshape(1, 3, 147, 768), v4, v5, jnp.transpose(g_qkv, (1, 0, 2)), qvb, relh, relw, g_proj, v2, v0, v1, g_fc1,
            fc1b.reshape(-1), g_fc2.T, v3,
        )

    shard = jnp.stack(
        [
            jnp.concatenate([qkv_weight.reshape(-1, 576), proj_weight.T], axis=1),
            fc1_weight,
            fc2_weight.T,
        ]
    )
    xh, coth = home_blocks(tokens), home_blocks(out_grad)

    wi, wj, wv = token_positions()
    wi, wj, wv = jnp.asarray(wi, jnp.int32), jnp.asarray(wj, jnp.int32), jnp.asarray(wv)
    qi = jnp.pad(lax.dynamic_slice_in_dim(wi, rank * BP, BP), (0, QR - BP))
    qj = jnp.pad(lax.dynamic_slice_in_dim(wj, rank * BP, BP), (0, QR - BP))
    qv = jnp.pad(lax.dynamic_slice_in_dim(wv, rank * BP, BP), (0, QR - BP))
    ids = window_ids.reshape(9)
    slots = jnp.asarray([[m * 3 + s for m, s in WINDOWS_OF[dev]] + [4, 4] for dev in range(4)], jnp.int32)
    wid = jnp.take(ids, lax.dynamic_index_in_dim(slots, rank, 0, keepdims=False), axis=0)

    across = (GRID + WS - 1) // WS

    def valid(w, i, j, ok):
        return ok & (w < across * across) & ((w // across) * WS + i < GRID) & ((w % across) * WS + j < GRID)

    mask = jnp.concatenate(
        [valid(wid[0], wi, wj, wv), valid(wid[1], wi, wj, wv), valid(wid[2], qi, qj, qv), valid(wid[3], wi, wj, wv)]
    ).astype(F32)[:, None]
    ii = jnp.concatenate([wi, wi, qi])
    jj = jnp.concatenate([wj, wj, qj])
    fwd, back = pick_lanes(ii, jj)

    small = jnp.zeros((8, 768), F32).at[0].set(fc1_bias.astype(F32))
    small = small.at[1, :192].set(qv_bias[0].astype(F32)).at[1, 384:576].set(qv_bias[1].astype(F32))
    vec = jnp.stack(
        [norm1_gain, norm1_bias, proj_bias, norm2_gain, norm2_bias, fc2_bias, fc2_bias, fc2_bias]
    ).astype(F32)
    tab = jnp.zeros((128, 64), BF).at[0:27].set(rel_height).at[32:59].set(rel_width)
    tabt = (tab * BF(8)).T
    ktail = jnp.asarray(key_tail(), BF)

    x, cot, whole = plain_gather(xh, coth, shard)
    small = lax.all_gather(small, "tensor", axis=0)
    out, gn, gh, grads, vg, tg = compute(
        x, cot, mask, whole.reshape(3, 4, 768, 768), vec, small[:, 1:2, :576], small[:, 0:1], ktail, fwd, back, tab, tabt
    )
    own, out, dx, vg, tg = plain_scatter(grads, x, mask[:NR], vec, gn, gh, vg, tg, out)

    def tokens_of(blocks):
        return blocks.reshape(9, BP, 768)[:, :BT].reshape(tokens.shape)

    output = tokens_of(out)
    grad_tokens = tokens_of(dx).astype(F32)
    g_qkv = own[0, :, :576].reshape(qkv_weight.shape)
    g_proj = own[0, :, 576:].T
    g_fc1 = own[1]
    g_fc2 = own[2].T
    g_qv = jnp.stack([vg[12:16, :192].reshape(-1), vg[12:16, 384:576].reshape(-1)])
    return (
        output, grad_tokens, vg[4], vg[5], g_qkv, g_qv, tg[0:27, :64] * 8.0, tg[32:59, :64] * 8.0, g_proj,
        vg[2], vg[0], vg[1], g_fc1, vg[8:12].reshape(-1), g_fc2, vg[3],
    )


def solution(mesh):
    in_specs = (
        P("dp", "win", "tensor", None), P("dp", "win", None), P(), P(), P(("dp", "win"), None, "tensor"),
        P(None, "tensor"), P(), P(), P("tensor", ("dp", "win")), P(), P(), P(), P(("dp", "win"), "tensor"), P("tensor"),
        P("tensor", ("dp", "win")), P(), P("dp", "win", "tensor", None),
    )
    out_specs = (
        P("dp", "win", "tensor", None), P("dp", "win", "tensor", None), P(), P(), P(("dp", "win"), None, "tensor"), P(),
        P(), P(), P("tensor", ("dp", "win")), P(), P(), P(), P(("dp", "win"), "tensor"), P(),
        P("tensor", ("dp", "win")), P(),
    )
    links = dict(mesh.shape) == {"dp": 2, "win": 4, "tensor": 4}
    return jax.shard_map(partial(per_device, links), mesh=mesh, in_specs=in_specs, out_specs=out_specs, check_vma=False)
```

```python
import math
from functools import partial

import jax
import jax.numpy as jnp
import numpy as np
from jax import lax
from jax.experimental import pallas as pl
from jax.experimental.pallas import tpu as pltpu
from jax.sharding import PartitionSpec as P

HEADS = 12
HD = 64
WS = 14
GRID = 64
WT = 196
BT = 49
BP = 56
WR = 4 * BP
QR = 64
NR = 2 * WR + QR
NE = NR + WR
BF = jnp.bfloat16
F32 = jnp.float32

WINDOWS_OF = (((0, 0), (1, 0)), ((2, 0), (0, 1)), ((2, 2), (2, 1)), ((0, 2), (1, 2)))
SHARED = (1, 1)


def block_table():
    rows = []
    for dev in range(4):
        row = []
        for m, s in WINDOWS_OF[dev]:
            row += [m * 12 + 4 * s + j for j in range(4)]
        row.append(SHARED[0] * 12 + 4 * SHARED[1] + dev)
        row += [SHARED[0] * 12 + 4 * SHARED[1] + j for j in range(4)]
        rows.append(row)
    return np.array(rows, np.int32)


def home_table():
    table = block_table()
    place = {}
    for dev in range(4):
        for slot in range(9):
            place[int(table[dev, slot])] = dev * 9 + slot
    return np.array([[place[m * 12 + 3 * dev + b] for m in range(3) for b in range(3)] for dev in range(4)], np.int32)


def token_positions():
    row = np.arange(WR)
    off = row % BP
    token = (row // BP) * BT + np.minimum(off, BT - 1)
    return token // WS, token % WS, off < BT


def key_tail():
    i, j, valid = token_positions()
    tail = np.zeros((WR, 128), np.float32)
    for m in range(WS):
        tail[:, 64 + m] = i == m
        tail[:, 78 + m] = j == m
    tail[:, 92:120] = tail[:, 64:92]
    tail[:, :120] *= valid[:, None]
    tail[:, 120] = np.where(valid, 0.0, -1e30)
    return tail


def pick_lanes(i, j):
    lane = np.arange(128)[None, :]
    m = np.clip((lane - 64) % 28, 0, 27)
    is_w = m >= 14
    fwd = jnp.where(is_w, 32 + j[:, None] - (m - 14) + 13, i[:, None] - m + 13)
    fwd = jnp.where((lane >= 64) & (lane < 120), fwd, 0)
    d = lane % 32
    pos = jnp.where(lane >= 32, j[:, None], i[:, None]) + 13 - d
    ok = (pos >= 0) & (pos < WS) & (lane < 64) & (d < 27)
    back = jnp.where(ok, pos + jnp.where(lane >= 32, 78, 64), 127)
    return fwd.astype(jnp.int32), back.astype(jnp.int32)


def dotf(a, b, dims):
    return lax.dot_general(a, b, (dims, ((), ())), preferred_element_type=F32)


NN = ((1,), (0,))
NT = ((1,), (1,))
TN = ((0,), (0,))


def compute_kernel(
    x_ref, cot_ref, mask_ref, w_ref, vec_ref, qkvb_ref, fc1b_ref, ktail_ref, fwd_ref, back_ref, tab_ref, tabt_ref,
    out_ref, gn_ref, gh_ref, g_ref, vg_ref, tg_ref,
    nrm, proj, qaug, kaug, vals, probs, att, hid, nr2, mix, gn2, act, gup, gml, gbl, dqkv,
):
    g1, b1, pb, g2, b2, fb = (vec_ref[i : i + 1, :] for i in range(6))

    def stats(v):
        mu = jnp.mean(v, axis=-1, keepdims=True)
        c = v - mu
        var = jnp.mean(c * c, axis=-1, keepdims=True)
        return c, lax.rsqrt(var + 1e-6)

    vg_ref[...] = jnp.zeros_like(vg_ref)

    for r0 in range(0, NE, 32):
        rows = slice(r0, r0 + 32)
        c, rs = stats(x_ref[r0 // 8 : r0 // 8 + 4].astype(F32).reshape(32, 768))
        nrm[rows, :] = (mask_ref[rows, :] * (c * rs * g1 + b1)).astype(BF)

    def fwd_t(t, _):
        proj[...] = dotf(nrm[...], w_ref[0, t][:, :576], NN) + qkvb_ref[t]
        for h in range(3):
            hh = 3 * t + h
            qs = (proj[:NR, 64 * h : 64 * h + 64].astype(BF) * BF(0.125)).astype(BF)
            rel = dotf(qs, tabt_ref[...], NN)
            lane = lax.broadcasted_iota(jnp.int32, (NR, 128), 1)
            got = jnp.take_along_axis(rel, fwd_ref[...], axis=1, mode="promise_in_bounds")
            hi = got.astype(BF).astype(F32)
            tail = jnp.where(lane < 92, hi, got - hi)
            tail = jnp.where(lane == 120, 1.0, jnp.where(lane < 120, tail, 0.0)).astype(BF)
            qa = jnp.concatenate([qs, tail[:, 64:]], axis=1)
            qaug[hh] = qa
            for w in range(3):
                src = slice(w * WR, w * WR + WR) if w < 2 else slice(NR, NE)
                k = proj[src, 192 + 64 * h : 256 + 64 * h].astype(BF)
                kaug[hh, w] = jnp.concatenate([k, ktail_ref[:, 64:]], axis=1)
                vals[hh, w] = proj[src, 384 + 64 * h : 448 + 64 * h].astype(BF)
        return 0

    lax.fori_loop(0, 4, fwd_t, 0)
    mix[...] = jnp.zeros_like(mix)

    def att_t(t, _):
        for h in range(3):
            hh = 3 * t + h
            for w in range(3):
                rows = slice(w * WR, w * WR + WR) if w < 2 else slice(2 * WR, NR)
                s = dotf(qaug[hh, rows, :], kaug[hh, w], NT)
                e = jnp.exp(s - jnp.max(s, axis=-1, keepdims=True))
                p = (e * (1.0 / jnp.sum(e, axis=-1, keepdims=True))).astype(BF)
                probs[hh, rows, :] = p
                att[t, rows, 64 * h : 64 * h + 64] = dotf(p, vals[hh, w], NN).astype(BF)
        mix[...] += dotf(att[t], w_ref[0, t][:, 576:], NT)
        return 0

    lax.fori_loop(0, 4, att_t, 0)

    for r0 in range(0, NR, 32):
        rows = slice(r0, r0 + 32)
        x = x_ref[r0 // 8 : r0 // 8 + 4].astype(F32).reshape(32, 768)
        hv = x + mask_ref[rows, :] * (mix[rows, :] + pb)
        hid[rows, :] = hv
        c, rs = stats(hv)
        nr2[rows, :] = (c * rs * g2 + b2).astype(BF)
        gm = mask_ref[rows, :] * cot_ref[r0 // 8 : r0 // 8 + 4].astype(F32).reshape(32, 768)
        gml[rows, :] = gm.astype(BF)
    mix[...] = jnp.zeros_like(mix)
    gn2[...] = jnp.zeros_like(gn2)

    def mlp_t(t, _):
        for f in range(3):
            cols = slice(256 * f, 256 * f + 256)
            for r0 in range(0, NR, 128):
                rows = slice(r0, r0 + 128)
                up = dotf(nr2[rows, :], w_ref[1, t][:, cols], NN) + fc1b_ref[t][:, cols]
                ga = dotf(gml[rows, :], w_ref[2, t][:, cols], NN)
                cdf = 0.5 * (1.0 + lax.erf(up * (1.0 / math.sqrt(2.0))))
                pdf = jnp.exp(-0.5 * up * up) * (1.0 / math.sqrt(2.0 * math.pi))
                act[rows, cols] = (up * cdf).astype(BF)
                gup[rows, cols] = (ga * (cdf + up * pdf)).astype(BF)
        vg_ref[pl.ds(8 + t, 1), :] = jnp.sum(gup[...].astype(F32), axis=0, keepdims=True)
        mix[...] += dotf(act[...], w_ref[2, t], NT)
        gn2[...] += dotf(gup[...], w_ref[1, t], NT)
        g_ref[2, t] = dotf(gml[...], act[...], TN).astype(BF)
        g_ref[1, t] = dotf(nr2[...], gup[...], TN).astype(BF)
        return 0

    lax.fori_loop(0, 4, mlp_t, 0)

    sums = [jnp.zeros((8, 768), F32) for _ in range(4)]

    def fold(v):
        return jnp.sum(v.reshape(4, 8, 768), axis=0)

    for r0 in range(0, NR, 32):
        rows = slice(r0, r0 + 32)
        mk = mask_ref[rows, :]
        gm = mk * cot_ref[r0 // 8 : r0 // 8 + 4].astype(F32).reshape(32, 768)
        hv = hid[rows, :]
        out_ref[r0 // 8 : r0 // 8 + 4] = (mk * (hv + mix[rows, :] + fb)).reshape(4, 8, 768).astype(BF)
        c, rs = stats(hv)
        xh = c * rs
        gn = gn2[rows, :]
        e2 = gn * g2
        gh = gm + rs * (e2 - jnp.mean(e2, axis=-1, keepdims=True) - xh * jnp.mean(e2 * xh, axis=-1, keepdims=True))
        gb = mk * gh
        gh_ref[rows, :] = gh
        gbl[rows, :] = gb.astype(BF)
        for n, v in enumerate((gn * xh, gn, gb, gm)):
            sums[n] = sums[n] + fold(v)
    for n in range(4):
        vg_ref[n : n + 1, :] = jnp.sum(sums[n], axis=0, keepdims=True)
    tg_ref[...] = jnp.zeros_like(tg_ref)
    gn_ref[...] = jnp.zeros_like(gn_ref)

    def bwd_t(t, _):
        att_w = att[t]
        g_ref[0, t, :, 576:] = dotf(gbl[...], att_w, TN).astype(BF)
        proj[:NR, :192] = dotf(gbl[...], w_ref[0, t][:, 576:], NN)
        dqkv[...] = jnp.zeros_like(dqkv)
        for h in range(3):
            hh = 3 * t + h
            lo = 64 * h
            for w in range(3):
                rows = slice(w * WR, w * WR + WR) if w < 2 else slice(2 * WR, NR)
                dst = rows if w < 2 else slice(NR, NE)
                do = proj[rows, lo : lo + 64].astype(BF)
                p = probs[hh, rows, :]
                pf = p.astype(F32)
                dp = dotf(do, vals[hh, w], NT)
                delta = jnp.sum(pf * dp, axis=-1, keepdims=True)
                ds = (pf * (dp - delta)).astype(BF)
                dq = dotf(ds, kaug[hh, w], NN)
                qa = qaug[hh, rows, :]
                dqkv[dst, 192 + lo : 256 + lo] = dotf(ds, qa, TN)[:, :64].astype(BF)
                dqkv[dst, 384 + lo : 448 + lo] = dotf(p, do, TN).astype(BF)
                rel = jnp.take_along_axis(dq, back_ref[rows, :], axis=1, mode="promise_in_bounds").astype(BF)
                gq = dq[:, :64] * 0.125 + dotf(rel, tab_ref[...], NN)
                dqkv[rows, lo : lo + 64] = gq.astype(BF)
                tg_ref[...] += dotf(rel, qa, TN)[:64]
        vg_ref[pl.ds(12 + t, 1), 0:576] = jnp.sum(dqkv[...].astype(F32), axis=0, keepdims=True)
        g_ref[0, t, :, :576] = dotf(nrm[...], dqkv[...], TN).astype(BF)
        gn_ref[...] += dotf(dqkv[...], w_ref[0, t][:, :576], NT)
        return 0

    lax.fori_loop(0, 4, bwd_t, 0)


def compute(x, cot, mask, w, vec, qkvb, fc1b, ktail, fwd, back, tab, tabt):
    shp = jax.ShapeDtypeStruct
    vm = pl.BlockSpec(memory_space=pltpu.VMEM)
    return pl.pallas_call(
        compute_kernel,
        out_shape=(
            shp((NR // 8, 8, 768), BF), shp((NE, 768), F32), shp((NR, 768), F32), shp((3, 4, 768, 768), BF),
            shp((16, 768), F32), shp((64, 128), F32),
        ),
        in_specs=[vm] * 12,
        out_specs=(vm,) * 6,
        scratch_shapes=[
            pltpu.VMEM((NE, 768), BF), pltpu.VMEM((NE, 576), F32), pltpu.VMEM((HEADS, NR, 128), BF),
            pltpu.VMEM((HEADS, 3, WR, 128), BF), pltpu.VMEM((HEADS, 3, WR, 64), BF), pltpu.VMEM((HEADS, NR, WR), BF),
            pltpu.VMEM((4, NR, 192), BF), pltpu.VMEM((NR, 768), F32), pltpu.VMEM((NR, 768), BF),
            pltpu.VMEM((NR, 768), F32), pltpu.VMEM((NR, 768), F32), pltpu.VMEM((NR, 768), BF), pltpu.VMEM((NR, 768), BF),
            pltpu.VMEM((NR, 768), BF), pltpu.VMEM((NR, 768), BF), pltpu.VMEM((NE, 576), BF),
        ],
        compiler_params=pltpu.CompilerParams(vmem_limit_bytes=67043328),
    )(x, cot, mask, w, vec, qkvb, fc1b, ktail, fwd, back, tab, tabt)


MESH = pl.DeviceIdType.MESH


class Links:
    def __init__(self, send, recv):
        self.send, self.recv = send, recv
        self.x = lax.axis_index("dp")
        win = lax.axis_index("win")
        self.y, self.c = win // 2, win % 2
        self.z = lax.axis_index("tensor")
        self.xn = (1 - self.x, win, self.z)
        self.yn = (self.x, (1 - self.y) * 2 + self.c, self.z)
        self.sib = (self.x, self.y * 2 + 1 - self.c, self.z)
        self.win = win

    def zdev(self, z):
        return (self.x, self.win, z)

    def barrier(self):
        sem = pltpu.get_barrier_semaphore()
        others = [self.xn, self.yn, self.sib] + [self.zdev((self.z + d) % 4) for d in (1, 2, 3)]
        for dev in others:
            pl.semaphore_signal(sem, inc=1, device_id=dev, device_id_type=MESH)
        pl.semaphore_wait(sem, len(others))

    def copy(self, src, dst, n, dev):
        return pltpu.make_async_remote_copy(
            src_ref=src, dst_ref=dst, send_sem=self.send.at[n], recv_sem=self.recv.at[n], device_id=dev,
            device_id_type=MESH,
        )


AG_SEMS = 3 * 39


class Gather:
    def __init__(self, links, shards, w, local, base):
        self.l, self.shards, self.w, self.local, self.base = links, shards, w, local, base

    def sem(self, k, kind, i):
        start = {"z": 0, "x": 3, "y": 7, "hx": 11, "hy": 15, "so": 19, "sx": 23, "sy": 27, "sa": 31, "sb": 35}[kind]
        return self.base + k * 39 + start + i

    def rank(self, i):
        return (self.l.z + 4 - i) % 4

    def piece(self, k, i, px, py, c, half=None):
        ref = self.w.at[k, self.rank(i), px, py, c]
        return ref if half is None else ref.at[pl.ds(48 * half, 48)]

    def move(self, k, kind, i):
        l = self.l
        if kind == "z":
            src = self.shards[k]
            return l.copy(src, self.piece(k, 0, l.x, l.y, l.c), self.sem(k, kind, i - 1), l.zdev((l.z + i) % 4))
        px, py, half, dev = {
            "x": (l.x, l.y, None, l.xn), "y": (l.x, l.y, None, l.yn),
            "hx": (l.x, 1 - l.y, 1, l.xn), "hy": (1 - l.x, l.y, 0, l.yn),
            "so": (l.x, l.y, None, l.sib), "sx": (1 - l.x, l.y, None, l.sib), "sy": (l.x, 1 - l.y, None, l.sib),
            "sa": (1 - l.x, 1 - l.y, 0, l.sib), "sb": (1 - l.x, 1 - l.y, 1, l.sib),
        }[kind]
        dst = self.piece(k, i, px, py, l.c, half)
        own = kind in ("x", "y", "so") and i == 0
        return l.copy(self.shards[k] if own else dst, dst, self.sem(k, kind, i), dev)

    def start(self, k, kind, i):
        self.move(k, kind, i).start()

    def arrived(self, k, kind, i):
        self.move(k, kind, i).wait_recv()

    def keep(self, k):
        l = self.l
        return pltpu.make_async_copy(self.shards[k], self.piece(k, 0, l.x, l.y, l.c), self.local.at[k])

    def own_z(self, k):
        for i in (1, 3, 2):
            self.start(k, "z", i)

    def along(self, k, i):
        if i:
            self.arrived(k, "z", i)
        else:
            self.keep(k).start()
        for kind in ("x", "y", "so"):
            self.start(k, kind, i)

    def across(self, k, i):
        self.arrived(k, "x", i)
        self.start(k, "hy", i)
        self.start(k, "sx", i)
        self.arrived(k, "y", i)
        self.start(k, "hx", i)
        self.start(k, "sy", i)

    def corner(self, k, i):
        self.arrived(k, "hy", i)
        self.start(k, "sa", i)
        self.arrived(k, "hx", i)
        self.start(k, "sb", i)

    def partner(self, k, i):
        for kind in ("so", "sx", "sy", "sa", "sb"):
            self.arrived(k, kind, i)
        if not i:
            self.keep(k).wait()

    def drain(self, k, i):
        for kind in ("x", "y", "hx", "hy", "so", "sx", "sy", "sa", "sb"):
            self.move(k, kind, i).wait_send()


RS_SEMS = 12 * 6


class Scatter:
    def __init__(self, links, w, r1, r2, r3, r4, base):
        self.l, self.w, self.r1, self.r2, self.r3, self.r4, self.base = links, w, r1, r2, r3, r4, base

    def g(self, k, i):
        return self.w.at[k, (self.l.z + 4 - i) % 4]

    def moves(self, k, i, stage):
        l, n = self.l, 4 * k + i
        s = self.base + 6 * n
        g = self.g(k, i)
        if stage == 1:
            return [l.copy(g.at[:, :, 1 - l.c], self.r1.at[n], s, l.sib)]
        if stage == 2:
            return [
                l.copy(g.at[:, 1 - l.y, l.c, 0:48], self.r2.at[n, 0], s + 1, l.yn),
                l.copy(g.at[1 - l.x, :, l.c, 48:96], self.r2.at[n, 1], s + 2, l.xn),
            ]
        if stage == 3:
            return [
                l.copy(g.at[1 - l.x, l.y, l.c, 0:48], self.r3.at[n, 0], s + 3, l.xn),
                l.copy(g.at[l.x, 1 - l.y, l.c, 48:96], self.r3.at[n, 1], s + 4, l.yn),
            ]
        return [l.copy(g.at[l.x, l.y, l.c], self.r4.at[k, i - 1], s + 5, l.zdev((l.z + 4 - i) % 4))] if i else []

    def start(self, k, i, stage):
        for m in self.moves(k, i, stage):
            m.start()

    def wait(self, k, i, stage):
        for m in self.moves(k, i, stage):
            m.wait_recv()

    def step(self, k, i, stage):
        l, g, n = self.l, self.g(k, i), 4 * k + i
        self.wait(k, i, stage - 1)
        if stage == 2:
            for a in range(2):
                for b in range(2):
                    ref = g.at[a, b, l.c]
                    ref[...] = ref[...] + self.r1[n, a, b]
        elif stage == 3:
            for a in range(2):
                ref = g.at[a, l.y, l.c, 0:48]
                ref[...] = ref[...] + self.r2[n, 0, a]
                ref = g.at[l.x, a, l.c, 48:96]
                ref[...] = ref[...] + self.r2[n, 1, a]
        else:
            for h in range(2):
                ref = g.at[l.x, l.y, l.c, pl.ds(48 * h, 48)]
                ref[...] = ref[...] + self.r3[n, h]
        self.start(k, i, stage)

    def total(self, k):
        l = self.l
        fin = self.g(k, 0)[l.x, l.y, l.c].astype(F32)
        for i in (1, 2, 3):
            self.wait(k, i, 4)
            fin = fin + self.r4[k, i - 1].astype(F32)
        return fin

    def drain(self):
        for k in range(3):
            for i in range(4):
                for stage in (1, 2, 3, 4):
                    for m in self.moves(k, i, stage):
                        m.wait_send()


class Rows:
    TABLE = block_table()

    def __init__(self, links, local):
        self.l, self.local = links, local

    @staticmethod
    def home(block):
        m, b = divmod(int(block), 12)
        return b // 3, m * 3 + b % 3

    @staticmethod
    def unit(slot):
        return 7 * slot if slot < 9 else NR // 8 + 7 * (slot - 9)

    def inward(self, held, rows, slots, base, do):
        l = self.l
        for me in range(4):

            @pl.when(l.z == me)
            def _():
                sent = 0
                for slot in slots:
                    for step in range(4):
                        dev = (me + step) % 4
                        owner, idx = self.home(self.TABLE[dev, slot])
                        if owner != me:
                            continue
                        dst = rows.at[pl.ds(self.unit(slot), 7)]
                        if dev == me:
                            if do != "drain":
                                c = pltpu.make_async_copy(held.at[idx], dst, self.local.at[base + slot])
                                c.start() if do == "start" else c.wait()
                            continue
                        sent += 1
                        if do == "wait":
                            continue
                        c = pltpu.make_async_remote_copy(
                            src_ref=held.at[idx], dst_ref=dst, send_sem=l.send.at[base + sent - 1],
                            recv_sem=l.recv.at[base + slot], device_id=l.zdev(dev), device_id_type=MESH,
                        )
                        c.start() if do == "start" else c.wait_send()
                    owner, idx = self.home(self.TABLE[me, slot])
                    if do == "wait" and owner != me:
                        pltpu.make_async_remote_copy(
                            src_ref=held.at[0], dst_ref=rows.at[pl.ds(self.unit(slot), 7)], send_sem=l.send.at[base],
                            recv_sem=l.recv.at[base + slot], device_id=l.zdev(owner), device_id_type=MESH,
                        ).wait_recv()

    def outward(self, rows, held, base, mine, do):
        l = self.l
        for me in range(4):

            @pl.when(l.z == me)
            def _():
                for slot in range(9):
                    owner, idx = self.home(self.TABLE[me, slot])
                    src = rows.at[pl.ds(7 * slot, 7)]
                    if owner == me:
                        if do != "drain":
                            c = pltpu.make_async_copy(src, held.at[idx], self.local.at[mine + slot])
                            c.start() if do == "start" else c.wait()
                    elif do != "wait":
                        c = pltpu.make_async_remote_copy(
                            src_ref=src, dst_ref=held.at[idx], send_sem=l.send.at[base + slot],
                            recv_sem=l.recv.at[base + idx], device_id=l.zdev(owner), device_id_type=MESH,
                        )
                        c.start() if do == "start" else c.wait_send()
                for dev in range(4):
                    for slot in range(9):
                        owner, idx = self.home(self.TABLE[dev, slot])
                        if do == "wait" and owner == me and dev != me:
                            pltpu.make_async_remote_copy(
                                src_ref=rows.at[pl.ds(0, 7)], dst_ref=held.at[idx], send_sem=l.send.at[base],
                                recv_sem=l.recv.at[base + idx], device_id=l.zdev(dev), device_id_type=MESH,
                            ).wait_recv()


XS, CS, BS = 0, 13, 22
AG0 = BS + 3
RET0 = AG0 + AG_SEMS
DX0 = RET0 + 9
SH0 = DX0 + 9
VS0 = SH0 + 3
RS0 = VS0 + 10
SEMS = RS0 + RS_SEMS
X_SLOTS = (0, 1, 2, 3, 4, 5, 6, 7, 9, 10, 11, 12)

ORD = (0, 1, 3, 2)
BACK = (2, 1, 3, 0)
BLOCKS = ((0, 0), (1, 0), (0, 1), (0, 3), (0, 2), (2, 0), (1, 1), (2, 1), (1, 3), (2, 3), (1, 2), (2, 2))


PLACES = (
    [("M", n, j) for n in range(4) for j in range(5)] + ["N"] + [("B", n, j) for n in range(4) for j in range(3)]
    + ["T0", "T1", "T2", "S0", "S1", "S2", "S3", "S4", "T3"]
)
TICKS = {1: ("F", 0, 0), 2: ("F", 0, 3), 3: ("F", 1, 2), 4: ("F", 2, 2), 5: ("F", 3, 2), 6: "L", 7: ("M", 0, 0), 8: ("M", 0, 4),
         9: ("M", 1, 1), 10: ("M", 1, 4), 11: ("M", 2, 1)}
MLP_LAGS = ((1, 9, 15), (3, 11, 17))
BWD_LAGS = (0, 3, 5)


def timetable():
    plan = {}

    def put(place, *event):
        plan.setdefault(place, []).append(event)

    for s, place in TICKS.items():
        put(place, "tick", s)
    for n in range(4):
        for k, lags in zip((2, 1), MLP_LAGS):
            made = PLACES.index(("M", n, 4)) + 1
            for stage, lag in zip((2, 3, 4), lags):
                put(PLACES[made + lag], "step", k, ORD[n], stage)
        made = PLACES.index(("B", n, 2)) + 1
        for stage, lag in zip((2, 3, 4), BWD_LAGS):
            put(PLACES[made + lag], "step", 0, BACK[n], stage)
    return plan


def places(rows, first):
    r = lax.broadcasted_iota(jnp.int32, (rows, 128), 0)
    blk = sum((r >= BP * n).astype(jnp.int32) for n in range(1, 4)) if rows == WR else jnp.zeros_like(r)
    off = r - BP * blk
    token = (blk + first) * BT + jnp.minimum(off, BT - 1)
    i = (token * 4682) >> 16
    return i, token - WS * i, off < BT


def lanes_of(i, j):
    lane = lax.broadcasted_iota(jnp.int32, i.shape, 1)
    m = lane - 64
    m = m - 28 * ((m >= 28).astype(jnp.int32) + (m >= 56).astype(jnp.int32))
    fwd = jnp.where(m >= 14, 32 + j - (m - 14) + 13, i - m + 13)
    fwd = jnp.where((lane >= 64) & (lane < 120), fwd, 0)
    d = lane & 31
    pos = jnp.where(lane >= 32, j, i) + 13 - d
    ok = (pos >= 0) & (pos < WS) & (lane < 64) & (d < 27)
    return fwd, jnp.where(ok, pos + jnp.where(lane >= 32, 78, 64), 127)


def fill_tables(z, ids, mask_ref, fwd_ref, back_ref):
    across = (GRID + WS - 1) // WS

    def valid(w, i, j, ok):
        a = lax.div(w, jnp.int32(across))
        hi = jnp.where(w < across * across, GRID - a * WS, 0)
        wi = GRID - (w - across * a) * WS
        return jnp.where(ok & (i < hi) & (j < wi), 1.0, 0.0)[:, :1]

    def window(n):
        m, s = (jnp.int32(v) for v in WINDOWS_OF[3][n])
        for dev in range(3):
            m = jnp.where(z == dev, WINDOWS_OF[dev][n][0], m)
            s = jnp.where(z == dev, WINDOWS_OF[dev][n][1], s)
        return ids[m, 0, s]

    i, j, ok = places(WR, 0)
    fwd, back = lanes_of(i, j)
    shared = ids[SHARED[0], 0, SHARED[1]]
    for n in range(2):
        rows = slice(n * WR, n * WR + WR)
        fwd_ref[rows, :] = fwd
        back_ref[rows, :] = back
        mask_ref[rows, :] = valid(window(n), i, j, ok)
    mask_ref[NR:NE, :] = valid(shared, i, j, ok)
    i, j, ok = places(QR, z)
    fwd, back = lanes_of(i, j)
    fwd_ref[2 * WR : NR, :] = fwd
    back_ref[2 * WR : NR, :] = back
    mask_ref[2 * WR : NR, :] = valid(shared, i, j, ok)


def whole_kernel(
    x_raw, cot_raw, ids, *refs,
):
    given, refs, held_in, load = refs[:15], refs[15:-16], refs[-16:-1], refs[-1]
    qkv_w, proj_w, fc1_w, fc2_w, u0, u1, u2, u3, u4, u5, u6, qvb_in, relh_in, relw_in, ktail_ref = held_in
    (
        own, out_h, dx_h, vg_out, tg_out, shard0, small, mask_ref, fwd_ref, back_ref, vec_ref, tab_ref, tabf, w, r1,
        r2, r3, r4, x, cot, sm, raw, dx, gn, hid, gn2, gs, gsr, vg, tg, vr, tr, nrm, proj, qaug, kaug, vals, probs,
        att, nr2, act, gup, gml, dqkv, send, recv, local,
    ) = refs
    links = Links(send, recv)
    z = links.z
    rows_of = Rows(links, local)
    ag = Gather(links, (shard0, fc1_w, fc2_w), w, local.at[pl.ds(40, 3)], AG0)
    rs = Scatter(links, w, r1, r2, r3, r4, RS0)

    def rank(order, m):
        i = jnp.int32(order[3])
        for n in range(3):
            i = jnp.where(m == n, order[n], i)
        return (z + 4 - i) % 4

    def weight(k, t):
        return w[k, t].reshape(768, 768)

    def tick(s):
        if s + 2 < 12:
            ag.along(*BLOCKS[s + 2])
        if s + 1 < 12:
            ag.across(*BLOCKS[s + 1])
        ag.corner(*BLOCKS[s])

    def at(m, plan):
        for n, todo in plan.items():

            @pl.when(m == n)
            def _():
                for f in todo:
                    f()

    plan = timetable()

    def run(events):
        for what, *which in events:
            if what == "tick":
                tick(*which)
            else:
                rs.step(*which)

    def now(place):
        run(plan.get(place, ()))

    def hook(m, loop, j):
        for n in range(4):
            todo = plan.get((loop, n, j))
            if todo:

                @pl.when(m == n)
                def _():
                    run(todo)

    def stats(v):
        mu = jnp.mean(v, axis=-1, keepdims=True)
        c = v - mu
        var = jnp.mean(c * c, axis=-1, keepdims=True)
        return c, lax.rsqrt(var + 1e-6)

    read_x = pltpu.make_async_copy(x_raw, raw, local.at[44])
    read_x.start()
    loads = [pltpu.make_async_copy(a, b, load.at[n]) for n, (a, b) in enumerate(zip(given, held_in))]
    for c in loads:
        c.start()
    loads[0].wait()
    loads[1].wait()
    for t in range(3):
        shard0[:, 192 * t : 192 * t + 192] = qkv_w[t]
    shard0[:, 576:] = proj_w[...].astype(F32).T.astype(BF)
    x[63] = jnp.zeros((8, 768), BF)
    cot[63] = jnp.zeros((8, 768), BF)
    def pad_blocks(held):
        for m in range(3):
            gn2[0:147, :] = raw[m].astype(F32)
            for b in range(3):
                v = gn2[BT * b : BT * b + BP, :]
                v = jnp.where(lax.broadcasted_iota(jnp.int32, v.shape, 0) < BT, v, 0.0)
                held[3 * m + b] = v.astype(BF).reshape(7, 8, 768)

    held = dx.at[pl.ds(0, 63)].reshape(9, 7, 8, 768)
    read_x.wait()
    pad_blocks(held)
    links.barrier()
    rows_of.inward(held, x, X_SLOTS, XS, "start")
    for c in loads[2:]:
        c.wait()
    for b in (0, 1):
        ag.along(*BLOCKS[b])
    small[...] = jnp.zeros_like(small)
    for n, u in enumerate((u0, u1, u2, u3, u4, u5, u6)):
        ref, row = (vec_ref, n) if n < 6 else (small, 0)
        uf = u[...].astype(F32)
        for c in range(6):
            ref[row : row + 1, 128 * c : 128 * c + 128] = uf[c : c + 1, :]
    qvb = qvb_in[...].astype(F32)
    small[1:2, 0:192] = qvb[0:1]
    small[1:2, 384:576] = qvb[1:2]
    bias = [links.copy(small, sm.at[z], BS + d - 1, links.zdev((z + d) % 4)) for d in (1, 2, 3)]
    keep_bias = pltpu.make_async_copy(small, sm.at[z], local.at[43])
    keep_bias.start()
    for c in bias:
        c.start()

    ag.own_z(0)
    read_cot = pltpu.make_async_copy(cot_raw, raw, local.at[44])
    read_cot.start()
    ag.own_z(1)
    tabf[...] = jnp.zeros_like(tabf)
    tabf[0:27, :] = relh_in[...].astype(F32)
    tabf[32:59, :] = relw_in[...].astype(F32)
    tab_ref[...] = tabf[...].astype(BF)

    vg[...] = jnp.zeros_like(vg)
    tg[...] = jnp.zeros_like(tg)
    fill_tables(z, ids, mask_ref, fwd_ref, back_ref)
    rows_of.inward(held, x, X_SLOTS, XS, "wait")
    x[56:63] = x[pl.ds(NR // 8 + 7 * z, 7)]
    for c in bias:
        c.wait_recv()
    keep_bias.wait()

    g1, b1, pb, g2, b2, fb = (vec_ref[i : i + 1, :] for i in range(6))

    for r0 in range(0, NE, 32):
        rows = slice(r0, r0 + 32)
        c, rstd = stats(x[r0 // 8 : r0 // 8 + 4].astype(F32).reshape(32, 768))
        nrm[rows, :] = (mask_ref[rows, :] * (c * rstd * g1 + b1)).astype(BF)

    ag.across(*BLOCKS[0])
    tick(0)
    ag.own_z(2)
    rows_of.inward(held, x, X_SLOTS, XS, "drain")
    read_cot.wait()
    pad_blocks(held)
    rows_of.inward(held, cot, range(9), CS, "start")
    mix = gn.at[pl.ds(0, NR)]
    mix[...] = jnp.zeros_like(mix)

    def fwd_t(m, _):
        at(m, {n: [partial(ag.partner, 0, ORD[n])] for n in range(4)})
        t = rank(ORD, m)
        proj[...] = dotf(nrm[...], weight(0, t)[:, :576], NN) + sm[t][1:2, :576]
        for h in range(3):
            hh = 3 * t + h
            qs = (proj[:NR, 64 * h : 64 * h + 64].astype(BF) * BF(0.125)).astype(BF)
            rel = dotf(qs, tab_ref[...], NT) * 8.0
            lane = lax.broadcasted_iota(jnp.int32, (NR, 128), 1)
            got = jnp.take_along_axis(rel, fwd_ref[...], axis=1, mode="promise_in_bounds")
            hi = got.astype(BF).astype(F32)
            tail = jnp.where(lane < 92, hi, got - hi)
            tail = jnp.where(lane == 120, 1.0, jnp.where(lane < 120, tail, 0.0)).astype(BF)
            qa = jnp.concatenate([qs, tail[:, 64:]], axis=1)
            qaug[hh] = qa
            for wn in range(3):
                src = slice(wn * WR, wn * WR + WR) if wn < 2 else slice(NR, NE)
                k = proj[src, 192 + 64 * h : 256 + 64 * h].astype(BF)
                kaug[hh, wn] = jnp.concatenate([k, ktail_ref[:, 64:]], axis=1)
                vals[hh, wn] = proj[src, 384 + 64 * h : 448 + 64 * h].astype(BF)
        hook(m, "F", 0)
        for h in range(3):
            hh = 3 * t + h
            for wn in range(3):
                rows = slice(wn * WR, wn * WR + WR) if wn < 2 else slice(2 * WR, NR)
                s = dotf(qaug[hh, rows, :], kaug[hh, wn], NT)
                e = jnp.exp(s - jnp.max(s, axis=-1, keepdims=True))
                p = (e * (1.0 / jnp.sum(e, axis=-1, keepdims=True))).astype(BF)
                probs[hh, rows, :] = p
                att[t, rows, 64 * h : 64 * h + 64] = dotf(p, vals[hh, wn], NN).astype(BF)
            if h < 2:
                hook(m, "F", 1 + h)
        mix[...] += dotf(att[t], weight(0, t)[:, 576:], NT)
        hook(m, "F", 3)
        return 0

    lax.fori_loop(0, 4, fwd_t, 0)
    rows_of.inward(held, cot, range(9), CS, "wait")
    now("L")

    for r0 in range(0, NR, 32):
        rows = slice(r0, r0 + 32)
        xv = x[r0 // 8 : r0 // 8 + 4].astype(F32).reshape(32, 768)
        hv = xv + mask_ref[rows, :] * (mix[rows, :] + pb)
        hid[rows, :] = hv
        c, rstd = stats(hv)
        nr2[rows, :] = (c * rstd * g2 + b2).astype(BF)
        gm = mask_ref[rows, :] * cot[r0 // 8 : r0 // 8 + 4].astype(F32).reshape(32, 768)
        gml[rows, :] = gm.astype(BF)
    mix[...] = jnp.zeros_like(mix)
    gn2[...] = jnp.zeros_like(gn2)

    def mlp_t(m, _):
        at(m, {n: [partial(ag.partner, 1, ORD[n]), partial(ag.partner, 2, ORD[n])] for n in range(4)})
        t = rank(ORD, m)
        for f in range(3):
            cols = slice(256 * f, 256 * f + 256)
            for r0 in range(0, NR, 128):
                rows = slice(r0, r0 + 128)
                up = dotf(nr2[rows, :], weight(1, t)[:, cols], NN) + sm[t][0:1, cols]
                ga = dotf(gml[rows, :], weight(2, t)[:, cols], NN)
                cdf = 0.5 * (1.0 + lax.erf(up * (1.0 / math.sqrt(2.0))))
                pdf = jnp.exp(-0.5 * up * up) * (1.0 / math.sqrt(2.0 * math.pi))
                act[rows, cols] = (up * cdf).astype(BF)
                gup[rows, cols] = (ga * (cdf + up * pdf)).astype(BF)
            hook(m, "M", f)
        vg[0, pl.ds(8 + t, 1), :] = jnp.sum(gup[...].astype(F32), axis=0, keepdims=True)
        mix[...] += dotf(act[...], weight(2, t), NT)
        hook(m, "M", 3)
        gn2[...] += dotf(gup[...], weight(1, t), NT)
        hook(m, "M", 4)
        at(m, {n: [partial(ag.drain, 2, ORD[n])] for n in range(4)})
        w[2, t] = dotf(gml[...], act[...], TN).astype(BF).reshape(2, 2, 2, 96, 768)
        at(m, {n: [partial(rs.start, 2, ORD[n], 1), partial(ag.drain, 1, ORD[n])] for n in range(4)})
        w[1, t] = dotf(nr2[...], gup[...], TN).astype(BF).reshape(2, 2, 2, 96, 768)
        at(m, {n: [partial(rs.start, 1, ORD[n], 1)] for n in range(4)})
        return 0

    lax.fori_loop(0, 4, mlp_t, 0)
    now("N")

    sums = [jnp.zeros((8, 768), F32) for _ in range(4)]

    def fold(v):
        return jnp.sum(v.reshape(4, 8, 768), axis=0)

    gbl = act
    rows_of.inward(held, cot, range(9), CS, "drain")
    ob = cot
    for r0 in range(0, NR, 32):
        rows = slice(r0, r0 + 32)
        mk = mask_ref[rows, :]
        gm = gml[rows, :].astype(F32)
        hv = hid[rows, :]
        ob[r0 // 8 : r0 // 8 + 4] = (mk * (hv + mix[rows, :] + fb)).reshape(4, 8, 768).astype(BF)
        c, rstd = stats(hv)
        xh = c * rstd
        gv = gn2[rows, :]
        e2 = gv * g2
        gh = gm + rstd * (e2 - jnp.mean(e2, axis=-1, keepdims=True) - xh * jnp.mean(e2 * xh, axis=-1, keepdims=True))
        gb = mk * gh
        hid[rows, :] = gh
        gbl[rows, :] = gb.astype(BF)
        for n, v in enumerate((gv * xh, gv, gb, gm)):
            sums[n] = sums[n] + fold(v)
    for n in range(4):
        vg[0, n : n + 1, :] = jnp.sum(sums[n], axis=0, keepdims=True)
    rows_of.outward(ob, out_h, RET0, 22, "start")
    gn[...] = jnp.zeros_like(gn)

    def bwd_t(m, _):
        t = rank(BACK, m)
        at(m, {n: [partial(ag.drain, 0, BACK[n])] for n in range(4)})
        att_w = att[t]
        proj[:NR, :192] = dotf(gbl[...], weight(0, t)[:, 576:], NN)
        dqkv[...] = jnp.zeros_like(dqkv)
        for h in range(3):
            hh = 3 * t + h
            lo = 64 * h
            for wn in range(3):
                rows = slice(wn * WR, wn * WR + WR) if wn < 2 else slice(2 * WR, NR)
                dst = rows if wn < 2 else slice(NR, NE)
                do = proj[rows, lo : lo + 64].astype(BF)
                p = probs[hh, rows, :]
                pf = p.astype(F32)
                dp = dotf(do, vals[hh, wn], NT)
                delta = jnp.sum(pf * dp, axis=-1, keepdims=True)
                ds = (pf * (dp - delta)).astype(BF)
                dq = dotf(ds, kaug[hh, wn], NN)
                qa = qaug[hh, rows, :]
                dqkv[dst, 192 + lo : 256 + lo] = dotf(ds, qa, TN)[:, :64].astype(BF)
                dqkv[dst, 384 + lo : 448 + lo] = dotf(p, do, TN).astype(BF)
                rel = jnp.take_along_axis(dq, back_ref[rows, :], axis=1, mode="promise_in_bounds").astype(BF)
                gq = dq[:, :64] * 0.125 + dotf(rel, tab_ref[...], NN)
                dqkv[rows, lo : lo + 64] = gq.astype(BF)
                tg[0] += dotf(rel, qa, TN)[:64]
            hook(m, "B", h)
        vg[0, pl.ds(12 + t, 1), 0:576] = jnp.sum(dqkv[...].astype(F32), axis=0, keepdims=True)
        gn[...] += dotf(dqkv[...], weight(0, t)[:, :576], NT)
        gw = jnp.concatenate([dotf(nrm[...], dqkv[...], TN).astype(BF), dotf(gbl[...], att_w, TN).astype(BF)], axis=1)
        w[0, t] = gw.reshape(2, 2, 2, 96, 768)
        at(m, {n: [partial(rs.start, 0, BACK[n], 1)] for n in range(4)})
        return 0

    lax.fori_loop(0, 4, bwd_t, 0)

    gs[...] = gn[NR:].reshape(WR // 8, 8, 768).astype(BF)
    sh = [
        links.copy(gs.at[pl.ds(7 * ((z + d) % 4), 7)], gsr.at[d - 1], SH0 + d - 1, links.zdev((z + d) % 4)) for d in (1, 2, 3)
    ]
    for c in sh:
        c.start()
    now("T0")
    for c in sh:
        c.wait_recv()
    now("T1")
    first_norm_back(links, x, mask_ref, vec_ref, gn, hid, gsr, dx, vg.at[0])
    rows_of.outward(dx, dx_h, DX0, 31, "start")
    now("T2")
    small_sums(links, vg, tg, vr, tr, now)
    now("T3")
    vg_out[...] = vg[5]
    tg_out[...] = tg[5]
    for k in (2, 1, 0):
        own[k] = rs.total(k)
    rows_of.outward(ob, out_h, RET0, 22, "wait")
    rows_of.outward(dx, dx_h, DX0, 31, "wait")
    rows_of.outward(ob, out_h, RET0, 22, "drain")
    rows_of.outward(dx, dx_h, DX0, 31, "drain")
    for c in sh + bias:
        c.wait_send()
    for k in range(3):
        for i in (1, 2, 3):
            ag.move(k, "z", i).wait_send()
    rs.drain()


def first_norm_back(links, x, mask_ref, gain_ref, gn_ref, gh_ref, gsr, dx, vg):
    own = gn_ref[pl.ds(pl.multiple_of(NR + 56 * links.z, 8), 56), :]
    for d in range(3):
        own = own + gsr[d].astype(F32).reshape(56, 768)
    quarter = gn_ref[2 * WR : 2 * WR + 56, :] + own
    g1 = gain_ref[0:1, :]
    s_gain = jnp.zeros((8, 768), F32)
    s_bias = jnp.zeros((8, 768), F32)
    for r0, n in [(r, 32) for r in range(0, 2 * WR, 32)] + [(2 * WR, 56)]:
        rows = slice(r0, r0 + n)
        v = x[r0 // 8 : (r0 + n) // 8].astype(F32).reshape(n, 768)
        c = v - jnp.mean(v, axis=-1, keepdims=True)
        rs = lax.rsqrt(jnp.mean(c * c, axis=-1, keepdims=True) + 1e-6)
        xh = c * rs
        gn = mask_ref[rows, :] * (gn_ref[rows, :] if n == 32 else quarter)
        e1 = gn * g1
        gx = gh_ref[rows, :] + rs * (
            e1 - jnp.mean(e1, axis=-1, keepdims=True) - xh * jnp.mean(e1 * xh, axis=-1, keepdims=True)
        )
        dx[r0 // 8 : (r0 + n) // 8] = gx.reshape(n // 8, 8, 768).astype(BF)
        s_gain = s_gain + jnp.sum((gn * xh).reshape(n // 8, 8, 768), axis=0)
        s_bias = s_bias + jnp.sum(gn.reshape(n // 8, 8, 768), axis=0)
    vg[4:5, :] = jnp.sum(s_gain, axis=0, keepdims=True)
    vg[5:6, :] = jnp.sum(s_bias, axis=0, keepdims=True)


def small_sums(links, vg, tg, vr, tr, now):
    l = links
    partners = [l.sib, l.xn, l.yn, l.zdev((l.z // 2) * 2 + 1 - l.z % 2), l.zdev((l.z + 2) % 4)]
    copies = []
    for n, dev in enumerate(partners):
        pair = [l.copy(vg.at[n], vr.at[n], VS0 + 2 * n, dev), l.copy(tg.at[n], tr.at[n], VS0 + 2 * n + 1, dev)]
        for c in pair:
            c.start()
        now(f"S{n}")
        for c in pair:
            c.wait_recv()
        vg[n + 1] = vg[n] + vr[n]
        tg[n + 1] = tg[n] + tr[n]
        copies += pair
    for c in copies:
        c.wait_send()


def final_kernel(
    own, out_h, dx_h, vg, tg, out, dx, g_qkv, g_proj, g_fc1, g_fc2, v0, v1, v2, v3, v4, v5, fc1b_out, qvb_out, relh_out, relw_out,
    rows,
):
    for m in range(3):
        for b in range(3):
            n = BT * (3 * m + b)
            dx[n : n + BT, 0, :] = dx_h[3 * m + b].astype(F32).reshape(BP, 768)[:BT]
            rows[BT * b : BT * b + BT, :] = out_h[3 * m + b].astype(F32).reshape(BP, 768)[:BT]
        out[m] = rows[...].astype(BF)
    for n, ref in enumerate((v0, v1, v2, v3, v4, v5)):
        for c in range(6):
            ref[c : c + 1, :] = vg[n : n + 1, 128 * c : 128 * c + 128]
    for t in range(4):
        for c in range(6):
            fc1b_out[6 * t + c : 6 * t + c + 1, :] = vg[8 + t : 9 + t, 128 * c : 128 * c + 128]
        qvb_out[0:1, 192 * t : 192 * t + 192] = vg[12 + t : 13 + t, 0:192]
        qvb_out[1:2, 192 * t : 192 * t + 192] = vg[12 + t : 13 + t, 384:576]
    relh_out[...] = tg[0:27, :64] * 8.0
    relw_out[...] = tg[32:59, :64] * 8.0
    for t in range(3):
        g_qkv[t] = own[0, :, 192 * t : 192 * t + 192]
    g_proj[...] = own[0, :, 576:].T
    g_fc1[...] = own[1]
    g_fc2[...] = own[2]


def final_call(*arrays):
    shp = jax.ShapeDtypeStruct
    vm = pl.BlockSpec(memory_space=pltpu.VMEM)
    return pl.pallas_call(
        final_kernel,
        out_shape=(
            shp((3, 147, 768), BF), shp((441, 1, 768), F32), shp((3, 96, 192), F32), shp((192, 96), F32), shp((96, 768), F32),
            shp((96, 768), F32), *[shp((6, 128), F32)] * 6, shp((24, 128), F32), shp((2, 768), F32), shp((27, 64), F32),
            shp((27, 64), F32),
        ),
        in_specs=[vm] * 5,
        out_specs=(vm,) * 16,
        scratch_shapes=[pltpu.VMEM((147, 768), F32)],
    )(*arrays)


def whole_call(*arrays):
    shp = jax.ShapeDtypeStruct
    vm = pl.BlockSpec(memory_space=pltpu.VMEM)
    hbm = pl.BlockSpec(memory_space=pl.ANY)
    V = pltpu.VMEM
    dma = pltpu.SemaphoreType.DMA
    return pl.pallas_call(
        whole_kernel,
        out_shape=(
            shp((3, 96, 768), F32), shp((9, 7, 8, 768), BF), shp((9, 7, 8, 768), BF), shp((16, 768), F32), shp((64, 128), F32),
        ),
        in_specs=[hbm, hbm, pl.BlockSpec(memory_space=pltpu.SMEM)] + [hbm] * 15,
        out_specs=(vm, hbm, hbm, vm, vm),
        scratch_shapes=[
            V((96, 768), BF), V((8, 768), F32), V((NE, 1), F32), V((NR, 128), jnp.int32), V((NR, 128), jnp.int32),
            V((8, 768), F32), V((128, 64), BF), V((128, 64), F32),
            V((3, 4, 2, 2, 2, 96, 768), BF), V((12, 2, 2, 96, 768), BF), V((12, 2, 2, 48, 768), BF), V((12, 2, 48, 768), BF),
            V((3, 3, 96, 768), BF), V((NE // 8, 8, 768), BF), V((NR // 8, 8, 768), BF), V((4, 8, 768), F32),
            V((3, 147, 768), BF), V((NR // 8, 8, 768), BF), V((NE, 768), F32), V((NR, 768), F32), V((NR, 768), F32),
            V((WR // 8, 8, 768), BF), V((3, 7, 8, 768), BF), V((6, 16, 768), F32), V((6, 64, 128), F32),
            V((5, 16, 768), F32), V((5, 64, 128), F32),
            V((NE, 768), BF), V((NE, 576), F32), V((HEADS, NR, 128), BF), V((HEADS, 3, WR, 128), BF), V((HEADS, 3, WR, 64), BF),
            V((HEADS, NR, WR), BF), V((4, NR, 192), BF), V((NR, 768), BF), V((NR, 768), BF), V((NR, 768), BF), V((NR, 768), BF),
            V((NE, 576), BF), dma((SEMS,)), dma((SEMS,)), dma((48,)),
            *[V(a.shape, a.dtype) for a in arrays[3:]], dma((15,)),
        ],
        compiler_params=pltpu.CompilerParams(collective_id=0, has_side_effects=True, vmem_limit_bytes=67043328),
    )(*arrays)


def plain_gather(xh, coth, shard):
    mine = lax.dynamic_index_in_dim(jnp.asarray(block_table()), lax.axis_index("tensor"), 0, keepdims=False)

    def spread(held, count):
        blocks = lax.all_gather(held.reshape(3, 3, 7, 8, 768), "tensor", axis=1).reshape(36, 7, 8, 768)
        got = jnp.take(blocks, mine[:count], axis=0).reshape(-1, 8, 768)
        return jnp.concatenate([got[:63], jnp.zeros((1, 8, 768), BF), got[63:]], axis=0)

    whole = lax.all_gather(lax.all_gather(shard, ("dp", "win"), axis=1, tiled=True), "tensor", axis=1)
    return spread(xh, 13), spread(coth, 9), whole


def plain_scatter(grads, x, mask, vec, gn, gh, vg, tg, out):
    shared = lax.psum_scatter(gn[NR:], "tensor", scatter_dimension=0, tiled=True)
    gn = mask * (gn[:NR] + jnp.pad(shared, ((2 * WR, QR - BP), (0, 0))))
    xf = x[: NR // 8].reshape(NR, 768).astype(F32)
    cen = xf - jnp.mean(xf, axis=-1, keepdims=True)
    rs = lax.rsqrt(jnp.mean(cen * cen, axis=-1, keepdims=True) + 1e-6)
    xh = cen * rs
    e1 = gn * vec[0]
    gx = gh + rs * (e1 - jnp.mean(e1, axis=-1, keepdims=True) - xh * jnp.mean(e1 * xh, axis=-1, keepdims=True))
    vg = vg.at[4].set(jnp.sum(gn * xh, axis=0)).at[5].set(jnp.sum(gn, axis=0))
    back_to = lax.dynamic_index_in_dim(jnp.asarray(home_table()), lax.axis_index("tensor"), 0, keepdims=False)

    def bring(rows):
        blocks = lax.all_gather(rows[:63].reshape(9, 7, 8, 768), "tensor", axis=0, tiled=True)
        return jnp.take(blocks, back_to, axis=0)

    own = lax.psum_scatter(grads.reshape(3, 4, 768, 768), "tensor", scatter_dimension=1, tiled=False)
    own = lax.psum_scatter(own, ("dp", "win"), scatter_dimension=1, tiled=True).astype(F32)
    vg, tg = lax.psum((vg, tg), ("dp", "win", "tensor"))
    return own, bring(out), bring(gx.astype(BF).reshape(NR // 8, 8, 768)), vg, tg


def per_device(
    links, tokens, window_ids, norm1_gain, norm1_bias, qkv_weight, qv_bias, rel_height, rel_width, proj_weight, proj_bias,
    norm2_gain, norm2_bias, fc1_weight, fc1_bias, fc2_weight, fc2_bias, out_grad,
):
    rank = lax.axis_index("tensor")

    def home_blocks(rows):
        return jnp.pad(rows.reshape(9, BT, 768), ((0, 0), (0, BP - BT), (0, 0))).reshape(9, 7, 8, 768)

    if links:
        vectors = (norm1_gain, norm1_bias, proj_bias, norm2_gain, norm2_bias, fc2_bias, fc1_bias)
        done = whole_call(
            tokens[0], out_grad[0], jnp.transpose(window_ids, (1, 0, 2)), jnp.transpose(qkv_weight, (1, 0, 2)), proj_weight,
            fc1_weight, fc2_weight.T, *(v.reshape(6, 128) for v in vectors), qv_bias, rel_height, rel_width,
            jnp.asarray(key_tail(), BF),
        )
        out, dx, g_qkv, g_proj, g_fc1, g_fc2, v0, v1, v2, v3, v4, v5, fc1b, qvb, relh, relw = final_call(*done)
        v0, v1, v2, v3, v4, v5 = (v.reshape(768) for v in (v0, v1, v2, v3, v4, v5))
        return (
            out[None], dx.reshape(1, 3, 147, 768), v4, v5, jnp.transpose(g_qkv, (1, 0, 2)), qvb, relh, relw, g_proj, v2, v0, v1, g_fc1,
            fc1b.reshape(-1), g_fc2.T, v3,
        )

    shard = jnp.stack(
        [
            jnp.concatenate([qkv_weight.reshape(-1, 576), proj_weight.T], axis=1),
            fc1_weight,
            fc2_weight.T,
        ]
    )
    xh, coth = home_blocks(tokens), home_blocks(out_grad)

    wi, wj, wv = token_positions()
    wi, wj, wv = jnp.asarray(wi, jnp.int32), jnp.asarray(wj, jnp.int32), jnp.asarray(wv)
    qi = jnp.pad(lax.dynamic_slice_in_dim(wi, rank * BP, BP), (0, QR - BP))
    qj = jnp.pad(lax.dynamic_slice_in_dim(wj, rank * BP, BP), (0, QR - BP))
    qv = jnp.pad(lax.dynamic_slice_in_dim(wv, rank * BP, BP), (0, QR - BP))
    ids = window_ids.reshape(9)
    slots = jnp.asarray([[m * 3 + s for m, s in WINDOWS_OF[dev]] + [4, 4] for dev in range(4)], jnp.int32)
    wid = jnp.take(ids, lax.dynamic_index_in_dim(slots, rank, 0, keepdims=False), axis=0)

    across = (GRID + WS - 1) // WS

    def valid(w, i, j, ok):
        return ok & (w < across * across) & ((w // across) * WS + i < GRID) & ((w % across) * WS + j < GRID)

    mask = jnp.concatenate(
        [valid(wid[0], wi, wj, wv), valid(wid[1], wi, wj, wv), valid(wid[2], qi, qj, qv), valid(wid[3], wi, wj, wv)]
    ).astype(F32)[:, None]
    ii = jnp.concatenate([wi, wi, qi])
    jj = jnp.concatenate([wj, wj, qj])
    fwd, back = pick_lanes(ii, jj)

    small = jnp.zeros((8, 768), F32).at[0].set(fc1_bias.astype(F32))
    small = small.at[1, :192].set(qv_bias[0].astype(F32)).at[1, 384:576].set(qv_bias[1].astype(F32))
    vec = jnp.stack(
        [norm1_gain, norm1_bias, proj_bias, norm2_gain, norm2_bias, fc2_bias, fc2_bias, fc2_bias]
    ).astype(F32)
    tab = jnp.zeros((128, 64), BF).at[0:27].set(rel_height).at[32:59].set(rel_width)
    tabt = (tab * BF(8)).T
    ktail = jnp.asarray(key_tail(), BF)

    x, cot, whole = plain_gather(xh, coth, shard)
    small = lax.all_gather(small, "tensor", axis=0)
    out, gn, gh, grads, vg, tg = compute(
        x, cot, mask, whole.reshape(3, 4, 768, 768), vec, small[:, 1:2, :576], small[:, 0:1], ktail, fwd, back, tab, tabt
    )
    own, out, dx, vg, tg = plain_scatter(grads, x, mask[:NR], vec, gn, gh, vg, tg, out)

    def tokens_of(blocks):
        return blocks.reshape(9, BP, 768)[:, :BT].reshape(tokens.shape)

    output = tokens_of(out)
    grad_tokens = tokens_of(dx).astype(F32)
    g_qkv = own[0, :, :576].reshape(qkv_weight.shape)
    g_proj = own[0, :, 576:].T
    g_fc1 = own[1]
    g_fc2 = own[2].T
    g_qv = jnp.stack([vg[12:16, :192].reshape(-1), vg[12:16, 384:576].reshape(-1)])
    return (
        output, grad_tokens, vg[4], vg[5], g_qkv, g_qv, tg[0:27, :64] * 8.0, tg[32:59, :64] * 8.0, g_proj,
        vg[2], vg[0], vg[1], g_fc1, vg[8:12].reshape(-1), g_fc2, vg[3],
    )


def solution(mesh):
    in_specs = (
        P("dp", "win", "tensor", None), P("dp", "win", None), P(), P(), P(("dp", "win"), None, "tensor"),
        P(None, "tensor"), P(), P(), P("tensor", ("dp", "win")), P(), P(), P(), P(("dp", "win"), "tensor"), P("tensor"),
        P("tensor", ("dp", "win")), P(), P("dp", "win", "tensor", None),
    )
    out_specs = (
        P("dp", "win", "tensor", None), P("dp", "win", "tensor", None), P(), P(), P(("dp", "win"), None, "tensor"), P(),
        P(), P(), P("tensor", ("dp", "win")), P(), P(), P(), P(("dp", "win"), "tensor"), P(),
        P("tensor", ("dp", "win")), P(),
    )
    links = dict(mesh.shape) == {"dp": 2, "win": 4, "tensor": 4}
    return jax.shard_map(partial(per_device, links), mesh=mesh, in_specs=in_specs, out_specs=out_specs, check_vma=False)
```
